32 devices in a mesh: section: 2 (over core), dp: 4 (over z), tensor: 4 (over y, x).
Axes of the slice: x: 2, y: 2, z: 4, core: 2. Of those that a mesh axis runs over, the one named last changes fastest.
Arguments:
- inputs: bfloat16 [1024, 8, 1024], P('tensor', 'dp'), may hold values from -6 to 6
- segments: int32 [8, 1024], P('dp'), may hold values from 0 to 3, never falling along the last dimension, each value on 1 to 512 neighbouring positions
- cotangent: bfloat16 [1024, 8, 1024], P('tensor', 'dp'), may hold values from -6 to 6
- gain_attn: float32 [2, 1024], P('section'), may hold values from 0.1 to 1.9
- joint_projection_weight: bfloat16 [2, 1024, 3, 1024], P('section', None, None, 'tensor'), may hold values from -0.1875 to 0.1875
- query_down_factor: bfloat16 [2, 1024, 4], P('section'), may hold values from -0.1875 to 0.1875
- query_up_factor: bfloat16 [2, 4, 1024], P('section', None, 'tensor'), may hold values from -0.1875 to 0.1875
- value_down_factor: bfloat16 [2, 1024, 4], P('section'), may hold values from -0.1875 to 0.1875
- value_up_factor: bfloat16 [2, 4, 1024], P('section', None, 'tensor'), may hold values from -0.1875 to 0.1875
- w_out: bfloat16 [2, 1024, 1024], P('section', 'tensor'), may hold values from -1.5 to 1.5
- gain_mlp: float32 [2, 1024], P('section'), may hold values from 0.1 to 1.9
- w_fc: bfloat16 [2, 1024, 4096], P('section', None, 'tensor'), may hold values from -0.1875 to 0.1875
- w_proj: bfloat16 [2, 4096, 1024], P('section', 'tensor'), may hold values from -0.09375 to 0.09375
Outputs:
- activations: bfloat16 [2, 1024, 8, 1024], P('section', 'tensor', 'dp')
- input_grads: bfloat16 [2, 1024, 8, 1024], P('section', 'tensor', 'dp')
- grad_a_query: float32 [2, 1024, 4], P('section')
- grad_b_query: float32 [2, 4, 1024], P('section')
- grad_a_value: float32 [2, 1024, 4], P('section')
- grad_b_value: float32 [2, 4, 1024], P('section')
The draws below stay inside these ranges and needn't reach their ends.
Inputs may be any that keep to these rules, and one draw needn't show every extreme that they name: `segments`: along a row the segment numbers never fall; a segment holds at most 512 slots of a row, and some segment holds exactly that many.
All inputs are finite; a program needn't handle non-finite values.
Results may differ from the reference program's by a relative error of at most 0.034.
Values may be sent and summed in bfloat16 or wider, within the bound.
A program may use at most 128 MiB of HBM per device.

```python
import math
import jax
import jax.numpy as jnp
import numpy as np
from jax import lax

D = 1024
HEADS = 16
HEAD_DIM = 64
FF = 4096
RANK = 4
SEQ = 1024
ROWS_MB = 1
LAYER_TOTAL = 2
ROWS = 8


def level_of(rng, dims, pieces, low, high):
    factor_of = 1.0
    for dim, parts in pieces:
        steps = jax.random.uniform(jax.random.fold_in(jax.random.fold_in(rng, 6), dim), (parts,), jnp.float32, low / len(pieces), high / len(pieces))
        factor_of = factor_of * jnp.repeat(jnp.exp(steps), dims[dim] // parts).reshape((-1,) + (1,) * (len(dims) - 1 - dim))
    return factor_of


def length_profile(count, total, reach, slope):
    loads = [(1 << 20) // math.isqrt(rank ** slope) + 1 for rank in range(2, count + 1)]
    rest, counts = total - reach - (count - 1), [1] * (count - 1)
    while rest > 0:
        candidates = [i for i in range(count - 1) if counts[i] < reach]
        pool, left = sum([loads[i] for i in candidates]), rest
        for i in candidates:
            extra = min(reach - counts[i], max(1, left * loads[i] // pool), rest)
            counts[i] = counts[i] + extra
            rest = rest - extra
    return np.array([reach] + counts)


def uneven_parts(key, number_of, total, most, lean):
    if number_of == 2:
        one = jax.random.randint(key, (), max(1, total - most), min(most, total - 1) + 1)
        return jnp.stack([one, total - one])
    sizes = jnp.asarray(length_profile(number_of, total, most, lean), jnp.int32)
    couples = (number_of - 1) // 2
    source_of, sink = sizes[1:1 + 2 * couples:2], sizes[2:2 + 2 * couples:2]
    room = jnp.minimum(source_of - 1, most - sink)
    shifted = jax.random.randint(jax.random.fold_in(key, 1), (couples,), 0, 1 << 20) % (room + 1)
    sizes = sizes.at[1:1 + 2 * couples:2].set(source_of - shifted).at[2:2 + 2 * couples:2].set(sink + shifted)
    return sizes[jax.random.permutation(jax.random.fold_in(key, 2), number_of)]


def gaussian(key, extent, width, reach, pieces=(), dtype=jnp.bfloat16):
    values = width * jax.random.normal(key, extent, jnp.float32)
    if pieces:
        values = values * level_of(key, extent, pieces, -0.22, 0.18)
    return jnp.clip(values, -reach, reach).astype(dtype)


def setup_inputs(seed: int = 0) -> dict:
    seeds = jax.random.split(jax.random.key(seed), 14)
    inputs = gaussian(seeds[0], (SEQ, ROWS, D), 1.0, 6.0, ((0, 4), (1, 4)))
    segments = jax.vmap(lambda own: jnp.searchsorted(jnp.cumsum(uneven_parts(own, 4, SEQ, SEQ // 2, 1)), jnp.arange(SEQ), side="right"))(jax.random.split(seeds[1], ROWS)).reshape((ROWS, SEQ)).astype(jnp.int32)
    cotangent = gaussian(seeds[2], (SEQ, ROWS, D), 1.0, 6.0, ((0, 4), (1, 4)))
    gain_attn = jnp.clip(1.0 + 0.18 * jax.random.normal(seeds[3], (LAYER_TOTAL, D), jnp.float32), 0.1, 1.9)
    joint_projection_weight = gaussian(seeds[4], (LAYER_TOTAL, D, 3, D), D ** -0.5, 0.1875, ((0, 2), (3, 4)))
    query_down_factor = gaussian(seeds[5], (LAYER_TOTAL, D, RANK), D ** -0.5, 0.1875, ((0, 2),))
    query_up_factor = gaussian(seeds[6], (LAYER_TOTAL, RANK, D), 0.03, 0.1875, ((0, 2), (2, 4)))
    value_down_factor = gaussian(seeds[7], (LAYER_TOTAL, D, RANK), D ** -0.5, 0.1875, ((0, 2),))
    value_up_factor = gaussian(seeds[8], (LAYER_TOTAL, RANK, D), 0.03, 0.1875, ((0, 2), (2, 4)))
    w_out = gaussian(seeds[9], (LAYER_TOTAL, D, D), (D // 64) ** -0.5, 1.5, ((0, 2), (1, 4)))
    gain_mlp = jnp.clip(1.0 + 0.18 * jax.random.normal(seeds[10], (LAYER_TOTAL, D), jnp.float32), 0.1, 1.9)
    w_fc = gaussian(seeds[11], (LAYER_TOTAL, D, FF), D ** -0.5, 0.1875, ((0, 2), (2, 4)))
    w_proj = gaussian(seeds[12], (LAYER_TOTAL, FF, D), FF ** -0.5, 0.09375, ((0, 2), (1, 4)))
    return dict(inputs=inputs, segments=segments, cotangent=cotangent, gain_attn=gain_attn, joint_projection_weight=joint_projection_weight, query_down_factor=query_down_factor, query_up_factor=query_up_factor, value_down_factor=value_down_factor, value_up_factor=value_up_factor, w_out=w_out, gain_mlp=gain_mlp, w_fc=w_fc, w_proj=w_proj)


EPSILON = 1e-05
PRECISE = lax.Precision.HIGHEST
MASKED = -1000000000.0
CUBIC_TERM = 0.044715
TANH_SCALE = 0.7978845608028654

@jax.custom_vjp
def low(v):
    return lax.optimization_barrier(v.astype(jnp.bfloat16)).astype(jnp.float32)

@jax.custom_vjp
def low_back(v):
    return v

def low_keep(v):
    return (low(v), None)

def low_pass(kept, grad):
    return (grad,)

def back_keep(v):
    return (v, None)

def back_low(kept, grad):
    return (low(grad),)
low.defvjp(low_keep, low_pass)
low_back.defvjp(back_keep, back_low)

def gelu_tanh(value):
    return 0.5 * value * (1.0 + jnp.tanh(TANH_SCALE * (value + CUBIC_TERM * value * value * value)))

def normalize(residual_stream, gain):
    middle = lax.optimization_barrier(jnp.mean(residual_stream, axis=-1, keepdims=True))
    centred = residual_stream - middle
    inverse = lax.rsqrt(lax.optimization_barrier(jnp.mean(centred * centred, axis=-1, keepdims=True)) + EPSILON)
    return centred * inverse * gain

def attend_row(packed):
    queries, keys_all, values_all, segment_row = packed
    length = queries.shape[0]
    scores = jnp.einsum('qhe,khe->hqk', queries, keys_all, precision=PRECISE) * HEAD_DIM ** (-0.5)
    scores = low_back(scores)
    positions = jnp.arange(length)
    allowed = (segment_row[:, None] == segment_row[None, :]) & (positions[None, :] <= positions[:, None])
    scores = jnp.where(allowed[None], scores, MASKED)
    row_max = lax.optimization_barrier(jnp.max(scores, axis=-1, keepdims=True))
    exponent = jnp.exp(scores - row_max)
    weights_soft = low(exponent / lax.optimization_barrier(jnp.sum(exponent, axis=-1, keepdims=True)))
    return jnp.einsum('hqk,khe->qhe', weights_soft, values_all, precision=PRECISE)

def single_layer(residual_stream, segment_row_span, fixed_weights, adapter_pair):
    gain_a, joint_projection_weight, w_out, gain_m, w_fc, w_proj = fixed_weights
    query_down_factor, query_up_factor, value_down_factor, value_up_factor = adapter_pair
    factor = 32.0 / RANK
    length, row_count = (residual_stream.shape[0], residual_stream.shape[1])
    norm_rows = low(normalize(residual_stream, gain_a))
    joined = jnp.einsum('srd,dcf->srcf', norm_rows, joint_projection_weight, precision=PRECISE)
    narrow_query_rows = jnp.einsum('srd,dk->srk', norm_rows, query_down_factor, precision=PRECISE)
    narrow_value_rows = jnp.einsum('srd,dk->srk', norm_rows, value_down_factor, precision=PRECISE)
    extra_query = factor * jnp.einsum('srk,kf->srf', narrow_query_rows, query_up_factor, precision=PRECISE)
    extra_value = factor * jnp.einsum('srk,kf->srf', narrow_value_rows, value_up_factor, precision=PRECISE)
    queries = low_back(low(joined[:, :, 0] + extra_query))
    keys_all = low_back(low(joined[:, :, 1]))
    values_all = low_back(low(joined[:, :, 2] + extra_value))

    def split_heads(matrix):
        return jnp.moveaxis(matrix.reshape(length, row_count, HEADS, HEAD_DIM), 1, 0)
    attended = lax.map(jax.checkpoint(attend_row), (split_heads(queries), split_heads(keys_all), split_heads(values_all), segment_row_span))
    attended = jnp.moveaxis(attended, 0, 1).reshape(length, row_count, HEADS * HEAD_DIM)
    attended = low_back(low(attended))
    middle = residual_stream + low_back(jnp.einsum('srf,fd->srd', attended, w_out, precision=PRECISE))
    normed_mlp = low(normalize(middle, gain_m))
    pre_act = low_back(jnp.einsum('srd,df->srf', normed_mlp, w_fc, precision=PRECISE))
    hidden = low(gelu_tanh(pre_act))
    return middle + low_back(jnp.einsum('srf,fd->srd', hidden, w_proj, precision=PRECISE))

def reference(inputs, segments, cotangent, gain_attn, joint_projection_weight, query_down_factor, query_up_factor, value_down_factor, value_up_factor, w_out, gain_mlp, w_fc, w_proj):

    def expand_columns(matrix):
        return matrix.astype(jnp.float32)
    fixed_weights = [tuple((expand_columns(weight_matrix[layer_position]) for weight_matrix in (gain_attn, joint_projection_weight, w_out, gain_mlp, w_fc, w_proj))) for layer_position in range(LAYER_TOTAL)]
    adapter_list = tuple((tuple((expand_columns(weight_matrix[layer_position]) for weight_matrix in (query_down_factor, query_up_factor, value_down_factor, value_up_factor))) for layer_position in range(LAYER_TOTAL)))
    groups = ROWS // ROWS_MB

    def one_group(gradient_totals, group_index):
        first_row = group_index * ROWS_MB
        residual_stream = expand_columns(lax.dynamic_slice_in_dim(inputs, first_row, ROWS_MB, 1))
        target_rows = expand_columns(lax.dynamic_slice_in_dim(cotangent, first_row, ROWS_MB, 1))
        segment_row_span = lax.dynamic_slice_in_dim(segments, first_row, ROWS_MB, 0)

        def paired_layers(layer_input_rows, check_offset, adapter_stack):
            first_layer_output = single_layer(layer_input_rows, segment_row_span, fixed_weights[0], adapter_stack[0])
            second_layer_input = low_back(low(first_layer_output)) + check_offset
            return (first_layer_output, single_layer(second_layer_input, segment_row_span, fixed_weights[1], adapter_stack[1]))
        check_offset = jnp.zeros_like(residual_stream)
        (first_layer_output, second_layer_output), backward_function = jax.vjp(paired_layers, residual_stream, check_offset, adapter_list)
        input_gradient, gradient_check, adapter_gradients = backward_function((jnp.zeros_like(first_layer_output), target_rows))
        gradient_totals = jax.tree.map(jnp.add, gradient_totals, adapter_gradients)
        outputs = jnp.stack([first_layer_output, second_layer_output]).astype(jnp.bfloat16)
        gradients = jnp.stack([input_gradient, gradient_check]).astype(jnp.bfloat16)
        return (gradient_totals, (outputs, gradients))
    empty_gradients = jax.tree.map(jnp.zeros_like, adapter_list)
    gradient_totals, (outputs, gradients) = lax.scan(one_group, empty_gradients, jnp.arange(groups))
    outputs = jnp.moveaxis(outputs, 0, 2).reshape(LAYER_TOTAL, SEQ, ROWS, D)
    gradients = jnp.moveaxis(gradients, 0, 2).reshape(LAYER_TOTAL, SEQ, ROWS, D)
    grad_aq = jnp.stack([gradient_totals[0][0], gradient_totals[1][0]])
    grad_bq = jnp.stack([gradient_totals[0][1], gradient_totals[1][1]])
    grad_av = jnp.stack([gradient_totals[0][2], gradient_totals[1][2]])
    grad_bv = jnp.stack([gradient_totals[0][3], gradient_totals[1][3]])
    return (outputs, gradients, grad_aq, grad_bq, grad_av, grad_bv)
```

```python
import functools

import jax
import jax.numpy as jnp
from jax import lax
from jax.experimental import pallas as pl
from jax.experimental.pallas import tpu as pltpu
from jax.sharding import PartitionSpec as P

HEAD_DIM = 64
MICRO = 2


EPSILON = 1e-05
PRECISE = lax.Precision.HIGHEST
MASKED = -1000000000.0
CUBIC_TERM = 0.044715
TANH_SCALE = 0.7978845608028654


def passed_along(block, axis, distance):
    devices = range(lax.axis_size(axis))
    route = [(i - distance, i) for i in devices if i - distance in devices]
    return lax.ppermute(block, axis, route)


def gelu_tanh(value):
    return 0.5 * value * (1.0 + jnp.tanh(TANH_SCALE * (value + CUBIC_TERM * value * value * value)))


def normalize(residual_stream, gain):
    middle = jnp.mean(residual_stream, axis=-1, keepdims=True)
    centred = residual_stream - middle
    inverse = lax.rsqrt(jnp.mean(centred * centred, axis=-1, keepdims=True) + EPSILON)
    unit_rows = centred * inverse
    return (unit_rows * gain, unit_rows, inverse)


def normalize_back(grad_norm, unit_rows, inverse, gain):
    scaled = grad_norm * gain
    return inverse * (
        scaled
        - jnp.mean(scaled, axis=-1, keepdims=True)
        - unit_rows * jnp.mean(scaled * unit_rows, axis=-1, keepdims=True)
    )


def block_mask(segment_row_span, first_row, block):
    length = segment_row_span.shape[1]
    segment_part = lax.dynamic_slice_in_dim(segment_row_span, first_row, block, 1)
    query_places = first_row + jnp.arange(block)
    key_places = jnp.arange(length)
    same_doc = segment_part[:, :, None] == segment_row_span[:, None, :]
    return same_doc & (key_places[None, None, :] <= query_places[None, :, None])


def projected_rows(row_portion, joint_projection_weight, adapter_pair):
    query_down_factor, query_up_factor, value_down_factor, value_up_factor = adapter_pair
    factor = 32.0 / query_down_factor.shape[-1]
    joined = jnp.einsum(
        "srd,dcf->srcf", row_portion, joint_projection_weight, preferred_element_type=jnp.float32
    )
    narrow_query_rows = jnp.einsum(
        "srd,dk->srk", row_portion, query_down_factor, preferred_element_type=jnp.float32
    )
    narrow_value_rows = jnp.einsum(
        "srd,dk->srk", row_portion, value_down_factor, preferred_element_type=jnp.float32
    )
    queries = joined[:, :, 0] + factor * jnp.einsum(
        "srk,kf->srf", narrow_query_rows, query_up_factor.astype(jnp.float32), precision=PRECISE
    )
    values_all = joined[:, :, 2] + factor * jnp.einsum(
        "srk,kf->srf", narrow_value_rows, value_up_factor.astype(jnp.float32), precision=PRECISE
    )
    stacked_weights = jnp.stack([queries, joined[:, :, 1], values_all], axis=2).astype(jnp.bfloat16)
    return (stacked_weights, narrow_query_rows, narrow_value_rows)


def attention_forward(queries, keys_all, values_all, segment_row_span):
    length, row_count, head_count, width = queries.shape
    block = min(512, length)
    factor = width ** (-0.5)

    def one_block(block_index):
        first_row = block_index * block
        query_part = lax.dynamic_slice_in_dim(queries, first_row, block, 0)
        scores = (
            jnp.einsum("qrhe,krhe->rhqk", query_part, keys_all, preferred_element_type=jnp.float32)
            * factor
        )
        allowed = block_mask(segment_row_span, first_row, block)
        scores = jnp.where(allowed[:, None], scores, MASKED)
        row_max = jnp.max(scores, axis=-1, keepdims=True)
        exponent = jnp.exp(scores - row_max)
        total = jnp.sum(exponent, axis=-1, keepdims=True)
        weights_soft = (exponent / total).astype(jnp.bfloat16)
        attended = jnp.einsum(
            "rhqk,krhe->qrhe", weights_soft, values_all, preferred_element_type=jnp.float32
        )
        return (attended, (row_max + jnp.log(total))[..., 0])

    attended, log_sums = lax.map(one_block, jnp.arange(length // block))
    attended = attended.reshape(length, row_count, head_count, width)
    log_sums = jnp.moveaxis(log_sums, 0, 2).reshape(row_count, head_count, length)
    return (attended, log_sums)


def attention_backward(queries, keys_all, values_all, segment_row_span, log_sums, grad_heads):
    length = queries.shape[0]
    block = min(512, length)
    factor = queries.shape[-1] ** (-0.5)

    def one_block(carry, block_index):
        grad_keys, grad_values = carry
        first_row = block_index * block
        query_part = lax.dynamic_slice_in_dim(queries, first_row, block, 0)
        grad_part = lax.dynamic_slice_in_dim(grad_heads, first_row, block, 0)
        sums_part = lax.dynamic_slice_in_dim(log_sums, first_row, block, 2)
        scores = (
            jnp.einsum("qrhe,krhe->rhqk", query_part, keys_all, preferred_element_type=jnp.float32)
            * factor
        )
        allowed = block_mask(segment_row_span, first_row, block)
        scores = jnp.where(allowed[:, None], scores, MASKED)
        weights_soft = jnp.exp(scores - sums_part[..., None])
        grad_soft = jnp.einsum(
            "qrhe,krhe->rhqk", grad_part, values_all, preferred_element_type=jnp.float32
        )
        grad_scores = weights_soft * (
            grad_soft - jnp.sum(weights_soft * grad_soft, axis=-1, keepdims=True)
        )
        grad_scores = grad_scores.astype(jnp.bfloat16)
        grad_query = (
            jnp.einsum("rhqk,krhe->qrhe", grad_scores, keys_all, preferred_element_type=jnp.float32)
            * factor
        )
        grad_keys = (
            grad_keys
            + jnp.einsum(
                "rhqk,qrhe->krhe", grad_scores, query_part, preferred_element_type=jnp.float32
            )
            * factor
        )
        grad_values = grad_values + jnp.einsum(
            "rhqk,qrhe->krhe",
            weights_soft.astype(jnp.bfloat16),
            grad_part,
            preferred_element_type=jnp.float32,
        )
        return ((grad_keys, grad_values), grad_query)

    start_state = (jnp.zeros(keys_all.shape, jnp.float32), jnp.zeros(values_all.shape, jnp.float32))
    (grad_keys, grad_values), grad_blocks = lax.scan(
        one_block, start_state, jnp.arange(length // block)
    )
    return (grad_blocks.reshape(queries.shape), grad_keys, grad_values)


def attend_all(stacked_weights, segment_row_span):
    length, row_count = (stacked_weights.shape[0], stacked_weights.shape[1])
    head_view = stacked_weights.reshape(length, row_count, 3, -1, HEAD_DIM)
    queries, keys_all, values_all = (head_view[:, :, 0], head_view[:, :, 1], head_view[:, :, 2])
    attended, log_sums = attention_forward(queries, keys_all, values_all, segment_row_span)
    return (
        attended.reshape(length, row_count, -1).astype(jnp.bfloat16),
        log_sums,
        (queries, keys_all, values_all),
    )


def attention_project(attended_b, w_out):
    return lax.psum_scatter(
        jnp.einsum("srf,fd->srd", attended_b, w_out, preferred_element_type=jnp.float32).astype(
            jnp.bfloat16
        ),
        "tensor",
        scatter_dimension=0,
        tiled=True,
    ).astype(jnp.float32)


def attention_grad_heads(grad_middle_b, w_out):
    grad_attended = jnp.einsum(
        "srd,fd->srf",
        lax.all_gather(grad_middle_b, "tensor", axis=0, tiled=True),
        w_out,
        preferred_element_type=jnp.float32,
    )
    return grad_attended.astype(jnp.bfloat16)


def mlp_pre(normed_b, w_fc):
    return jnp.einsum(
        "srd,df->srf",
        lax.all_gather(normed_b, "tensor", axis=0, tiled=True),
        w_fc,
        preferred_element_type=jnp.float32,
    )


def mlp_out(hidden_b, w_proj):
    return lax.psum_scatter(
        jnp.einsum("srf,fd->srd", hidden_b, w_proj, preferred_element_type=jnp.float32).astype(
            jnp.bfloat16
        ),
        "tensor",
        scatter_dimension=0,
        tiled=True,
    ).astype(jnp.float32)


def mlp_back(grad_mlp, pre_act, w_fc, w_proj):
    grad_hidden = jnp.einsum(
        "srd,fd->srf",
        lax.all_gather(grad_mlp, "tensor", axis=0, tiled=True),
        w_proj,
        preferred_element_type=jnp.float32,
    )
    activated, slope = jax.vjp(gelu_tanh, pre_act)
    grad_pre = slope(grad_hidden)[0].astype(jnp.bfloat16)
    return lax.psum_scatter(
        jnp.einsum("srf,df->srd", grad_pre, w_fc, preferred_element_type=jnp.float32).astype(
            jnp.bfloat16
        ),
        "tensor",
        scatter_dimension=0,
        tiled=True,
    ).astype(jnp.float32)


def forward_layer_step(layer_input_rows, segment_row_span, fixed_weights, adapter_pair):
    norm_rows = normalize(layer_input_rows, fixed_weights[0])[0].astype(jnp.bfloat16)
    stacked_weights = projected_rows(
        lax.all_gather(norm_rows, "tensor", axis=0, tiled=True), fixed_weights[1], adapter_pair
    )[0]
    attended_b = attend_all(stacked_weights, segment_row_span)[0]
    middle = layer_input_rows + attention_project(attended_b, fixed_weights[2])
    normed_mlp = normalize(middle, fixed_weights[3])[0].astype(jnp.bfloat16)
    pre_act = mlp_pre(normed_mlp, fixed_weights[4])
    hidden_b = gelu_tanh(pre_act).astype(jnp.bfloat16)
    return middle + mlp_out(hidden_b, fixed_weights[5])


def backward_layer_step(
    layer_input_rows, segment_row_span, upstream_gradient, fixed_weights, adapter_pair
):
    gain_a, joint_projection_weight, w_out, gain_m, w_fc, w_proj = fixed_weights
    query_down_factor, query_up_factor, value_down_factor, value_up_factor = adapter_pair
    factor = 32.0 / query_down_factor.shape[-1]
    norm_rows, unit_first, inverse_first = normalize(layer_input_rows, gain_a)
    collected_rows = lax.all_gather(norm_rows.astype(jnp.bfloat16), "tensor", axis=0, tiled=True)
    stacked_weights, narrow_query_rows, narrow_value_rows = projected_rows(
        collected_rows, joint_projection_weight, adapter_pair
    )
    length, row_count = (collected_rows.shape[0], collected_rows.shape[1])
    attended_b, log_sums, head_views = attend_all(stacked_weights, segment_row_span)
    queries, keys_all, values_all = head_views
    middle = layer_input_rows + attention_project(attended_b, w_out)
    normed_mlp, unit_second, inverse_second = normalize(middle, gain_m)
    pre_act = mlp_pre(normed_mlp.astype(jnp.bfloat16), w_fc)
    grad_norm_mlp = mlp_back(upstream_gradient.astype(jnp.bfloat16), pre_act, w_fc, w_proj)
    grad_middle = upstream_gradient + normalize_back(
        grad_norm_mlp, unit_second, inverse_second, gain_m
    )
    grad_attended = attention_grad_heads(grad_middle.astype(jnp.bfloat16), w_out)
    grad_heads = grad_attended.reshape(queries.shape)
    grad_queries, grad_keys, grad_values = attention_backward(
        queries, keys_all, values_all, segment_row_span, log_sums, grad_heads
    )
    grad_stack = (
        jnp.stack([grad_queries, grad_keys, grad_values], axis=2)
        .astype(jnp.bfloat16)
        .reshape(length, row_count, 3, -1)
    )
    grad_query_rows = grad_stack[:, :, 0]
    grad_value_rows = grad_stack[:, :, 2]
    thin_grad_query = factor * jnp.einsum(
        "srf,kf->srk", grad_query_rows, query_up_factor, preferred_element_type=jnp.float32
    )
    thin_grad_value = factor * jnp.einsum(
        "srf,kf->srk", grad_value_rows, value_up_factor, preferred_element_type=jnp.float32
    )
    grad_bq = factor * jnp.einsum(
        "srk,srf->kf", narrow_query_rows, grad_query_rows.astype(jnp.float32), precision=PRECISE
    )
    grad_bv = factor * jnp.einsum(
        "srk,srf->kf", narrow_value_rows, grad_value_rows.astype(jnp.float32), precision=PRECISE
    )
    gathered_wide = collected_rows.astype(jnp.float32)
    grad_aq = jnp.einsum("srd,srk->dk", gathered_wide, thin_grad_query, precision=PRECISE)
    grad_av = jnp.einsum("srd,srk->dk", gathered_wide, thin_grad_value, precision=PRECISE)
    a_query_wide = query_down_factor.astype(jnp.float32)
    a_value_wide = value_down_factor.astype(jnp.float32)
    term = jnp.einsum(
        "srcf,dcf->srd", grad_stack, joint_projection_weight, preferred_element_type=jnp.float32
    )
    term = term + jnp.einsum("srk,dk->srd", thin_grad_query, a_query_wide, precision=PRECISE)
    grad_norm_attn = lax.psum_scatter(
        (term + jnp.einsum("srk,dk->srd", thin_grad_value, a_value_wide, precision=PRECISE)).astype(
            jnp.bfloat16
        ),
        "tensor",
        scatter_dimension=0,
        tiled=True,
    ).astype(jnp.float32)
    layer_output_rows = grad_middle + normalize_back(
        grad_norm_attn, unit_first, inverse_first, gain_a
    )
    return (layer_output_rows, (grad_aq, grad_bq, grad_av, grad_bv))


def body(
    inputs,
    segments,
    cotangent,
    gain_attn,
    joint_projection_weight,
    query_down_factor,
    query_up_factor,
    value_down_factor,
    value_up_factor,
    w_out,
    gain_mlp,
    w_fc,
    w_proj,
):
    fixed_weights = (
        gain_attn[0],
        joint_projection_weight[0],
        w_out[0],
        gain_mlp[0],
        w_fc[0],
        w_proj[0],
    )
    adapter_pair = (
        query_down_factor[0],
        query_up_factor[0],
        value_down_factor[0],
        value_up_factor[0],
    )
    sections = lax.axis_size("section")
    section_index = lax.axis_index("section")
    is_first = section_index == 0
    is_last = section_index == sections - 1
    rows_mb = inputs.shape[1] // MICRO
    ticks = MICRO + sections - 1
    block_shape = (inputs.shape[0], rows_mb, inputs.shape[2])
    activations = jnp.zeros_like(inputs)
    kept_inputs = jnp.zeros((MICRO,) + block_shape, jnp.bfloat16)
    arriving = jnp.zeros(block_shape, jnp.bfloat16)
    for tick_index in range(ticks):
        own_index = min(tick_index, MICRO - 1)
        mb_slot = tick_index - section_index
        is_valid = (mb_slot >= 0) & (mb_slot < MICRO)
        mb_slot = jnp.clip(mb_slot, 0, MICRO - 1)
        fresh = lax.slice_in_dim(inputs, own_index * rows_mb, (own_index + 1) * rows_mb, axis=1)
        layer_input_rows = jnp.where(is_first, fresh, arriving)
        segment_row_span = lax.dynamic_slice_in_dim(segments, mb_slot * rows_mb, rows_mb, 0)
        layer_output_rows = forward_layer_step(
            layer_input_rows.astype(jnp.float32), segment_row_span, fixed_weights, adapter_pair
        ).astype(jnp.bfloat16)
        activations = jnp.where(
            is_valid,
            lax.dynamic_update_slice_in_dim(activations, layer_output_rows, mb_slot * rows_mb, 1),
            activations,
        )
        kept_inputs = jnp.where(
            is_valid, kept_inputs.at[mb_slot].set(layer_input_rows), kept_inputs
        )
        if tick_index < ticks - 1:
            arriving = passed_along(layer_output_rows, "section", 1)
    input_grads = jnp.zeros_like(inputs)
    gradient_totals = tuple(
        (jnp.zeros(factor_tensor.shape, jnp.float32) for factor_tensor in adapter_pair)
    )
    arriving = jnp.zeros(block_shape, jnp.bfloat16)
    for tick_index in range(ticks):
        own_index = min(tick_index, MICRO - 1)
        mb_slot = tick_index - (sections - 1 - section_index)
        is_valid = (mb_slot >= 0) & (mb_slot < MICRO)
        mb_slot = jnp.clip(mb_slot, 0, MICRO - 1)
        given = lax.slice_in_dim(cotangent, own_index * rows_mb, (own_index + 1) * rows_mb, axis=1)
        upstream_gradient = jnp.where(is_last, given, arriving).astype(jnp.float32)
        layer_input_rows = kept_inputs[mb_slot].astype(jnp.float32)
        segment_row_span = lax.dynamic_slice_in_dim(segments, mb_slot * rows_mb, rows_mb, 0)
        layer_output_rows, row_pieces = backward_layer_step(
            layer_input_rows, segment_row_span, upstream_gradient, fixed_weights, adapter_pair
        )
        leaving_b = layer_output_rows.astype(jnp.bfloat16)
        input_grads = jnp.where(
            is_valid,
            lax.dynamic_update_slice_in_dim(input_grads, leaving_b, mb_slot * rows_mb, 1),
            input_grads,
        )
        gradient_totals = tuple(
            (
                running + jnp.where(is_valid, piece_grad, 0.0)
                for running, piece_grad in zip(gradient_totals, row_pieces)
            )
        )
        if tick_index < ticks - 1:
            arriving = passed_along(leaving_b, "section", -1)
    adapter_rank = adapter_pair[1].shape[0]
    model_width = inputs.shape[2]
    column_total = adapter_pair[1].shape[1]
    offset = lax.axis_index("tensor") * column_total
    full_query = lax.dynamic_update_slice_in_dim(
        jnp.zeros((adapter_rank, model_width), jnp.float32), gradient_totals[1], offset, 1
    )
    full_value = lax.dynamic_update_slice_in_dim(
        jnp.zeros((adapter_rank, model_width), jnp.float32), gradient_totals[3], offset, 1
    )
    summed = lax.psum(
        (gradient_totals[0], full_query, gradient_totals[2], full_value), ("dp", "tensor")
    )
    return (
        activations[None],
        input_grads[None],
        summed[0][None],
        summed[1][None],
        summed[2][None],
        summed[3][None],
    )


ROUTE_AXES = ("section", "dp", "tensor")
REACH = 512
BF16 = jnp.bfloat16
F32 = jnp.float32


def route(planes, rule):
    pairs = []
    for c in range(2):
        for z in range(planes):
            for y in range(2):
                for x in range(2):
                    target = rule(c, z, y, x)
                    if target is not None:
                        tc, tz, ty, tx = target
                        pairs.append(
                            ((c * planes + z) * 4 + 2 * y + x, (tc * planes + tz) * 4 + 2 * ty + tx)
                        )
    return pairs


def dot_nn(a, b):
    return lax.dot_general(a, b, (((1,), (0,)), ((), ())), preferred_element_type=F32)


def dot_nt(a, b):
    return lax.dot_general(a, b, (((1,), (1,)), ((), ())), preferred_element_type=F32)


def dot_tn(a, b):
    return lax.dot_general(a, b, (((0,), (0,)), ((), ())), preferred_element_type=F32)


def norm_stats(rows):
    middle = jnp.mean(rows, axis=-1, keepdims=True)
    centred = rows - middle
    inverse = lax.rsqrt(jnp.mean(centred * centred, axis=-1, keepdims=True) + EPSILON)
    return centred * inverse, inverse


def key_span(i, block):
    return max(0, i - REACH // block) * block, (i + 1) * block


def allowed_keys(i, block, seg_col_ref, seg_row_ref):
    low, high = key_span(i, block)
    seg_q = seg_col_ref[i * block : (i + 1) * block, :]
    seg_k = seg_row_ref[:, low:high]
    places_q = i * block + lax.broadcasted_iota(jnp.int32, (block, high - low), 0)
    places_k = low + lax.broadcasted_iota(jnp.int32, (block, high - low), 1)
    return (seg_q == seg_k) & (places_k <= places_q)


def head_lanes(rows, h):
    lane = lax.broadcasted_iota(jnp.int32, (rows, 128), 1)
    return (lane < HEAD_DIM) if h == 0 else (lane >= HEAD_DIM)


def attention_forward_kernel(block, width, qkv_ref, seg_col_ref, seg_row_ref, out_ref):
    length = qkv_ref.shape[0]
    for i in range(length // block):
        low, high = key_span(i, block)
        rows = slice(i * block, (i + 1) * block)
        allowed = allowed_keys(i, block, seg_col_ref, seg_row_ref)
        for pair in range(width // 128):
            lanes = slice(pair * 128, pair * 128 + 128)
            queries = qkv_ref[rows, lanes] * BF16(HEAD_DIM**-0.5)
            keys = qkv_ref[low:high, width + pair * 128 : width + pair * 128 + 128]
            values = qkv_ref[low:high, 2 * width + pair * 128 : 2 * width + pair * 128 + 128]
            parts = []
            for h in range(2):
                mine = jnp.where(head_lanes(block, h), queries, BF16(0))
                scores = jnp.where(allowed, dot_nt(mine, keys), MASKED)
                exponent = jnp.exp(scores - jnp.max(scores, axis=-1, keepdims=True))
                total = jnp.sum(exponent, axis=-1, keepdims=True)
                parts.append(dot_nn(exponent.astype(BF16), values) / total)
            out_ref[rows, lanes] = jnp.where(head_lanes(block, 0), parts[0], parts[1]).astype(BF16)


def attention_backward_kernel(
    block, width, qkv_ref, grad_ref, seg_col_ref, seg_row_ref, out_ref, dk_ref, dv_ref
):
    length = qkv_ref.shape[0]
    scale = HEAD_DIM**-0.5
    for pair in range(width // 128):
        lanes = slice(pair * 128, pair * 128 + 128)
        lanes_k = slice(width + pair * 128, width + pair * 128 + 128)
        lanes_v = slice(2 * width + pair * 128, 2 * width + pair * 128 + 128)
        dk_ref[...] = jnp.zeros_like(dk_ref)
        dv_ref[...] = jnp.zeros_like(dv_ref)
        for i in range(length // block):
            low, high = key_span(i, block)
            rows = slice(i * block, (i + 1) * block)
            allowed = allowed_keys(i, block, seg_col_ref, seg_row_ref)
            queries = qkv_ref[rows, lanes] * BF16(scale)
            keys = qkv_ref[low:high, lanes_k]
            values = qkv_ref[low:high, lanes_v]
            grads = grad_ref[rows, lanes]
            parts = []
            for h in range(2):
                mine = jnp.where(head_lanes(block, h), queries, BF16(0))
                grad = jnp.where(head_lanes(block, h), grads, BF16(0))
                scores = jnp.where(allowed, dot_nt(mine, keys), MASKED)
                exponent = jnp.exp(scores - jnp.max(scores, axis=-1, keepdims=True))
                soft = exponent * (1.0 / jnp.sum(exponent, axis=-1, keepdims=True))
                grad_soft = dot_nt(grad, values)
                weighted = soft * grad_soft
                grad_scores = (
                    weighted - soft * jnp.sum(weighted, axis=-1, keepdims=True)
                ).astype(BF16)
                parts.append(dot_nn(grad_scores, keys))
                dk_ref[low:high, :] += dot_tn(grad_scores, mine)
                dv_ref[low:high, :] += dot_tn(soft.astype(BF16), grad)
            out_ref[rows, lanes] = (
                jnp.where(head_lanes(block, 0), parts[0], parts[1]) * scale
            ).astype(BF16)
        out_ref[:, lanes_k] = dk_ref[...].astype(BF16)
        out_ref[:, lanes_v] = dv_ref[...].astype(BF16)


SLOTS = 3


def weight_stream(core_ref, own_refs, twin_refs, fc_buf, proj_buf, sems, chunk):
    width = own_refs[0].shape[0]
    per = width // chunk
    first = core_ref[0] == 0

    def copies(k, slot, flag):
        array = k // per
        cut = pl.ds((k % per) * chunk, chunk)
        fc_from, proj_from = (own_refs, twin_refs) if flag else (twin_refs, own_refs)
        return (
            pltpu.make_async_copy(fc_from[array].at[:, cut], fc_buf.at[slot], sems.at[0, slot]),
            pltpu.make_async_copy(proj_from[array].at[cut, :], proj_buf.at[slot], sems.at[1, slot]),
        )

    def start(k):
        @pl.when(first)
        def _():
            for copy in copies(k, k % SLOTS, True):
                copy.start()

        @pl.when(jnp.logical_not(first))
        def _():
            for copy in copies(k, k % SLOTS, False):
                copy.start()

    def wait(k):
        for copy in copies(k, k % SLOTS, True):
            copy.wait()

    return start, wait, per * len(own_refs)


def mlp_forward_kernel(
    chunk, arrays, core_ref, x_ref, o_ref, w_out_ref, gain_ref, *refs
):
    own_refs, twin_refs = refs[:arrays], refs[arrays : 2 * arrays]
    middle_ref, pre_ref, act_ref, fc_buf, proj_buf, sems = refs[2 * arrays :]
    start, wait, steps = weight_stream(core_ref, own_refs, twin_refs, fc_buf, proj_buf, sems, chunk)
    for k in range(min(SLOTS - 1, steps)):
        start(k)
    middle = x_ref[...].astype(F32) + dot_nn(o_ref[...], w_out_ref[...])
    middle_ref[...] = middle
    unit, _ = norm_stats(middle)
    normed = (unit * gain_ref[...]).astype(BF16)
    total = middle
    for k in range(steps):
        wait(k)
        if k + SLOTS - 1 < steps:
            start(k + SLOTS - 1)
        pre = dot_nn(normed, fc_buf[k % SLOTS])
        pre_ref[:, k * chunk : (k + 1) * chunk] = pre.astype(BF16)
        hidden = gelu_tanh(pre).astype(BF16)
        total = total + dot_nn(hidden, proj_buf[k % SLOTS])
    act_ref[...] = total.astype(BF16)


def mlp_backward_kernel(
    chunk, arrays, core_ref, up_ref, middle_ref, pre_ref, w_out_ref, gain_ref, *refs
):
    own_refs, twin_refs = refs[:arrays], refs[arrays : 2 * arrays]
    grad_ref, heads_ref, fc_buf, proj_buf, sems = refs[2 * arrays :]
    start, wait, steps = weight_stream(core_ref, own_refs, twin_refs, fc_buf, proj_buf, sems, chunk)
    for k in range(min(SLOTS - 1, steps)):
        start(k)
    upstream = up_ref[...]
    grad_norm = None
    for k in range(steps):
        wait(k)
        if k + SLOTS - 1 < steps:
            start(k + SLOTS - 1)
        grad_hidden = dot_nt(upstream, proj_buf[k % SLOTS])
        pre = pre_ref[:, k * chunk : (k + 1) * chunk].astype(F32)
        square = pre * pre
        bent = jnp.tanh(TANH_SCALE * (pre + CUBIC_TERM * square * pre))
        slope = 0.5 * (1.0 + bent) + (0.5 * TANH_SCALE) * pre * (1.0 - bent * bent) * (
            1.0 + (3.0 * CUBIC_TERM) * square
        )
        term = dot_nt((grad_hidden * slope).astype(BF16), fc_buf[k % SLOTS])
        grad_norm = term if grad_norm is None else grad_norm + term
    unit, inverse = norm_stats(middle_ref[...])
    grad_middle = upstream.astype(F32) + normalize_back(grad_norm, unit, inverse, gain_ref[...])
    grad_ref[...] = grad_middle
    heads_ref[...] = dot_nt(grad_middle.astype(BF16), w_out_ref[...]).astype(BF16)


def in_vmem():
    return pl.BlockSpec(memory_space=pltpu.VMEM)


def kernel_params():
    return pltpu.CompilerParams(vmem_limit_bytes=48 * 1024 * 1024)


def attend_forward(qkv, seg_col, seg_row, block):
    length, wide = qkv.shape
    width = wide // 3
    return pl.pallas_call(
        functools.partial(attention_forward_kernel, block, width),
        out_shape=jax.ShapeDtypeStruct((length, width), BF16),
        in_specs=[in_vmem()] * 3,
        out_specs=in_vmem(),
        compiler_params=kernel_params(),
        cost_estimate=pl.CostEstimate(
            flops=6_000_000_000, bytes_accessed=2_000_000, transcendentals=0
        ),
    )(qkv, seg_col, seg_row)


def attend_backward(qkv, grads, seg_col, seg_row, block):
    length, wide = qkv.shape
    width = wide // 3
    return pl.pallas_call(
        functools.partial(attention_backward_kernel, block, width),
        out_shape=jax.ShapeDtypeStruct((length, wide), BF16),
        in_specs=[in_vmem()] * 4,
        out_specs=in_vmem(),
        scratch_shapes=[pltpu.VMEM((length, 128), F32), pltpu.VMEM((length, 128), F32)],
        compiler_params=kernel_params(),
        cost_estimate=pl.CostEstimate(
            flops=12_000_000_000, bytes_accessed=4_000_000, transcendentals=0
        ),
    )(qkv, grads, seg_col, seg_row)


def mlp_call(kernel, core, given, weights, outs, chunk):
    own, twin = weights
    anywhere = pl.BlockSpec(memory_space=pl.ANY)
    width = own[0].shape[1]
    return pl.pallas_call(
        functools.partial(kernel, chunk, len(own)),
        out_shape=outs,
        in_specs=[pl.BlockSpec(memory_space=pltpu.SMEM)]
        + [in_vmem()] * len(given)
        + [anywhere] * (2 * len(own)),
        out_specs=[in_vmem()] * len(outs),
        scratch_shapes=[
            pltpu.VMEM((SLOTS, width, chunk), BF16),
            pltpu.VMEM((SLOTS, chunk, width), BF16),
            pltpu.SemaphoreType.DMA((2, SLOTS)),
        ],
        compiler_params=kernel_params(),
        cost_estimate=pl.CostEstimate(
            flops=5_000_000_000, bytes_accessed=20_000_000, transcendentals=0
        ),
    )(core, *given, *own, *twin)


def fast_body(
    planes,
    inputs,
    segments,
    cotangent,
    gain_attn,
    joint_projection_weight,
    query_down_factor,
    query_up_factor,
    value_down_factor,
    value_up_factor,
    w_out,
    gain_mlp,
    w_fc,
    w_proj,
):
    core = lax.axis_index("section")
    place = lax.axis_index("tensor")
    y, x = place // 2, place % 2
    block, _, model = inputs.shape
    width = joint_projection_weight.shape[3]
    rank = query_down_factor.shape[2]
    factor = 32.0 / rank
    core_0, y_0, x_0 = core == 0, y == 0, x == 0

    def sent(value, rule):
        return lax.ppermute(value, ROUTE_AXES, route(planes, rule))

    def c_flip(value):
        return sent(value, lambda c, z, y, x: (1 - c, z, y, x))

    def y_flip(value):
        return sent(value, lambda c, z, y, x: (c, z, 1 - y, x))

    def x_flip(value):
        return sent(value, lambda c, z, y, x: (c, z, y, 1 - x))

    def z_flip(value, bit):
        return sent(value, lambda c, z, y, x: (c, z ^ bit, y, x))

    def in_order(first, one, other):
        return jnp.concatenate(
            [jnp.where(first, one, other), jnp.where(first, other, one)], axis=0
        )

    def both_layers(own):
        twin = c_flip(own)
        return jnp.where(core_0, own, twin), jnp.where(core_0, twin, own)

    def to_row(array):
        mine = jnp.where(x_0, array[:, 0], array[:, 1])
        other = jnp.where(x_0, array[:, 1], array[:, 0])
        came = sent(other, lambda c, z, y, x: (c, z, y, 1 - x) if c == x else None)
        return jnp.where(core == x, mine, came)

    layer_input = to_row(inputs)
    segment_row = jnp.where(x_0, segments[0], segments[1])
    seg_col, seg_row = segment_row[:, None], segment_row[None, :]
    small = jnp.concatenate(
        [
            gain_attn,
            gain_mlp,
            query_down_factor[0].T.astype(F32),
            value_down_factor[0].T.astype(F32),
        ],
        axis=0,
    )
    smalls = both_layers(small)
    gains_a = [s[0:1] for s in smalls]
    gains_m = [s[1:2] for s in smalls]
    downs = [s[2 : 2 + 2 * rank].T.astype(BF16) for s in smalls]

    blank = jnp.zeros((rank, width), BF16)
    ups_own = jnp.concatenate(
        [
            jnp.concatenate([query_up_factor[0], blank, blank], axis=1),
            jnp.concatenate([blank, blank, value_up_factor[0]], axis=1),
        ],
        axis=0,
    )
    packed = jnp.concatenate(
        [joint_projection_weight[0].reshape(model, 3 * width), ups_own, jnp.zeros_like(ups_own)],
        axis=0,
    )
    heads_weights = []
    for own in both_layers(packed):
        came = sent(own, lambda c, z, y, x: (c, z, y, 1 - x) if c == x else None)
        heads_weights.append(jnp.where(core == x, own, came))
    w_qkv = [w[:model] for w in heads_weights]
    ups = [w[model : model + 2 * rank] for w in heads_weights]
    w_outs = both_layers(lax.all_gather(w_out[0], "tensor", axis=0, tiled=True))

    twin = c_flip(jnp.where(core_0, w_proj[0], w_fc[0]))
    kept = jnp.where(core_0, w_fc[0], w_proj[0])
    half = model // 2
    ff_weights = []
    before = None
    for own in (jnp.where(core_0, kept, twin), jnp.where(core_0, twin, kept)):
        if before is not None:
            own, _ = lax.optimization_barrier((own, before))
        over_x = x_flip(own)
        over_y = y_flip(own)
        diagonal = jnp.concatenate([y_flip(over_x[:half]), x_flip(over_y[half:])], axis=0)
        arrays = (own, over_x, over_y, diagonal)
        ff_weights.append((arrays, tuple(c_flip(a) for a in arrays)))
        before = over_y
    core_id = core.astype(jnp.int32).reshape(1)

    def gathered(own):
        over_y = y_flip(own)
        chip = in_order(core_0, own, c_flip(own))
        across = in_order(core_0, over_y, c_flip(over_y))
        return in_order(y_0, chip, across)

    def split(array):
        upper, lower = array[: 2 * block], array[2 * block :]
        return jnp.where(y_0, upper, lower), jnp.where(y_0, lower, upper)

    def mine_and_twins(pair):
        upper, lower = pair[:block], pair[block:]
        return jnp.where(core_0, upper, lower), jnp.where(core_0, lower, upper)

    def heads_to_slots(attended):
        here, there = split(attended)
        here_mine, here_twin = mine_and_twins(here)
        there_mine, there_twin = mine_and_twins(there)
        came = c_flip(jnp.concatenate([here_twin, there_twin], axis=0))
        here_all = in_columns(core_0, here_mine, came[:block])
        there_all = in_columns(core_0, there_mine, came[block:])
        return in_columns(y_0, here_all, y_flip(there_all))

    def in_columns(first, one, other):
        return jnp.concatenate(
            [jnp.where(first, one, other), jnp.where(first, other, one)], axis=1
        )

    def slots_to_heads(slots):
        left, right = slots[:, : 2 * width], slots[:, 2 * width :]
        across = y_flip(jnp.where(y_0, right, left))
        pair = jnp.concatenate([jnp.where(y_0, left, right), across], axis=0)
        left, right = pair[:, :width], pair[:, width:]
        came = c_flip(jnp.where(core_0, right, left))
        own = jnp.where(core_0, left, right)
        here = in_order(core_0, own[:block], came[:block])
        there = in_order(core_0, own[block:], came[block:])
        return in_order(y_0, here, there)

    kept_layers = []
    acts = []
    for layer in range(2):
        unit, inverse = norm_stats(layer_input.astype(F32))
        rows = gathered((unit * gains_a[layer]).astype(BF16))
        thin = dot_nn(rows, downs[layer])
        extra = factor * dot_nn(thin.astype(BF16), ups[layer])
        qkv = (dot_nn(rows, w_qkv[layer]) + extra).astype(BF16)
        attended = heads_to_slots(attend_forward(qkv, seg_col, seg_row, block))
        middle, pre_act, act = mlp_call(
            mlp_forward_kernel,
            core_id,
            (layer_input, attended, w_outs[layer], gains_m[layer]),
            ff_weights[layer],
            (
                jax.ShapeDtypeStruct((block, model), F32),
                jax.ShapeDtypeStruct((block, 4 * model), BF16),
                jax.ShapeDtypeStruct((block, model), BF16),
            ),
            512,
        )
        kept_layers.append((layer_input, rows, thin, qkv, middle, pre_act))
        acts.append(act)
        layer_input = act

    grads_in = [None, None]
    sums = [None, None]
    upstream = to_row(cotangent)
    for layer in (1, 0):
        layer_input, rows, thin, qkv, middle, pre_act = kept_layers[layer]
        grad_middle, grad_heads = mlp_call(
            mlp_backward_kernel,
            core_id,
            (upstream, middle, pre_act, w_outs[layer], gains_m[layer]),
            ff_weights[layer],
            (
                jax.ShapeDtypeStruct((block, model), F32),
                jax.ShapeDtypeStruct((block, model), BF16),
            ),
            512,
        )
        grad_qkv = attend_backward(qkv, slots_to_heads(grad_heads), seg_col, seg_row, block)
        thin_grad = factor * dot_nt(grad_qkv, ups[layer])
        thin_grad_b = thin_grad.astype(BF16)
        term = dot_nt(grad_qkv, w_qkv[layer]) + dot_nt(thin_grad_b, downs[layer])
        here, there = split(term)
        here_mine, here_twin = mine_and_twins(here)
        there_mine, there_twin = mine_and_twins(there)
        came = c_flip(jnp.concatenate([here_twin, there_twin], axis=0).astype(BF16)).astype(F32)
        across = y_flip((there_mine + came[block:]).astype(BF16)).astype(F32)
        grad_norm = here_mine + came[:block] + across
        unit, inverse = norm_stats(layer_input.astype(F32))
        upstream = (
            grad_middle + normalize_back(grad_norm, unit, inverse, gains_a[layer])
        ).astype(BF16)
        grads_in[layer] = upstream
        grad_down = dot_tn(thin_grad_b, rows)
        thin_b = thin.astype(BF16)
        spread = [
            lax.dynamic_update_slice_in_dim(
                jnp.zeros((rank, model), F32), factor * dot_tn(one, grads), (2 * y + core) * width, 1
            )
            for one, grads in (
                (thin_b[:, :rank], grad_qkv[:, :width]),
                (thin_b[:, rank:], grad_qkv[:, 2 * width :]),
            )
        ]
        total = jnp.concatenate([grad_down, *spread], axis=0)
        total = total + c_flip(total)
        total = total + x_flip(total)
        total = total + y_flip(total)
        bit = 1
        while bit < planes:
            total = total + z_flip(total, bit)
            bit *= 2
        sums[layer] = total

    def placed(pair):
        same, other = [], []
        for layer in range(2):
            same.append(
                sent(pair[layer], lambda c, z, y, x: (layer, z, y, x) if c == x else None)
            )
            other.append(
                sent(pair[layer], lambda c, z, y, x: (layer, z, y, 1 - x) if c != x else None)
            )
        same = jnp.where(core_0, same[0], same[1])
        other = jnp.where(core_0, other[0], other[1])
        return jnp.stack([jnp.where(x_0, same, other), jnp.where(x_0, other, same)], axis=1)[None]

    total = jnp.where(core_0, sums[0], sums[1])
    return (
        placed(acts),
        placed(grads_in),
        total[:rank].T[None],
        total[2 * rank : 3 * rank][None],
        total[rank : 2 * rank].T[None],
        total[3 * rank :][None],
    )


def fits_fast(mesh, shapes):
    planes = mesh.shape["dp"]
    return (
        mesh.shape["section"] == 2
        and mesh.shape["tensor"] == 4
        and planes & (planes - 1) == 0
        and shapes[0][1] == 2 * planes
        and shapes[0][0] % 1024 == 0
        and shapes[0][0] // 4 <= REACH
        and REACH % (shapes[0][0] // 4) == 0
    )


def solution(mesh):
    placed = (
        P("tensor", "dp", None),
        P("dp", None),
        P("tensor", "dp", None),
        P("section", None),
        P("section", None, None, "tensor"),
        P("section", None, None),
        P("section", None, "tensor"),
        P("section", None, None),
        P("section", None, "tensor"),
        P("section", "tensor", None),
        P("section", None),
        P("section", None, "tensor"),
        P("section", "tensor", None),
    )
    def choose(*args):
        picked = body
        if fits_fast(mesh, [a.shape for a in args]):
            picked = functools.partial(fast_body, mesh.shape["dp"])
        return mapped(picked)(*args)

    def mapped(picked):
      return jax.shard_map(
        picked,
        mesh=mesh,
        in_specs=placed,
        out_specs=(
            P("section", "tensor", "dp", None),
            P("section", "tensor", "dp", None),
            P("section", None, None),
            P("section", None, None),
            P("section", None, None),
            P("section", None, None),
        ),
        check_vma=False,
    )

    return choose
```

```python
import functools

import jax
import jax.numpy as jnp
from jax import lax
from jax.experimental import pallas as pl
from jax.experimental.pallas import tpu as pltpu
from jax.sharding import PartitionSpec as P

HEAD_DIM = 64
MICRO = 2


EPSILON = 1e-05
PRECISE = lax.Precision.HIGHEST
MASKED = -1000000000.0
CUBIC_TERM = 0.044715
TANH_SCALE = 0.7978845608028654


def passed_along(block, axis, distance):
    devices = range(lax.axis_size(axis))
    route = [(i - distance, i) for i in devices if i - distance in devices]
    return lax.ppermute(block, axis, route)


def gelu_tanh(value):
    return 0.5 * value * (1.0 + jnp.tanh(TANH_SCALE * (value + CUBIC_TERM * value * value * value)))


def normalize(residual_stream, gain):
    middle = jnp.mean(residual_stream, axis=-1, keepdims=True)
    centred = residual_stream - middle
    inverse = lax.rsqrt(jnp.mean(centred * centred, axis=-1, keepdims=True) + EPSILON)
    unit_rows = centred * inverse
    return (unit_rows * gain, unit_rows, inverse)


def normalize_back(grad_norm, unit_rows, inverse, gain):
    scaled = grad_norm * gain
    return inverse * (
        scaled
        - jnp.mean(scaled, axis=-1, keepdims=True)
        - unit_rows * jnp.mean(scaled * unit_rows, axis=-1, keepdims=True)
    )


def block_mask(segment_row_span, first_row, block):
    length = segment_row_span.shape[1]
    segment_part = lax.dynamic_slice_in_dim(segment_row_span, first_row, block, 1)
    query_places = first_row + jnp.arange(block)
    key_places = jnp.arange(length)
    same_doc = segment_part[:, :, None] == segment_row_span[:, None, :]
    return same_doc & (key_places[None, None, :] <= query_places[None, :, None])


def projected_rows(row_portion, joint_projection_weight, adapter_pair):
    query_down_factor, query_up_factor, value_down_factor, value_up_factor = adapter_pair
    factor = 32.0 / query_down_factor.shape[-1]
    joined = jnp.einsum(
        "srd,dcf->srcf", row_portion, joint_projection_weight, preferred_element_type=jnp.float32
    )
    narrow_query_rows = jnp.einsum(
        "srd,dk->srk", row_portion, query_down_factor, preferred_element_type=jnp.float32
    )
    narrow_value_rows = jnp.einsum(
        "srd,dk->srk", row_portion, value_down_factor, preferred_element_type=jnp.float32
    )
    queries = joined[:, :, 0] + factor * jnp.einsum(
        "srk,kf->srf", narrow_query_rows, query_up_factor.astype(jnp.float32), precision=PRECISE
    )
    values_all = joined[:, :, 2] + factor * jnp.einsum(
        "srk,kf->srf", narrow_value_rows, value_up_factor.astype(jnp.float32), precision=PRECISE
    )
    stacked_weights = jnp.stack([queries, joined[:, :, 1], values_all], axis=2).astype(jnp.bfloat16)
    return (stacked_weights, narrow_query_rows, narrow_value_rows)


def attention_forward(queries, keys_all, values_all, segment_row_span):
    length, row_count, head_count, width = queries.shape
    block = min(512, length)
    factor = width ** (-0.5)

    def one_block(block_index):
        first_row = block_index * block
        query_part = lax.dynamic_slice_in_dim(queries, first_row, block, 0)
        scores = (
            jnp.einsum("qrhe,krhe->rhqk", query_part, keys_all, preferred_element_type=jnp.float32)
            * factor
        )
        allowed = block_mask(segment_row_span, first_row, block)
        scores = jnp.where(allowed[:, None], scores, MASKED)
        row_max = jnp.max(scores, axis=-1, keepdims=True)
        exponent = jnp.exp(scores - row_max)
        total = jnp.sum(exponent, axis=-1, keepdims=True)
        weights_soft = (exponent / total).astype(jnp.bfloat16)
        attended = jnp.einsum(
            "rhqk,krhe->qrhe", weights_soft, values_all, preferred_element_type=jnp.float32
        )
        return (attended, (row_max + jnp.log(total))[..., 0])

    attended, log_sums = lax.map(one_block, jnp.arange(length // block))
    attended = attended.reshape(length, row_count, head_count, width)
    log_sums = jnp.moveaxis(log_sums, 0, 2).reshape(row_count, head_count, length)
    return (attended, log_sums)


def attention_backward(queries, keys_all, values_all, segment_row_span, log_sums, grad_heads):
    length = queries.shape[0]
    block = min(512, length)
    factor = queries.shape[-1] ** (-0.5)

    def one_block(carry, block_index):
        grad_keys, grad_values = carry
        first_row = block_index * block
        query_part = lax.dynamic_slice_in_dim(queries, first_row, block, 0)
        grad_part = lax.dynamic_slice_in_dim(grad_heads, first_row, block, 0)
        sums_part = lax.dynamic_slice_in_dim(log_sums, first_row, block, 2)
        scores = (
            jnp.einsum("qrhe,krhe->rhqk", query_part, keys_all, preferred_element_type=jnp.float32)
            * factor
        )
        allowed = block_mask(segment_row_span, first_row, block)
        scores = jnp.where(allowed[:, None], scores, MASKED)
        weights_soft = jnp.exp(scores - sums_part[..., None])
        grad_soft = jnp.einsum(
            "qrhe,krhe->rhqk", grad_part, values_all, preferred_element_type=jnp.float32
        )
        grad_scores = weights_soft * (
            grad_soft - jnp.sum(weights_soft * grad_soft, axis=-1, keepdims=True)
        )
        grad_scores = grad_scores.astype(jnp.bfloat16)
        grad_query = (
            jnp.einsum("rhqk,krhe->qrhe", grad_scores, keys_all, preferred_element_type=jnp.float32)
            * factor
        )
        grad_keys = (
            grad_keys
            + jnp.einsum(
                "rhqk,qrhe->krhe", grad_scores, query_part, preferred_element_type=jnp.float32
            )
            * factor
        )
        grad_values = grad_values + jnp.einsum(
            "rhqk,qrhe->krhe",
            weights_soft.astype(jnp.bfloat16),
            grad_part,
            preferred_element_type=jnp.float32,
        )
        return ((grad_keys, grad_values), grad_query)

    start_state = (jnp.zeros(keys_all.shape, jnp.float32), jnp.zeros(values_all.shape, jnp.float32))
    (grad_keys, grad_values), grad_blocks = lax.scan(
        one_block, start_state, jnp.arange(length // block)
    )
    return (grad_blocks.reshape(queries.shape), grad_keys, grad_values)


def attend_all(stacked_weights, segment_row_span):
    length, row_count = (stacked_weights.shape[0], stacked_weights.shape[1])
    head_view = stacked_weights.reshape(length, row_count, 3, -1, HEAD_DIM)
    queries, keys_all, values_all = (head_view[:, :, 0], head_view[:, :, 1], head_view[:, :, 2])
    attended, log_sums = attention_forward(queries, keys_all, values_all, segment_row_span)
    return (
        attended.reshape(length, row_count, -1).astype(jnp.bfloat16),
        log_sums,
        (queries, keys_all, values_all),
    )


def attention_project(attended_b, w_out):
    return lax.psum_scatter(
        jnp.einsum("srf,fd->srd", attended_b, w_out, preferred_element_type=jnp.float32).astype(
            jnp.bfloat16
        ),
        "tensor",
        scatter_dimension=0,
        tiled=True,
    ).astype(jnp.float32)


def attention_grad_heads(grad_middle_b, w_out):
    grad_attended = jnp.einsum(
        "srd,fd->srf",
        lax.all_gather(grad_middle_b, "tensor", axis=0, tiled=True),
        w_out,
        preferred_element_type=jnp.float32,
    )
    return grad_attended.astype(jnp.bfloat16)


def mlp_pre(normed_b, w_fc):
    return jnp.einsum(
        "srd,df->srf",
        lax.all_gather(normed_b, "tensor", axis=0, tiled=True),
        w_fc,
        preferred_element_type=jnp.float32,
    )


def mlp_out(hidden_b, w_proj):
    return lax.psum_scatter(
        jnp.einsum("srf,fd->srd", hidden_b, w_proj, preferred_element_type=jnp.float32).astype(
            jnp.bfloat16
        ),
        "tensor",
        scatter_dimension=0,
        tiled=True,
    ).astype(jnp.float32)


def mlp_back(grad_mlp, pre_act, w_fc, w_proj):
    grad_hidden = jnp.einsum(
        "srd,fd->srf",
        lax.all_gather(grad_mlp, "tensor", axis=0, tiled=True),
        w_proj,
        preferred_element_type=jnp.float32,
    )
    activated, slope = jax.vjp(gelu_tanh, pre_act)
    grad_pre = slope(grad_hidden)[0].astype(jnp.bfloat16)
    return lax.psum_scatter(
        jnp.einsum("srf,df->srd", grad_pre, w_fc, preferred_element_type=jnp.float32).astype(
            jnp.bfloat16
        ),
        "tensor",
        scatter_dimension=0,
        tiled=True,
    ).astype(jnp.float32)


def forward_layer_step(layer_input_rows, segment_row_span, fixed_weights, adapter_pair):
    norm_rows = normalize(layer_input_rows, fixed_weights[0])[0].astype(jnp.bfloat16)
    stacked_weights = projected_rows(
        lax.all_gather(norm_rows, "tensor", axis=0, tiled=True), fixed_weights[1], adapter_pair
    )[0]
    attended_b = attend_all(stacked_weights, segment_row_span)[0]
    middle = layer_input_rows + attention_project(attended_b, fixed_weights[2])
    normed_mlp = normalize(middle, fixed_weights[3])[0].astype(jnp.bfloat16)
    pre_act = mlp_pre(normed_mlp, fixed_weights[4])
    hidden_b = gelu_tanh(pre_act).astype(jnp.bfloat16)
    return middle + mlp_out(hidden_b, fixed_weights[5])


def backward_layer_step(
    layer_input_rows, segment_row_span, upstream_gradient, fixed_weights, adapter_pair
):
    gain_a, joint_projection_weight, w_out, gain_m, w_fc, w_proj = fixed_weights
    query_down_factor, query_up_factor, value_down_factor, value_up_factor = adapter_pair
    factor = 32.0 / query_down_factor.shape[-1]
    norm_rows, unit_first, inverse_first = normalize(layer_input_rows, gain_a)
    collected_rows = lax.all_gather(norm_rows.astype(jnp.bfloat16), "tensor", axis=0, tiled=True)
    stacked_weights, narrow_query_rows, narrow_value_rows = projected_rows(
        collected_rows, joint_projection_weight, adapter_pair
    )
    length, row_count = (collected_rows.shape[0], collected_rows.shape[1])
    attended_b, log_sums, head_views = attend_all(stacked_weights, segment_row_span)
    queries, keys_all, values_all = head_views
    middle = layer_input_rows + attention_project(attended_b, w_out)
    normed_mlp, unit_second, inverse_second = normalize(middle, gain_m)
    pre_act = mlp_pre(normed_mlp.astype(jnp.bfloat16), w_fc)
    grad_norm_mlp = mlp_back(upstream_gradient.astype(jnp.bfloat16), pre_act, w_fc, w_proj)
    grad_middle = upstream_gradient + normalize_back(
        grad_norm_mlp, unit_second, inverse_second, gain_m
    )
    grad_attended = attention_grad_heads(grad_middle.astype(jnp.bfloat16), w_out)
    grad_heads = grad_attended.reshape(queries.shape)
    grad_queries, grad_keys, grad_values = attention_backward(
        queries, keys_all, values_all, segment_row_span, log_sums, grad_heads
    )
    grad_stack = (
        jnp.stack([grad_queries, grad_keys, grad_values], axis=2)
        .astype(jnp.bfloat16)
        .reshape(length, row_count, 3, -1)
    )
    grad_query_rows = grad_stack[:, :, 0]
    grad_value_rows = grad_stack[:, :, 2]
    thin_grad_query = factor * jnp.einsum(
        "srf,kf->srk", grad_query_rows, query_up_factor, preferred_element_type=jnp.float32
    )
    thin_grad_value = factor * jnp.einsum(
        "srf,kf->srk", grad_value_rows, value_up_factor, preferred_element_type=jnp.float32
    )
    grad_bq = factor * jnp.einsum(
        "srk,srf->kf", narrow_query_rows, grad_query_rows.astype(jnp.float32), precision=PRECISE
    )
    grad_bv = factor * jnp.einsum(
        "srk,srf->kf", narrow_value_rows, grad_value_rows.astype(jnp.float32), precision=PRECISE
    )
    gathered_wide = collected_rows.astype(jnp.float32)
    grad_aq = jnp.einsum("srd,srk->dk", gathered_wide, thin_grad_query, precision=PRECISE)
    grad_av = jnp.einsum("srd,srk->dk", gathered_wide, thin_grad_value, precision=PRECISE)
    a_query_wide = query_down_factor.astype(jnp.float32)
    a_value_wide = value_down_factor.astype(jnp.float32)
    term = jnp.einsum(
        "srcf,dcf->srd", grad_stack, joint_projection_weight, preferred_element_type=jnp.float32
    )
    term = term + jnp.einsum("srk,dk->srd", thin_grad_query, a_query_wide, precision=PRECISE)
    grad_norm_attn = lax.psum_scatter(
        (term + jnp.einsum("srk,dk->srd", thin_grad_value, a_value_wide, precision=PRECISE)).astype(
            jnp.bfloat16
        ),
        "tensor",
        scatter_dimension=0,
        tiled=True,
    ).astype(jnp.float32)
    layer_output_rows = grad_middle + normalize_back(
        grad_norm_attn, unit_first, inverse_first, gain_a
    )
    return (layer_output_rows, (grad_aq, grad_bq, grad_av, grad_bv))


def body(
    inputs,
    segments,
    cotangent,
    gain_attn,
    joint_projection_weight,
    query_down_factor,
    query_up_factor,
    value_down_factor,
    value_up_factor,
    w_out,
    gain_mlp,
    w_fc,
    w_proj,
):
    fixed_weights = (
        gain_attn[0],
        joint_projection_weight[0],
        w_out[0],
        gain_mlp[0],
        w_fc[0],
        w_proj[0],
    )
    adapter_pair = (
        query_down_factor[0],
        query_up_factor[0],
        value_down_factor[0],
        value_up_factor[0],
    )
    sections = lax.axis_size("section")
    section_index = lax.axis_index("section")
    is_first = section_index == 0
    is_last = section_index == sections - 1
    rows_mb = inputs.shape[1] // MICRO
    ticks = MICRO + sections - 1
    block_shape = (inputs.shape[0], rows_mb, inputs.shape[2])
    activations = jnp.zeros_like(inputs)
    kept_inputs = jnp.zeros((MICRO,) + block_shape, jnp.bfloat16)
    arriving = jnp.zeros(block_shape, jnp.bfloat16)
    for tick_index in range(ticks):
        own_index = min(tick_index, MICRO - 1)
        mb_slot = tick_index - section_index
        is_valid = (mb_slot >= 0) & (mb_slot < MICRO)
        mb_slot = jnp.clip(mb_slot, 0, MICRO - 1)
        fresh = lax.slice_in_dim(inputs, own_index * rows_mb, (own_index + 1) * rows_mb, axis=1)
        layer_input_rows = jnp.where(is_first, fresh, arriving)
        segment_row_span = lax.dynamic_slice_in_dim(segments, mb_slot * rows_mb, rows_mb, 0)
        layer_output_rows = forward_layer_step(
            layer_input_rows.astype(jnp.float32), segment_row_span, fixed_weights, adapter_pair
        ).astype(jnp.bfloat16)
        activations = jnp.where(
            is_valid,
            lax.dynamic_update_slice_in_dim(activations, layer_output_rows, mb_slot * rows_mb, 1),
            activations,
        )
        kept_inputs = jnp.where(
            is_valid, kept_inputs.at[mb_slot].set(layer_input_rows), kept_inputs
        )
        if tick_index < ticks - 1:
            arriving = passed_along(layer_output_rows, "section", 1)
    input_grads = jnp.zeros_like(inputs)
    gradient_totals = tuple(
        (jnp.zeros(factor_tensor.shape, jnp.float32) for factor_tensor in adapter_pair)
    )
    arriving = jnp.zeros(block_shape, jnp.bfloat16)
    for tick_index in range(ticks):
        own_index = min(tick_index, MICRO - 1)
        mb_slot = tick_index - (sections - 1 - section_index)
        is_valid = (mb_slot >= 0) & (mb_slot < MICRO)
        mb_slot = jnp.clip(mb_slot, 0, MICRO - 1)
        given = lax.slice_in_dim(cotangent, own_index * rows_mb, (own_index + 1) * rows_mb, axis=1)
        upstream_gradient = jnp.where(is_last, given, arriving).astype(jnp.float32)
        layer_input_rows = kept_inputs[mb_slot].astype(jnp.float32)
        segment_row_span = lax.dynamic_slice_in_dim(segments, mb_slot * rows_mb, rows_mb, 0)
        layer_output_rows, row_pieces = backward_layer_step(
            layer_input_rows, segment_row_span, upstream_gradient, fixed_weights, adapter_pair
        )
        leaving_b = layer_output_rows.astype(jnp.bfloat16)
        input_grads = jnp.where(
            is_valid,
            lax.dynamic_update_slice_in_dim(input_grads, leaving_b, mb_slot * rows_mb, 1),
            input_grads,
        )
        gradient_totals = tuple(
            (
                running + jnp.where(is_valid, piece_grad, 0.0)
                for running, piece_grad in zip(gradient_totals, row_pieces)
            )
        )
        if tick_index < ticks - 1:
            arriving = passed_along(leaving_b, "section", -1)
    adapter_rank = adapter_pair[1].shape[0]
    model_width = inputs.shape[2]
    column_total = adapter_pair[1].shape[1]
    offset = lax.axis_index("tensor") * column_total
    full_query = lax.dynamic_update_slice_in_dim(
        jnp.zeros((adapter_rank, model_width), jnp.float32), gradient_totals[1], offset, 1
    )
    full_value = lax.dynamic_update_slice_in_dim(
        jnp.zeros((adapter_rank, model_width), jnp.float32), gradient_totals[3], offset, 1
    )
    summed = lax.psum(
        (gradient_totals[0], full_query, gradient_totals[2], full_value), ("dp", "tensor")
    )
    return (
        activations[None],
        input_grads[None],
        summed[0][None],
        summed[1][None],
        summed[2][None],
        summed[3][None],
    )


REACH = 512
BF16 = jnp.bfloat16
F32 = jnp.float32
MESH = pl.DeviceIdType.MESH


def dot_nn(a, b):
    return lax.dot_general(a, b, (((1,), (0,)), ((), ())), preferred_element_type=F32)


def dot_nt(a, b):
    return lax.dot_general(a, b, (((1,), (1,)), ((), ())), preferred_element_type=F32)


def dot_tn(a, b):
    return lax.dot_general(a, b, (((0,), (0,)), ((), ())), preferred_element_type=F32)


def norm_stats(rows):
    middle = jnp.mean(rows, axis=-1, keepdims=True)
    centred = rows - middle
    inverse = lax.rsqrt(jnp.mean(centred * centred, axis=-1, keepdims=True) + EPSILON)
    return centred * inverse, inverse


def gelu_slope(pre):
    square = pre * pre
    bent = jnp.tanh(TANH_SCALE * (pre + CUBIC_TERM * square * pre))
    return 0.5 * (1.0 + bent) + (0.5 * TANH_SCALE) * pre * (1.0 - bent * bent) * (
        1.0 + (3.0 * CUBIC_TERM) * square
    )


def key_span(i, block):
    return max(0, i - REACH // block) * block, (i + 1) * block


def allowed_keys(i, block, seg_col_ref, seg_row_ref):
    low, high = key_span(i, block)
    seg_q = seg_col_ref[i * block : (i + 1) * block, :]
    seg_k = seg_row_ref[:, low:high]
    places_q = i * block + lax.broadcasted_iota(jnp.int32, (block, high - low), 0)
    places_k = low + lax.broadcasted_iota(jnp.int32, (block, high - low), 1)
    return (seg_q == seg_k) & (places_k <= places_q)


def head_lanes(rows, h):
    lane = lax.broadcasted_iota(jnp.int32, (rows, 128), 1)
    return (lane < HEAD_DIM) if h == 0 else (lane >= HEAD_DIM)


def both_halves(ref, *index):
    return jnp.concatenate([ref[(*index, 0)], ref[(*index, 1)]], axis=1)


class Wires:
    def __init__(self, send, recv):
        self.send, self.recv, self.count, self.sent = send, recv, 0, []

    def copy(self, source, target, where):
        k = self.count
        self.count += 1
        made = pltpu.make_async_remote_copy(
            src_ref=source,
            dst_ref=target,
            send_sem=self.send.at[k],
            recv_sem=self.recv.at[k],
            device_id=where,
            device_id_type=MESH,
        )
        self.sent.append(made)
        return made

    def forget(self, copy):
        self.sent = [one for one in self.sent if one is not copy]


WIRES = 40


def step_kernel(
    block,
    model,
    x_mine,
    x_other,
    cot_mine,
    cot_other,
    seg_col,
    seg_row,
    small,
    wq,
    up,
    wo,
    fc,
    proj,
    act,
    grad,
    down_sums,
    up_sums,
    xb,
    cb,
    sm,
    wq_all,
    up_all,
    wo_all,
    ff,
    rows,
    thin,
    qkv,
    o_out,
    o_in,
    middle,
    norm2,
    pre,
    part_out,
    part_in,
    own_sum,
    far_up,
    grad_mid,
    do_in,
    dqkv,
    dk_acc,
    dv_acc,
    c_out,
    c_in,
    y_out,
    y_in,
    wire_send,
    wire_recv,
    row_send,
    row_recv,
    wq_send,
    wq_recv,
    local_sem,
    o_send,
    o_recv,
):
    c = lax.axis_index("section")
    t = lax.axis_index("tensor")
    y, x = lax.div(t, 2), lax.rem(t, 2)
    over_x, over_y = 2 * y + (1 - x), 2 * (1 - y) + x
    mine, twin = 2 * y + c, 2 * y + (1 - c)
    far, far_twin = 2 * (1 - y) + c, 2 * (1 - y) + (1 - c)
    to_c, to_x, to_y = {"section": 1 - c}, {"tensor": over_x}, {"tensor": over_y}
    to_xc = {"section": 1 - c, "tensor": over_x}
    to_yc = {"section": 1 - c, "tensor": over_y}
    here = c == x
    wires = Wires(wire_send, wire_recv)
    width = wq.shape[2]
    factor = 8.0

    barrier = pltpu.get_barrier_semaphore()
    for peer in (to_c, to_x, to_y, to_xc, to_yc):
        pl.semaphore_signal(barrier, inc=1, device_id=peer, device_id_type=MESH)
    pl.semaphore_wait(barrier, 5)

    def row_copy(source, target, k):
        return pltpu.make_async_remote_copy(
            src_ref=source,
            dst_ref=target,
            send_sem=row_send.at[k],
            recv_sem=row_recv.at[k],
            device_id=to_x,
            device_id_type=MESH,
        )

    sm[c] = small[...]
    small_copy = wires.copy(small, sm.at[c], to_c)
    small_copy.start()
    x_copy = row_copy(x_other, xb, 0)

    @pl.when(here)
    def _():
        x_copy.start()
        xb[...] = x_mine[...]

    def wq_pair(k, where):
        return [
            pltpu.make_async_remote_copy(
                src_ref=source,
                dst_ref=target.at[c],
                send_sem=wq_send.at[k, j],
                recv_sem=wq_recv.at[c, j],
                device_id=where,
                device_id_type=MESH,
            )
            for j, (source, target) in enumerate(((wq, wq_all), (up, up_all)))
        ]

    def wq_local(layer):
        return [
            pltpu.make_async_copy(source, target.at[layer], wq_recv.at[layer, j])
            for j, (source, target) in enumerate(((wq, wq_all), (up, up_all)))
        ]

    def send_wq():
        for copy in wq_pair(1, {"section": x, "tensor": over_x}):
            copy.start()

        @pl.when(here)
        def _():
            for copy in wq_local(c):
                copy.start()

        @pl.when(jnp.logical_not(here))
        def _():
            for copy in wq_pair(0, to_c):
                copy.start()

    def sent_wq():
        for copy in wq_pair(1, to_x):
            copy.wait_send()

        @pl.when(jnp.logical_not(here))
        def _():
            for copy in wq_pair(0, to_c):
                copy.wait_send()

    pl.when(c == 0)(send_wq)

    locals_ = [
        pltpu.make_async_copy(source, target, local_sem.at[k])
        for k, (source, target) in enumerate(
            ((fc, ff.at[c, 0, 0]), (proj, ff.at[c, 1, 0]), (wo, wo_all.at[c, t]))
        )
    ]
    for copy in locals_:
        copy.start()
    ff_twin = [wires.copy(one, ff.at[c, k, 0], to_c) for k, one in enumerate((fc, proj))]
    ff_y = [wires.copy(one, ff.at[c, k, 1], to_y) for k, one in enumerate((fc, proj))]
    ff_y_twin = [wires.copy(ff.at[c, k, 1], ff.at[c, k, 1], to_c) for k in range(2)]
    wo_twin = wires.copy(wo, wo_all.at[c, t], to_c)
    wo_x = wires.copy(wo, wo_all.at[c, t], to_x)
    wo_y = wires.copy(wo, wo_all.at[c, t], to_y)
    half = width // 2
    wo_dy = wires.copy(
        wo_all.at[c, over_x, pl.ds(0, half)], wo_all.at[c, over_x, pl.ds(0, half)], to_y
    )
    wo_dx = wires.copy(
        wo_all.at[c, over_y, pl.ds(half, half)], wo_all.at[c, over_y, pl.ds(half, half)], to_x
    )
    corner = 2 * (1 - y) + (1 - x)
    wo_twins = [
        wires.copy(wo_all.at[c, q], wo_all.at[c, q], to_c) for q in (over_x, over_y, corner)
    ]

    def start_ff(layer):
        @pl.when(c == layer)
        def _():
            for copy in ff_y:
                copy.start()

    def pass_ff(layer):
        @pl.when(c == layer)
        def _():
            for copy, onward in zip(ff_y, ff_y_twin):
                copy.wait_recv()
                onward.start()

        @pl.when(c != layer)
        def _():
            for onward in ff_y_twin:
                onward.wait_recv()

    start_ff(0)
    for copy in ff_twin + [wo_twin]:
        copy.start()

    def arrived_wq(layer):
        for copy in wq_local(layer):
            copy.wait()

    def qkv_block(layer, b):
        normed = rows[layer, b]
        down = sm[layer, 16:32, :].astype(BF16)
        low = dot_nt(normed, down)
        low_b = low.astype(BF16)
        thin[layer, b] = low_b
        at = pl.ds(pl.multiple_of(b * block, block), block)
        for k in range(3):
            made = dot_nn(normed, wq_all[layer, k])
            if k == 0:
                made = made + factor * dot_nn(low_b, up_all[layer, 0])
            if k == 2:
                made = made + factor * dot_nn(low_b, up_all[layer, 1])
            made = made.astype(BF16)
            qkv[layer, k, 0, at, :] = made[:, :128]
            qkv[layer, k, 1, at, :] = made[:, 128:]

    def attend(layer, i):
        low, high = key_span(i, block)
        at = slice(i * block, (i + 1) * block)
        allowed = allowed_keys(i, block, seg_col, seg_row)

        def one_pair(pair, carry):
            queries = qkv[layer, 0, pair, at, :] * BF16(HEAD_DIM**-0.5)
            keys = qkv[layer, 1, pair, low:high, :]
            values = qkv[layer, 2, pair, low:high, :]
            parts = []
            for h in range(2):
                picked = jnp.where(head_lanes(block, h), queries, BF16(0))
                scores = jnp.where(allowed, dot_nt(picked, keys), MASKED)
                exponent = jnp.exp(scores - jnp.max(scores, axis=-1, keepdims=True))
                total = jnp.sum(exponent, axis=-1, keepdims=True)
                parts.append(dot_nn(exponent.astype(BF16), values) / total)
            o_out[i, pair] = jnp.where(head_lanes(block, 0), parts[0], parts[1]).astype(BF16)
            return carry

        lax.fori_loop(0, 2, one_pair, 0)

    def exchange_piece(i, target, phase):
        return pltpu.make_async_remote_copy(
            src_ref=o_out.at[i],
            dst_ref=target.at[mine],
            send_sem=o_send.at[i],
            recv_sem=o_recv.at[phase, mine],
            device_id={"section": i % 2, "tensor": 2 * (i // 2) + x},
            device_id_type=MESH,
        )

    def send_piece(i, target, phase):
        @pl.when(mine == i)
        def _():
            target[mine] = o_out[i]

        @pl.when(mine != i)
        def _():
            exchange_piece(i, target, phase).start()

    def wait_pieces(target, phase):
        for i in range(4):

            @pl.when(mine != i)
            def _():
                exchange_piece(i, target, phase).wait_send()
                pltpu.make_async_copy(o_out.at[i], target.at[i], o_recv.at[phase, i]).wait()

    def hidden_half(layer, who, source, q):
        total = None
        for cut in range(2):
            lanes = slice(cut * model // 2, (cut + 1) * model // 2)
            made = dot_nn(source, ff[layer, 0, q, :, lanes])
            pre[layer, who, q, :, lanes] = made.astype(BF16)
            term = dot_nn(gelu_tanh(made).astype(BF16), ff[layer, 1, q, lanes, :])
            total = term if total is None else total + term
        return total

    def hidden_back(layer, who, upstream, q):
        total = None
        for cut in range(2):
            lanes = slice(cut * model // 2, (cut + 1) * model // 2)
            grad_hidden = dot_nt(upstream, ff[layer, 1, q, lanes, :])
            slope = gelu_slope(pre[layer, who, q, :, lanes].astype(F32))
            term = dot_nt((grad_hidden * slope).astype(BF16), ff[layer, 0, q, :, lanes])
            total = term if total is None else total + term
        return total

    @pl.when(jnp.logical_not(here))
    def _():
        x_copy.wait_recv()

    small_copy.wait_recv()

    for layer in range(2):
        source = xb if layer == 0 else act.at[0]
        unit, _ = norm_stats(source[...].astype(F32))
        rows[layer, mine] = (unit * sm[layer, 0:1, :]).astype(BF16)
        row_y = wires.copy(rows.at[layer, mine], rows.at[layer, mine], to_y)
        row_c = wires.copy(rows.at[layer, mine], rows.at[layer, mine], to_c)
        row_yc = wires.copy(rows.at[layer, far], rows.at[layer, far], to_c)
        row_y.start()
        row_c.start()
        arrived_wq(layer)
        if layer == 0:
            for copy in (wo_x, wo_y):
                copy.start()
        qkv_block(layer, mine)
        row_c.wait_recv()
        qkv_block(layer, twin)
        row_y.wait_recv()
        row_yc.start()
        qkv_block(layer, far)
        row_yc.wait_recv()
        qkv_block(layer, far_twin)
        for i in range(4):
            attend(layer, i)
            send_piece(i, o_in, layer)
        if layer == 0:
            locals_[2].wait()
            wo_x.wait_recv()
            wo_dy.start()
            wo_twins[0].start()
            wo_y.wait_recv()
            wo_dx.start()
            wo_twins[1].start()
            wo_dy.wait_recv()
            wo_dx.wait_recv()
            wo_twins[2].start()
            wo_twin.wait_recv()
            for copy in wo_twins:
                copy.wait_recv()
        wait_pieces(o_in, layer)
        stream = source[...].astype(F32)
        for q in range(4):
            stream = stream + dot_nn(both_halves(o_in, q), wo_all[layer, q])
        middle[layer] = stream
        unit, _ = norm_stats(stream)
        norm2[0] = (unit * sm[layer, 8:9, :]).astype(BF16)
        norm_x = wires.copy(norm2.at[0], norm2.at[1], to_x)
        norm_x.start()
        if layer == 0:
            for copy in locals_[:2]:
                copy.wait()
            for copy in ff_twin:
                copy.wait_recv()
        own_sum[...] = hidden_half(layer, 0, norm2[0], 0)
        norm_x.wait_recv()
        away = hidden_half(layer, 1, norm2[1], 0)
        pass_ff(layer)
        away = away + hidden_half(layer, 1, norm2[1], 1)
        part_out[...] = away.astype(BF16)
        part_x = wires.copy(part_out, part_in.at[0], to_x)
        part_x.start()
        if layer == 0:
            start_ff(1)
            pl.when(c == 1)(send_wq)
        stream = middle[layer] + own_sum[...] + hidden_half(layer, 0, norm2[0], 1)
        part_x.wait()
        wires.forget(part_x)
        norm_x.wait_send()
        wires.forget(norm_x)
        act[layer] = (stream + part_in[0].astype(F32)).astype(BF16)
        if layer == 0:
            cot_copies = [row_copy(cot_other, cb.at[0], 1), row_copy(cot_mine, cb.at[1], 2)]

            @pl.when(here)
            def _():
                for copy in cot_copies:
                    copy.start()
                cb[0] = cot_mine[...]
                cb[1] = cot_other[...]

    @pl.when(jnp.logical_not(here))
    def _():
        for copy in cot_copies:
            copy.wait_recv()

    for layer in (1, 0):
        upstream = cb[0] if layer == 1 else grad[1]
        if layer == 1:
            away = hidden_back(layer, 1, cb[1], 0) + hidden_back(layer, 1, cb[1], 1)
        else:
            up_x = wires.copy(grad.at[1], far_up, to_x)
            up_x.start()
            own_sum[...] = hidden_back(layer, 0, upstream, 0) + hidden_back(layer, 0, upstream, 1)
            up_x.wait_recv()
            away = hidden_back(layer, 1, far_up[...], 0) + hidden_back(layer, 1, far_up[...], 1)
        part_out[...] = away.astype(BF16)
        part_x = wires.copy(part_out, part_in.at[1], to_x)
        part_x.start()
        if layer == 1:
            own_sum[...] = hidden_back(layer, 0, upstream, 0) + hidden_back(layer, 0, upstream, 1)
        unit, inverse = norm_stats(middle[layer])
        part_x.wait()
        wires.forget(part_x)
        grad_norm = own_sum[...] + part_in[1].astype(F32)
        grad_middle = upstream.astype(F32) + normalize_back(
            grad_norm, unit, inverse, sm[layer, 8:9, :]
        )
        grad_mid[...] = grad_middle
        grad_b = grad_middle.astype(BF16)
        for q in range(4):
            made = dot_nt(grad_b, wo_all[layer, q]).astype(BF16)
            o_out[q, 0] = made[:, :128]
            o_out[q, 1] = made[:, 128:]
            send_piece(q, do_in, 2 + layer)
        wait_pieces(do_in, 2 + layer)

        def back_pair(pair, carry):
            dk_acc[...] = jnp.zeros_like(dk_acc)
            dv_acc[...] = jnp.zeros_like(dv_acc)
            for i in range(4):
                low, high = key_span(i, block)
                at = slice(i * block, (i + 1) * block)
                allowed = allowed_keys(i, block, seg_col, seg_row)
                queries = qkv[layer, 0, pair, at, :] * BF16(HEAD_DIM**-0.5)
                keys = qkv[layer, 1, pair, low:high, :]
                values = qkv[layer, 2, pair, low:high, :]
                grads = do_in[i, pair]
                parts = []
                for h in range(2):
                    lanes = head_lanes(block, h)
                    picked = jnp.where(lanes, queries, BF16(0))
                    given = jnp.where(lanes, grads, BF16(0))
                    scores = jnp.where(allowed, dot_nt(picked, keys), MASKED)
                    exponent = jnp.exp(scores - jnp.max(scores, axis=-1, keepdims=True))
                    soft = exponent * (1.0 / jnp.sum(exponent, axis=-1, keepdims=True))
                    weighted = soft * dot_nt(given, values)
                    grad_scores = (
                        weighted - soft * jnp.sum(weighted, axis=-1, keepdims=True)
                    ).astype(BF16)
                    parts.append(dot_nn(grad_scores, keys))
                    dk_acc[low:high, :] += dot_tn(grad_scores, picked)
                    dv_acc[low:high, :] += dot_tn(soft.astype(BF16), given)
                dqkv[0, pair, at, :] = (
                    jnp.where(head_lanes(block, 0), parts[0], parts[1]) * HEAD_DIM**-0.5
                ).astype(BF16)
            dqkv[1, pair] = dk_acc[...].astype(BF16)
            dqkv[2, pair] = dv_acc[...].astype(BF16)
            return carry

        lax.fori_loop(0, 2, back_pair, 0)
        down = sm[layer, 16:32, :].astype(BF16)

        def block_grad(b, first):
            at = pl.ds(pl.multiple_of(b * block, block), block)
            parts = [
                jnp.concatenate([dqkv[k, 0, at, :], dqkv[k, 1, at, :]], axis=1) for k in range(3)
            ]
            low = factor * (
                dot_nt(parts[0], up_all[layer, 0]) + dot_nt(parts[2], up_all[layer, 1])
            )
            low_b = low.astype(BF16)
            term = dot_nn(low_b, down)
            for k in range(3):
                term = term + dot_nt(parts[k], wq_all[layer, k])
            kept = thin[layer, b]
            to_down = dot_tn(low_b, rows[layer, b])
            to_up = [factor * dot_tn(kept, parts[0]), factor * dot_tn(kept, parts[2])]
            if first:
                down_sums[layer] = to_down
                up_sums[layer, 0], up_sums[layer, 1] = to_up
            else:
                down_sums[layer] += to_down
                up_sums[layer, 0] += to_up[0]
                up_sums[layer, 1] += to_up[1]
            return term

        c_far = wires.copy(c_out.at[0], c_in.at[0], to_c)
        c_near = wires.copy(c_out.at[1], c_in.at[1], to_c)
        y_far = wires.copy(y_out, y_in, to_y)
        c_out[0] = block_grad(far_twin, True).astype(BF16)
        c_far.start()
        term = block_grad(far, False)
        c_far.wait_recv()
        y_out[...] = (term + c_in[0].astype(F32)).astype(BF16)
        y_far.start()
        c_out[1] = block_grad(twin, False).astype(BF16)
        c_near.start()
        term = block_grad(mine, False)
        c_near.wait_recv()
        term = term + c_in[1].astype(F32)
        source = xb if layer == 0 else act.at[0]
        unit, inverse = norm_stats(source[...].astype(F32))
        y_far.wait_recv()
        grad_norm = term + y_in[...].astype(F32)
        grad[layer] = (
            grad_mid[...] + normalize_back(grad_norm, unit, inverse, sm[layer, 0:1, :])
        ).astype(BF16)
        for copy in (c_far, c_near, y_far):
            copy.wait_send()
            wires.forget(copy)

    @pl.when(here)
    def _():
        x_copy.wait_send()
        for copy in cot_copies:
            copy.wait_send()

    sent_wq()
    for copy in wires.sent:
        copy.wait_send()


def step_call(block, model, width, rank, operands):
    slots = 4 * block
    in_vmem = pl.BlockSpec(memory_space=pltpu.VMEM)
    in_hbm = pl.BlockSpec(memory_space=pl.ANY)
    return pl.pallas_call(
        functools.partial(step_kernel, block, model),
        out_shape=(
            jax.ShapeDtypeStruct((2, block, model), BF16),
            jax.ShapeDtypeStruct((2, block, model), BF16),
            jax.ShapeDtypeStruct((2, 16, model), F32),
            jax.ShapeDtypeStruct((2, 2, 16, width), F32),
        ),
        in_specs=[in_vmem] * 7 + [in_hbm] * 5,
        out_specs=[in_vmem] * 4,
        scratch_shapes=[
            pltpu.VMEM((block, model), BF16),
            pltpu.VMEM((2, block, model), BF16),
            pltpu.VMEM((2, 32, model), F32),
            pltpu.VMEM((2, 3, model, width), BF16),
            pltpu.VMEM((2, 2, 16, width), BF16),
            pltpu.VMEM((2, 4, width, model), BF16),
            pltpu.VMEM((2, 2, 2, model, model), BF16),
            pltpu.VMEM((2, 4, block, model), BF16),
            pltpu.VMEM((2, 4, block, 16), BF16),
            pltpu.VMEM((2, 3, 2, slots, 128), BF16),
            pltpu.VMEM((4, 2, block, 128), BF16),
            pltpu.VMEM((4, 2, block, 128), BF16),
            pltpu.VMEM((2, block, model), F32),
            pltpu.VMEM((2, block, model), BF16),
            pltpu.VMEM((2, 2, 2, block, model), BF16),
            pltpu.VMEM((block, model), BF16),
            pltpu.VMEM((2, block, model), BF16),
            pltpu.VMEM((block, model), F32),
            pltpu.VMEM((block, model), BF16),
            pltpu.VMEM((block, model), F32),
            pltpu.VMEM((4, 2, block, 128), BF16),
            pltpu.VMEM((3, 2, slots, 128), BF16),
            pltpu.VMEM((slots, 128), F32),
            pltpu.VMEM((slots, 128), F32),
            pltpu.VMEM((2, block, model), BF16),
            pltpu.VMEM((2, block, model), BF16),
            pltpu.VMEM((block, model), BF16),
            pltpu.VMEM((block, model), BF16),
            pltpu.SemaphoreType.DMA((WIRES,)),
            pltpu.SemaphoreType.DMA((WIRES,)),
            pltpu.SemaphoreType.DMA((3,)),
            pltpu.SemaphoreType.DMA((3,)),
            pltpu.SemaphoreType.DMA((2, 2)),
            pltpu.SemaphoreType.DMA((2, 2)),
            pltpu.SemaphoreType.DMA((3,)),
            pltpu.SemaphoreType.DMA((4,)),
            pltpu.SemaphoreType.DMA((4, 4)),
        ],
        compiler_params=pltpu.CompilerParams(
            collective_id=0, has_side_effects=True, vmem_limit_bytes=61 * 1024 * 1024
        ),
    )(*operands)


ROUTE_AXES = ("section", "dp", "tensor")


def route(planes, rule):
    pairs = []
    for c in range(2):
        for z in range(planes):
            for y in range(2):
                for x in range(2):
                    target = rule(c, z, y, x)
                    if target is not None:
                        tc, tz, ty, tx = target
                        pairs.append(
                            ((c * planes + z) * 4 + 2 * y + x, (tc * planes + tz) * 4 + 2 * ty + tx)
                        )
    return pairs


def fast_body(
    planes,
    inputs,
    segments,
    cotangent,
    gain_attn,
    joint_projection_weight,
    query_down_factor,
    query_up_factor,
    value_down_factor,
    value_up_factor,
    w_out,
    gain_mlp,
    w_fc,
    w_proj,
):
    core = lax.axis_index("section")
    place = lax.axis_index("tensor")
    y, x = place // 2, place % 2
    block, _, model = inputs.shape
    width = joint_projection_weight.shape[3]
    rank = query_down_factor.shape[2]
    core_0, x_0 = core == 0, x == 0

    def sent(value, rule):
        return lax.ppermute(value, ROUTE_AXES, route(planes, rule))

    def both_rows(array):
        return (
            jnp.where(x_0, array[:, 0], array[:, 1]),
            jnp.where(x_0, array[:, 1], array[:, 0]),
        )

    segment_row = jnp.where(x_0, segments[0], segments[1])
    blank = jnp.zeros((7, model), F32)
    small = jnp.concatenate(
        [
            gain_attn,
            blank,
            gain_mlp,
            blank,
            query_down_factor[0].T.astype(F32),
            value_down_factor[0].T.astype(F32),
            jnp.zeros((16 - 2 * rank, model), F32),
        ],
        axis=0,
    )
    ups = jnp.stack(
        [
            jnp.pad(query_up_factor[0], ((0, 16 - rank), (0, 0))),
            jnp.pad(value_up_factor[0], ((rank, 16 - 2 * rank), (0, 0))),
        ]
    )
    acts, grads, down_sums, up_sums = step_call(
        block,
        model,
        width,
        rank,
        (
            *both_rows(inputs),
            *both_rows(cotangent),
            segment_row[:, None],
            segment_row[None, :],
            small,
            jnp.swapaxes(joint_projection_weight[0], 0, 1),
            ups,
            w_out[0],
            w_fc[0],
            w_proj[0],
        ),
    )
    totals = []
    for layer in (1, 0):
        placed_up = [
            lax.dynamic_update_slice_in_dim(
                jnp.zeros((rank, model), F32),
                up_sums[layer, k, k * rank : (k + 1) * rank],
                (2 * y + core) * width,
                1,
            )
            for k in range(2)
        ]
        total = jnp.concatenate([down_sums[layer, : 2 * rank], *placed_up], axis=0)
        total = total + sent(total, lambda c, z, y, x: (1 - c, z, y, x))
        total = total + sent(total, lambda c, z, y, x: (c, z, y, 1 - x))
        total = total + sent(total, lambda c, z, y, x: (c, z, 1 - y, x))
        bit = 1
        while bit < planes:
            total = total + sent(total, lambda c, z, y, x: (c, z ^ bit, y, x))
            bit *= 2
        totals.append(total)

    def placed(pair):
        same, other = [], []
        for layer in range(2):
            same.append(
                sent(pair[layer], lambda c, z, y, x: (layer, z, y, x) if c == x else None)
            )
            other.append(
                sent(pair[layer], lambda c, z, y, x: (layer, z, y, 1 - x) if c != x else None)
            )
        same = jnp.where(core_0, same[0], same[1])
        other = jnp.where(core_0, other[0], other[1])
        return jnp.stack([jnp.where(x_0, same, other), jnp.where(x_0, other, same)], axis=1)[None]

    total = jnp.where(core_0, totals[1], totals[0])
    return (
        placed(acts),
        placed(grads),
        total[:rank].T[None],
        total[2 * rank : 3 * rank][None],
        total[rank : 2 * rank].T[None],
        total[3 * rank :][None],
    )


def fits_fast(mesh, shapes):
    planes = mesh.shape["dp"]
    slots, rows_all, model = shapes[0]
    return (
        mesh.shape["section"] == 2
        and mesh.shape["tensor"] == 4
        and planes & (planes - 1) == 0
        and rows_all == 2 * planes
        and slots == 1024
        and model == 1024
        and shapes[4][3] == 1024
        and shapes[5][2] == 4
        and shapes[11][2] == 4096
    )


def solution(mesh):
    placed = (
        P("tensor", "dp", None),
        P("dp", None),
        P("tensor", "dp", None),
        P("section", None),
        P("section", None, None, "tensor"),
        P("section", None, None),
        P("section", None, "tensor"),
        P("section", None, None),
        P("section", None, "tensor"),
        P("section", "tensor", None),
        P("section", None),
        P("section", None, "tensor"),
        P("section", "tensor", None),
    )

    def mapped(picked):
        return jax.shard_map(
            picked,
            mesh=mesh,
            in_specs=placed,
            out_specs=(
                P("section", "tensor", "dp", None),
                P("section", "tensor", "dp", None),
                P("section", None, None),
                P("section", None, None),
                P("section", None, None),
                P("section", None, None),
            ),
            check_vma=False,
        )

    def choose(*args):
        if fits_fast(mesh, [a.shape for a in args]):
            return mapped(functools.partial(fast_body, mesh.shape["dp"]))(*args)
        return mapped(body)(*args)

    return choose
```

```python
import functools

import jax
import jax.numpy as jnp
from jax import lax
from jax.experimental import pallas as pl
from jax.experimental.pallas import tpu as pltpu
from jax.sharding import PartitionSpec as P

HEAD_DIM = 64
MICRO = 2


EPSILON = 1e-05
PRECISE = lax.Precision.HIGHEST
MASKED = -1000000000.0
CUBIC_TERM = 0.044715
TANH_SCALE = 0.7978845608028654


def passed_along(block, axis, distance):
    devices = range(lax.axis_size(axis))
    route = [(i - distance, i) for i in devices if i - distance in devices]
    return lax.ppermute(block, axis, route)


def gelu_tanh(value):
    return 0.5 * value * (1.0 + jnp.tanh(TANH_SCALE * (value + CUBIC_TERM * value * value * value)))


def normalize(residual_stream, gain):
    middle = jnp.mean(residual_stream, axis=-1, keepdims=True)
    centred = residual_stream - middle
    inverse = lax.rsqrt(jnp.mean(centred * centred, axis=-1, keepdims=True) + EPSILON)
    unit_rows = centred * inverse
    return (unit_rows * gain, unit_rows, inverse)


def normalize_back(grad_norm, unit_rows, inverse, gain):
    scaled = grad_norm * gain
    return inverse * (
        scaled
        - jnp.mean(scaled, axis=-1, keepdims=True)
        - unit_rows * jnp.mean(scaled * unit_rows, axis=-1, keepdims=True)
    )


def block_mask(segment_row_span, first_row, block):
    length = segment_row_span.shape[1]
    segment_part = lax.dynamic_slice_in_dim(segment_row_span, first_row, block, 1)
    query_places = first_row + jnp.arange(block)
    key_places = jnp.arange(length)
    same_doc = segment_part[:, :, None] == segment_row_span[:, None, :]
    return same_doc & (key_places[None, None, :] <= query_places[None, :, None])


def projected_rows(row_portion, joint_projection_weight, adapter_pair):
    query_down_factor, query_up_factor, value_down_factor, value_up_factor = adapter_pair
    factor = 32.0 / query_down_factor.shape[-1]
    joined = jnp.einsum(
        "srd,dcf->srcf", row_portion, joint_projection_weight, preferred_element_type=jnp.float32
    )
    narrow_query_rows = jnp.einsum(
        "srd,dk->srk", row_portion, query_down_factor, preferred_element_type=jnp.float32
    )
    narrow_value_rows = jnp.einsum(
        "srd,dk->srk", row_portion, value_down_factor, preferred_element_type=jnp.float32
    )
    queries = joined[:, :, 0] + factor * jnp.einsum(
        "srk,kf->srf", narrow_query_rows, query_up_factor.astype(jnp.float32), precision=PRECISE
    )
    values_all = joined[:, :, 2] + factor * jnp.einsum(
        "srk,kf->srf", narrow_value_rows, value_up_factor.astype(jnp.float32), precision=PRECISE
    )
    stacked_weights = jnp.stack([queries, joined[:, :, 1], values_all], axis=2).astype(jnp.bfloat16)
    return (stacked_weights, narrow_query_rows, narrow_value_rows)


def attention_forward(queries, keys_all, values_all, segment_row_span):
    length, row_count, head_count, width = queries.shape
    block = min(512, length)
    factor = width ** (-0.5)

    def one_block(block_index):
        first_row = block_index * block
        query_part = lax.dynamic_slice_in_dim(queries, first_row, block, 0)
        scores = (
            jnp.einsum("qrhe,krhe->rhqk", query_part, keys_all, preferred_element_type=jnp.float32)
            * factor
        )
        allowed = block_mask(segment_row_span, first_row, block)
        scores = jnp.where(allowed[:, None], scores, MASKED)
        row_max = jnp.max(scores, axis=-1, keepdims=True)
        exponent = jnp.exp(scores - row_max)
        total = jnp.sum(exponent, axis=-1, keepdims=True)
        weights_soft = (exponent / total).astype(jnp.bfloat16)
        attended = jnp.einsum(
            "rhqk,krhe->qrhe", weights_soft, values_all, preferred_element_type=jnp.float32
        )
        return (attended, (row_max + jnp.log(total))[..., 0])

    attended, log_sums = lax.map(one_block, jnp.arange(length // block))
    attended = attended.reshape(length, row_count, head_count, width)
    log_sums = jnp.moveaxis(log_sums, 0, 2).reshape(row_count, head_count, length)
    return (attended, log_sums)


def attention_backward(queries, keys_all, values_all, segment_row_span, log_sums, grad_heads):
    length = queries.shape[0]
    block = min(512, length)
    factor = queries.shape[-1] ** (-0.5)

    def one_block(carry, block_index):
        grad_keys, grad_values = carry
        first_row = block_index * block
        query_part = lax.dynamic_slice_in_dim(queries, first_row, block, 0)
        grad_part = lax.dynamic_slice_in_dim(grad_heads, first_row, block, 0)
        sums_part = lax.dynamic_slice_in_dim(log_sums, first_row, block, 2)
        scores = (
            jnp.einsum("qrhe,krhe->rhqk", query_part, keys_all, preferred_element_type=jnp.float32)
            * factor
        )
        allowed = block_mask(segment_row_span, first_row, block)
        scores = jnp.where(allowed[:, None], scores, MASKED)
        weights_soft = jnp.exp(scores - sums_part[..., None])
        grad_soft = jnp.einsum(
            "qrhe,krhe->rhqk", grad_part, values_all, preferred_element_type=jnp.float32
        )
        grad_scores = weights_soft * (
            grad_soft - jnp.sum(weights_soft * grad_soft, axis=-1, keepdims=True)
        )
        grad_scores = grad_scores.astype(jnp.bfloat16)
        grad_query = (
            jnp.einsum("rhqk,krhe->qrhe", grad_scores, keys_all, preferred_element_type=jnp.float32)
            * factor
        )
        grad_keys = (
            grad_keys
            + jnp.einsum(
                "rhqk,qrhe->krhe", grad_scores, query_part, preferred_element_type=jnp.float32
            )
            * factor
        )
        grad_values = grad_values + jnp.einsum(
            "rhqk,qrhe->krhe",
            weights_soft.astype(jnp.bfloat16),
            grad_part,
            preferred_element_type=jnp.float32,
        )
        return ((grad_keys, grad_values), grad_query)

    start_state = (jnp.zeros(keys_all.shape, jnp.float32), jnp.zeros(values_all.shape, jnp.float32))
    (grad_keys, grad_values), grad_blocks = lax.scan(
        one_block, start_state, jnp.arange(length // block)
    )
    return (grad_blocks.reshape(queries.shape), grad_keys, grad_values)


def attend_all(stacked_weights, segment_row_span):
    length, row_count = (stacked_weights.shape[0], stacked_weights.shape[1])
    head_view = stacked_weights.reshape(length, row_count, 3, -1, HEAD_DIM)
    queries, keys_all, values_all = (head_view[:, :, 0], head_view[:, :, 1], head_view[:, :, 2])
    attended, log_sums = attention_forward(queries, keys_all, values_all, segment_row_span)
    return (
        attended.reshape(length, row_count, -1).astype(jnp.bfloat16),
        log_sums,
        (queries, keys_all, values_all),
    )


def attention_project(attended_b, w_out):
    return lax.psum_scatter(
        jnp.einsum("srf,fd->srd", attended_b, w_out, preferred_element_type=jnp.float32).astype(
            jnp.bfloat16
        ),
        "tensor",
        scatter_dimension=0,
        tiled=True,
    ).astype(jnp.float32)


def attention_grad_heads(grad_middle_b, w_out):
    grad_attended = jnp.einsum(
        "srd,fd->srf",
        lax.all_gather(grad_middle_b, "tensor", axis=0, tiled=True),
        w_out,
        preferred_element_type=jnp.float32,
    )
    return grad_attended.astype(jnp.bfloat16)


def mlp_pre(normed_b, w_fc):
    return jnp.einsum(
        "srd,df->srf",
        lax.all_gather(normed_b, "tensor", axis=0, tiled=True),
        w_fc,
        preferred_element_type=jnp.float32,
    )


def mlp_out(hidden_b, w_proj):
    return lax.psum_scatter(
        jnp.einsum("srf,fd->srd", hidden_b, w_proj, preferred_element_type=jnp.float32).astype(
            jnp.bfloat16
        ),
        "tensor",
        scatter_dimension=0,
        tiled=True,
    ).astype(jnp.float32)


def mlp_back(grad_mlp, pre_act, w_fc, w_proj):
    grad_hidden = jnp.einsum(
        "srd,fd->srf",
        lax.all_gather(grad_mlp, "tensor", axis=0, tiled=True),
        w_proj,
        preferred_element_type=jnp.float32,
    )
    activated, slope = jax.vjp(gelu_tanh, pre_act)
    grad_pre = slope(grad_hidden)[0].astype(jnp.bfloat16)
    return lax.psum_scatter(
        jnp.einsum("srf,df->srd", grad_pre, w_fc, preferred_element_type=jnp.float32).astype(
            jnp.bfloat16
        ),
        "tensor",
        scatter_dimension=0,
        tiled=True,
    ).astype(jnp.float32)


def forward_layer_step(layer_input_rows, segment_row_span, fixed_weights, adapter_pair):
    norm_rows = normalize(layer_input_rows, fixed_weights[0])[0].astype(jnp.bfloat16)
    stacked_weights = projected_rows(
        lax.all_gather(norm_rows, "tensor", axis=0, tiled=True), fixed_weights[1], adapter_pair
    )[0]
    attended_b = attend_all(stacked_weights, segment_row_span)[0]
    middle = layer_input_rows + attention_project(attended_b, fixed_weights[2])
    normed_mlp = normalize(middle, fixed_weights[3])[0].astype(jnp.bfloat16)
    pre_act = mlp_pre(normed_mlp, fixed_weights[4])
    hidden_b = gelu_tanh(pre_act).astype(jnp.bfloat16)
    return middle + mlp_out(hidden_b, fixed_weights[5])


def backward_layer_step(
    layer_input_rows, segment_row_span, upstream_gradient, fixed_weights, adapter_pair
):
    gain_a, joint_projection_weight, w_out, gain_m, w_fc, w_proj = fixed_weights
    query_down_factor, query_up_factor, value_down_factor, value_up_factor = adapter_pair
    factor = 32.0 / query_down_factor.shape[-1]
    norm_rows, unit_first, inverse_first = normalize(layer_input_rows, gain_a)
    collected_rows = lax.all_gather(norm_rows.astype(jnp.bfloat16), "tensor", axis=0, tiled=True)
    stacked_weights, narrow_query_rows, narrow_value_rows = projected_rows(
        collected_rows, joint_projection_weight, adapter_pair
    )
    length, row_count = (collected_rows.shape[0], collected_rows.shape[1])
    attended_b, log_sums, head_views = attend_all(stacked_weights, segment_row_span)
    queries, keys_all, values_all = head_views
    middle = layer_input_rows + attention_project(attended_b, w_out)
    normed_mlp, unit_second, inverse_second = normalize(middle, gain_m)
    pre_act = mlp_pre(normed_mlp.astype(jnp.bfloat16), w_fc)
    grad_norm_mlp = mlp_back(upstream_gradient.astype(jnp.bfloat16), pre_act, w_fc, w_proj)
    grad_middle = upstream_gradient + normalize_back(
        grad_norm_mlp, unit_second, inverse_second, gain_m
    )
    grad_attended = attention_grad_heads(grad_middle.astype(jnp.bfloat16), w_out)
    grad_heads = grad_attended.reshape(queries.shape)
    grad_queries, grad_keys, grad_values = attention_backward(
        queries, keys_all, values_all, segment_row_span, log_sums, grad_heads
    )
    grad_stack = (
        jnp.stack([grad_queries, grad_keys, grad_values], axis=2)
        .astype(jnp.bfloat16)
        .reshape(length, row_count, 3, -1)
    )
    grad_query_rows = grad_stack[:, :, 0]
    grad_value_rows = grad_stack[:, :, 2]
    thin_grad_query = factor * jnp.einsum(
        "srf,kf->srk", grad_query_rows, query_up_factor, preferred_element_type=jnp.float32
    )
    thin_grad_value = factor * jnp.einsum(
        "srf,kf->srk", grad_value_rows, value_up_factor, preferred_element_type=jnp.float32
    )
    grad_bq = factor * jnp.einsum(
        "srk,srf->kf", narrow_query_rows, grad_query_rows.astype(jnp.float32), precision=PRECISE
    )
    grad_bv = factor * jnp.einsum(
        "srk,srf->kf", narrow_value_rows, grad_value_rows.astype(jnp.float32), precision=PRECISE
    )
    gathered_wide = collected_rows.astype(jnp.float32)
    grad_aq = jnp.einsum("srd,srk->dk", gathered_wide, thin_grad_query, precision=PRECISE)
    grad_av = jnp.einsum("srd,srk->dk", gathered_wide, thin_grad_value, precision=PRECISE)
    a_query_wide = query_down_factor.astype(jnp.float32)
    a_value_wide = value_down_factor.astype(jnp.float32)
    term = jnp.einsum(
        "srcf,dcf->srd", grad_stack, joint_projection_weight, preferred_element_type=jnp.float32
    )
    term = term + jnp.einsum("srk,dk->srd", thin_grad_query, a_query_wide, precision=PRECISE)
    grad_norm_attn = lax.psum_scatter(
        (term + jnp.einsum("srk,dk->srd", thin_grad_value, a_value_wide, precision=PRECISE)).astype(
            jnp.bfloat16
        ),
        "tensor",
        scatter_dimension=0,
        tiled=True,
    ).astype(jnp.float32)
    layer_output_rows = grad_middle + normalize_back(
        grad_norm_attn, unit_first, inverse_first, gain_a
    )
    return (layer_output_rows, (grad_aq, grad_bq, grad_av, grad_bv))


def body(
    inputs,
    segments,
    cotangent,
    gain_attn,
    joint_projection_weight,
    query_down_factor,
    query_up_factor,
    value_down_factor,
    value_up_factor,
    w_out,
    gain_mlp,
    w_fc,
    w_proj,
):
    fixed_weights = (
        gain_attn[0],
        joint_projection_weight[0],
        w_out[0],
        gain_mlp[0],
        w_fc[0],
        w_proj[0],
    )
    adapter_pair = (
        query_down_factor[0],
        query_up_factor[0],
        value_down_factor[0],
        value_up_factor[0],
    )
    sections = lax.axis_size("section")
    section_index = lax.axis_index("section")
    is_first = section_index == 0
    is_last = section_index == sections - 1
    rows_mb = inputs.shape[1] // MICRO
    ticks = MICRO + sections - 1
    block_shape = (inputs.shape[0], rows_mb, inputs.shape[2])
    activations = jnp.zeros_like(inputs)
    kept_inputs = jnp.zeros((MICRO,) + block_shape, jnp.bfloat16)
    arriving = jnp.zeros(block_shape, jnp.bfloat16)
    for tick_index in range(ticks):
        own_index = min(tick_index, MICRO - 1)
        mb_slot = tick_index - section_index
        is_valid = (mb_slot >= 0) & (mb_slot < MICRO)
        mb_slot = jnp.clip(mb_slot, 0, MICRO - 1)
        fresh = lax.slice_in_dim(inputs, own_index * rows_mb, (own_index + 1) * rows_mb, axis=1)
        layer_input_rows = jnp.where(is_first, fresh, arriving)
        segment_row_span = lax.dynamic_slice_in_dim(segments, mb_slot * rows_mb, rows_mb, 0)
        layer_output_rows = forward_layer_step(
            layer_input_rows.astype(jnp.float32), segment_row_span, fixed_weights, adapter_pair
        ).astype(jnp.bfloat16)
        activations = jnp.where(
            is_valid,
            lax.dynamic_update_slice_in_dim(activations, layer_output_rows, mb_slot * rows_mb, 1),
            activations,
        )
        kept_inputs = jnp.where(
            is_valid, kept_inputs.at[mb_slot].set(layer_input_rows), kept_inputs
        )
        if tick_index < ticks - 1:
            arriving = passed_along(layer_output_rows, "section", 1)
    input_grads = jnp.zeros_like(inputs)
    gradient_totals = tuple(
        (jnp.zeros(factor_tensor.shape, jnp.float32) for factor_tensor in adapter_pair)
    )
    arriving = jnp.zeros(block_shape, jnp.bfloat16)
    for tick_index in range(ticks):
        own_index = min(tick_index, MICRO - 1)
        mb_slot = tick_index - (sections - 1 - section_index)
        is_valid = (mb_slot >= 0) & (mb_slot < MICRO)
        mb_slot = jnp.clip(mb_slot, 0, MICRO - 1)
        given = lax.slice_in_dim(cotangent, own_index * rows_mb, (own_index + 1) * rows_mb, axis=1)
        upstream_gradient = jnp.where(is_last, given, arriving).astype(jnp.float32)
        layer_input_rows = kept_inputs[mb_slot].astype(jnp.float32)
        segment_row_span = lax.dynamic_slice_in_dim(segments, mb_slot * rows_mb, rows_mb, 0)
        layer_output_rows, row_pieces = backward_layer_step(
            layer_input_rows, segment_row_span, upstream_gradient, fixed_weights, adapter_pair
        )
        leaving_b = layer_output_rows.astype(jnp.bfloat16)
        input_grads = jnp.where(
            is_valid,
            lax.dynamic_update_slice_in_dim(input_grads, leaving_b, mb_slot * rows_mb, 1),
            input_grads,
        )
        gradient_totals = tuple(
            (
                running + jnp.where(is_valid, piece_grad, 0.0)
                for running, piece_grad in zip(gradient_totals, row_pieces)
            )
        )
        if tick_index < ticks - 1:
            arriving = passed_along(leaving_b, "section", -1)
    adapter_rank = adapter_pair[1].shape[0]
    model_width = inputs.shape[2]
    column_total = adapter_pair[1].shape[1]
    offset = lax.axis_index("tensor") * column_total
    full_query = lax.dynamic_update_slice_in_dim(
        jnp.zeros((adapter_rank, model_width), jnp.float32), gradient_totals[1], offset, 1
    )
    full_value = lax.dynamic_update_slice_in_dim(
        jnp.zeros((adapter_rank, model_width), jnp.float32), gradient_totals[3], offset, 1
    )
    summed = lax.psum(
        (gradient_totals[0], full_query, gradient_totals[2], full_value), ("dp", "tensor")
    )
    return (
        activations[None],
        input_grads[None],
        summed[0][None],
        summed[1][None],
        summed[2][None],
        summed[3][None],
    )


REACH = 512
BF16 = jnp.bfloat16
F32 = jnp.float32
MESH = pl.DeviceIdType.MESH


def dot_nn(a, b):
    return lax.dot_general(a, b, (((1,), (0,)), ((), ())), preferred_element_type=F32)


def dot_nt(a, b):
    return lax.dot_general(a, b, (((1,), (1,)), ((), ())), preferred_element_type=F32)


def dot_tn(a, b):
    return lax.dot_general(a, b, (((0,), (0,)), ((), ())), preferred_element_type=F32)


def norm_stats(rows):
    middle = jnp.mean(rows, axis=-1, keepdims=True)
    centred = rows - middle
    inverse = lax.rsqrt(jnp.mean(centred * centred, axis=-1, keepdims=True) + EPSILON)
    return centred * inverse, inverse


def gelu_slope(pre):
    square = pre * pre
    bent = jnp.tanh(TANH_SCALE * (pre + CUBIC_TERM * square * pre))
    return 0.5 * (1.0 + bent) + (0.5 * TANH_SCALE) * pre * (1.0 - bent * bent) * (
        1.0 + (3.0 * CUBIC_TERM) * square
    )


def key_span(i, block):
    return max(0, i - REACH // block) * block, (i + 1) * block


def allowed_keys(i, block, seg_col_ref, seg_row_ref):
    low, high = key_span(i, block)
    seg_q = seg_col_ref[i * block : (i + 1) * block, :]
    seg_k = seg_row_ref[:, low:high]
    places_q = i * block + lax.broadcasted_iota(jnp.int32, (block, high - low), 0)
    places_k = low + lax.broadcasted_iota(jnp.int32, (block, high - low), 1)
    return (seg_q == seg_k) & (places_k <= places_q)


def head_lanes(rows, h):
    lane = lax.broadcasted_iota(jnp.int32, (rows, 128), 1)
    return (lane < HEAD_DIM) if h == 0 else (lane >= HEAD_DIM)


def both_halves(ref, *index):
    return jnp.concatenate([ref[(*index, 0)], ref[(*index, 1)]], axis=1)


class Wires:
    def __init__(self, send, recv):
        self.send, self.recv, self.count, self.sent = send, recv, 0, []

    def copy(self, source, target, where):
        k = self.count
        self.count += 1
        made = pltpu.make_async_remote_copy(
            src_ref=source,
            dst_ref=target,
            send_sem=self.send.at[k],
            recv_sem=self.recv.at[k],
            device_id=where,
            device_id_type=MESH,
        )
        self.sent.append(made)
        return made

    def forget(self, copy):
        self.sent = [one for one in self.sent if one is not copy]


WIRES = 96


def step_kernel(
    block,
    model,
    planes,
    x_rows,
    cot_rows,
    seg_cols,
    seg_rows,
    gain_a,
    gain_m,
    downs_t,
    up_q,
    up_v,
    wq,
    wo,
    fc,
    proj,
    act_out,
    grad_out,
    sums_out,
    act,
    grad,
    xb,
    cb,
    seg_col,
    seg_row,
    sm,
    up,
    pad,
    wq_all,
    up_all,
    wo_all,
    ff,
    rows,
    thin,
    qkv,
    o_out,
    o_in,
    middle,
    norm2,
    pre,
    part_out,
    part_in,
    own_sum,
    do_in,
    dqkv,
    dk_acc,
    dv_acc,
    c_out,
    c_in,
    y_out,
    y_in,
    down_sums,
    up_sums,
    total_out,
    total_in,
    wire_send,
    wire_recv,
    row_send,
    row_recv,
    wq_send,
    wq_recv,
    wq_half,
    local_sem,
    o_send,
    o_recv,
    place_send,
    place_recv,
):
    c = lax.axis_index("section")
    z = lax.axis_index("dp")
    t = lax.axis_index("tensor")
    y, x = lax.div(t, 2), lax.rem(t, 2)
    over_x, over_y = 2 * y + (1 - x), 2 * (1 - y) + x
    mine, twin = 2 * y + c, 2 * y + (1 - c)
    far, far_twin = 2 * (1 - y) + c, 2 * (1 - y) + (1 - c)
    to_c, to_x, to_y = {"section": 1 - c}, {"tensor": over_x}, {"tensor": over_y}
    to_xc = {"section": 1 - c, "tensor": over_x}
    to_yc = {"section": 1 - c, "tensor": over_y}
    to_zs = []
    bit = 1
    while bit < planes:
        up_bit = lax.rem(lax.div(z, bit), 2)
        to_zs.append({"dp": z + bit - 2 * bit * up_bit})
        bit *= 2
    to_z = to_zs[0]
    odd = lax.rem(z, 2)
    here = c == x
    wires = Wires(wire_send, wire_recv)
    width = wq.shape[2]
    factor = 8.0

    barrier = pltpu.get_barrier_semaphore()
    peers = [to_c, to_x, to_y, to_xc, to_yc, *to_zs]
    for peer in peers:
        pl.semaphore_signal(barrier, inc=1, device_id=peer, device_id_type=MESH)
    pl.semaphore_wait(barrier, len(peers))

    def part(which, count):
        first = odd if which == 0 else 1 - odd
        return pl.ds(pl.multiple_of(first * (count // 2), count // 2), count // 2)

    def row_copy(source, target, k):
        return pltpu.make_async_remote_copy(
            src_ref=source,
            dst_ref=target,
            send_sem=row_send.at[k],
            recv_sem=row_recv.at[k],
            device_id=to_x,
            device_id_type=MESH,
        )

    x_copy = row_copy(x_rows.at[1 - x], xb, 0)

    @pl.when(here)
    def _():
        x_copy.start()
        pltpu.make_async_copy(x_rows.at[x], xb, row_recv.at[0]).start()

    pad[...] = jnp.zeros_like(pad)
    pad[0:4] = up_q[...].astype(F32)
    up[0] = pad[...].astype(BF16)
    pad[0:4] = jnp.zeros((4, width), F32)
    pad[4:8] = up_v[...].astype(F32)
    up[1] = pad[...].astype(BF16)

    def wq_twin():
        return [
            pltpu.make_async_remote_copy(
                src_ref=source,
                dst_ref=target.at[c],
                send_sem=wq_send.at[0, j],
                recv_sem=wq_recv.at[c, j],
                device_id=to_c,
                device_id_type=MESH,
            )
            for j, (source, target) in enumerate(((wq, wq_all), (up, up_all)))
        ]

    def wq_over_x():
        cut = part(0, model)
        where = {"section": x, "tensor": over_x}
        return [
            pltpu.make_async_remote_copy(
                src_ref=wq.at[:, cut],
                dst_ref=wq_all.at[c, :, cut],
                send_sem=wq_send.at[1, 0],
                recv_sem=wq_half.at[c, 0],
                device_id=where,
                device_id_type=MESH,
            ),
            pltpu.make_async_remote_copy(
                src_ref=up,
                dst_ref=up_all.at[c],
                send_sem=wq_send.at[1, 1],
                recv_sem=wq_recv.at[c, 1],
                device_id=where,
                device_id_type=MESH,
            ),
        ]

    def wq_over_z(layer):
        cut = part(0, model)
        return pltpu.make_async_remote_copy(
            src_ref=wq_all.at[layer, :, cut],
            dst_ref=wq_all.at[layer, :, cut],
            send_sem=wq_send.at[2, layer],
            recv_sem=wq_half.at[layer, 1],
            device_id=to_z,
            device_id_type=MESH,
        )

    def wq_local(layer):
        return [
            pltpu.make_async_copy(source, target.at[layer], wq_recv.at[layer, j])
            for j, (source, target) in enumerate(((wq, wq_all), (up, up_all)))
        ]

    def send_wq():
        for copy in wq_over_x():
            copy.start()

        @pl.when(here)
        def _():
            for copy in wq_local(c):
                copy.start()

        @pl.when(jnp.logical_not(here))
        def _():
            for copy in wq_twin():
                copy.start()

    def half_wait(layer, k):
        cut = part(k, model)
        pltpu.make_async_copy(wq.at[:, cut], wq_all.at[layer, :, cut], wq_half.at[layer, k]).wait()

    def pass_wq(layer):
        @pl.when(jnp.logical_not(here))
        def _():
            half_wait(layer, 0)
            wq_over_z(layer).start()

    def arrived_wq(layer):
        whole, small = wq_local(layer)
        small.wait()
        pl.when(here)(whole.wait)

        @pl.when(jnp.logical_not(here))
        def _():
            half_wait(layer, 1)

    def sent_wq():
        for copy in wq_over_x():
            copy.wait_send()

        @pl.when(jnp.logical_not(here))
        def _():
            for copy in wq_twin():
                copy.wait_send()
            for layer in range(2):
                wq_over_z(layer).wait_send()

    pl.when(c == 0)(send_wq)

    sm[c, 0:1] = gain_a[...]
    sm[c, 8:9] = gain_m[...]
    sm[c, 16:24] = downs_t[...].astype(F32)
    sm[c, 24:32] = jnp.zeros((8, model), F32)
    small_copy = wires.copy(sm.at[c], sm.at[c], to_c)
    small_copy.start()
    seg_row[...] = seg_rows[pl.ds(x, 1), :]
    seg_col[...] = jnp.where(x == 0, seg_cols[:, 0:1], seg_cols[:, 1:2])

    locals_ = [
        pltpu.make_async_copy(source, target, local_sem.at[k])
        for k, (source, target) in enumerate(
            ((fc, ff.at[c, 0, 0]), (proj, ff.at[c, 1, 0]), (wo, wo_all.at[c, t]))
        )
    ]
    ff_cut, ff_rest = part(0, model), part(1, model)
    ff_twin = [wires.copy(one, ff.at[c, k, 0], to_c) for k, one in enumerate((fc, proj))]
    ff_y = [
        wires.copy(one.at[ff_cut], ff.at[c, k, 1, ff_cut], to_y) for k, one in enumerate((fc, proj))
    ]
    ff_z = [wires.copy(ff.at[c, k, 1, ff_cut], ff.at[c, k, 1, ff_cut], to_z) for k in range(2)]
    ff_c = [
        [wires.copy(ff.at[c, k, 1, cut], ff.at[c, k, 1, cut], to_c) for cut in (ff_cut, ff_rest)]
        for k in range(2)
    ]

    def on_core(layer, action):
        pl.when(c == layer)(action)

    def start_ff(layer):
        @pl.when(c == layer)
        def _():
            for copy in ff_y:
                copy.start()

    def pass_ff_y(layer, k):
        @pl.when(c == layer)
        def _():
            ff_y[k].wait_recv()
            ff_z[k].start()
            ff_c[k][0].start()

    def pass_ff_z(layer, k):
        @pl.when(c == layer)
        def _():
            ff_z[k].wait_recv()
            ff_c[k][1].start()

    def arrived_ff(layer):
        @pl.when(c != layer)
        def _():
            for pair in ff_c:
                for copy in pair:
                    copy.wait_recv()

    corner = 2 * (1 - y) + (1 - x)
    wo_cut = part(0, width)
    quart = width // 4
    wo_low = pl.ds(pl.multiple_of(odd * (width // 2), quart), quart)
    wo_high = pl.ds(pl.multiple_of(odd * (width // 2) + quart, quart), quart)

    def wo_same(q, cut, where):
        if cut is None:
            return wires.copy(wo_all.at[c, q], wo_all.at[c, q], where)
        return wires.copy(wo_all.at[c, q, cut], wo_all.at[c, q, cut], where)

    wo_twin = wires.copy(wo, wo_all.at[c, t], to_c)
    wo_x = wires.copy(wo.at[wo_cut], wo_all.at[c, t, wo_cut], to_x)
    wo_y = wires.copy(wo.at[wo_cut], wo_all.at[c, t, wo_cut], to_y)
    wo_dy = wo_same(over_x, wo_low, to_y)
    wo_dx = wo_same(over_y, wo_high, to_x)
    wo_z = [wo_same(q, wo_cut, to_z) for q in (over_x, over_y, corner)]
    wo_c = [wo_same(q, None, to_c) for q in (over_x, over_y, corner)]

    def start_wo(layer):
        @pl.when(c == layer)
        def _():
            wo_x.start()
            wo_y.start()

    def pass_wo(layer, stage):
        @pl.when(c == layer)
        def _():
            if stage == 0:
                wo_x.wait_recv()
                wo_dy.start()
                wo_z[0].start()
                wo_y.wait_recv()
                wo_dx.start()
                wo_z[1].start()
            if stage == 1:
                wo_dy.wait_recv()
                wo_dx.wait_recv()
                wo_z[2].start()
            if stage == 2:
                for came, onward in zip(wo_z, wo_c):
                    came.wait_recv()
                    onward.start()

    def arrived_wo(layer):
        @pl.when(c == layer)
        def _():
            locals_[2].wait()

        @pl.when(c != layer)
        def _():
            wo_twin.wait_recv()
            for copy in wo_c:
                copy.wait_recv()

    start_ff(0)
    start_wo(0)
    for copy in locals_:
        copy.start()
    for copy in ff_twin + [wo_twin]:
        copy.start()

    def place_copy(kind, layer, source, target):
        return pltpu.make_async_remote_copy(
            src_ref=source,
            dst_ref=target.at[x],
            send_sem=place_send.at[kind, layer],
            recv_sem=place_recv.at[kind, x],
            device_id={"section": layer, "tensor": mine},
            device_id_type=MESH,
        )

    def place(kind, layer, source, target):
        stays = jnp.logical_and(here, c == layer)

        @pl.when(stays)
        def _():
            target[x] = source[...]

        @pl.when(jnp.logical_not(stays))
        def _():
            place_copy(kind, layer, source, target).start()

    def placed(kind, source, target):
        for layer in range(2):
            stays = jnp.logical_and(here, c == layer)

            @pl.when(jnp.logical_not(stays))
            def _():
                place_copy(kind, layer, source.at[layer], target).wait_send()

        for slot in range(2):
            came = jnp.logical_not(jnp.logical_and(here, x == slot))

            @pl.when(came)
            def _():
                pltpu.make_async_copy(
                    source.at[0], target.at[slot], place_recv.at[kind, slot]
                ).wait()

    def qkv_block(layer, b):
        normed = rows[layer, b]
        down = sm[layer, 16:32, :].astype(BF16)
        low = dot_nt(normed, down)
        low_b = low.astype(BF16)
        thin[layer, b] = low_b
        at = pl.ds(pl.multiple_of(b * block, block), block)
        for k in range(3):
            made = dot_nn(normed, wq_all[layer, k])
            if k == 0:
                made = made + factor * dot_nn(low_b, up_all[layer, 0])
            if k == 2:
                made = made + factor * dot_nn(low_b, up_all[layer, 1])
            made = made.astype(BF16)
            qkv[layer, k, 0, at, :] = made[:, :128]
            qkv[layer, k, 1, at, :] = made[:, 128:]

    def attend(layer, i):
        low, high = key_span(i, block)
        at = slice(i * block, (i + 1) * block)
        allowed = allowed_keys(i, block, seg_col, seg_row)

        def one_pair(pair, carry):
            queries = qkv[layer, 0, pair, at, :] * BF16(HEAD_DIM**-0.5)
            keys = qkv[layer, 1, pair, low:high, :]
            values = qkv[layer, 2, pair, low:high, :]
            parts = []
            for h in range(2):
                picked = jnp.where(head_lanes(block, h), queries, BF16(0))
                scores = jnp.where(allowed, dot_nt(picked, keys), MASKED)
                exponent = jnp.exp(scores - jnp.max(scores, axis=-1, keepdims=True))
                total = jnp.sum(exponent, axis=-1, keepdims=True)
                parts.append(dot_nn(exponent.astype(BF16), values) / total)
            o_out[i, pair] = jnp.where(head_lanes(block, 0), parts[0], parts[1]).astype(BF16)
            return carry

        lax.fori_loop(0, 2, one_pair, 0)

    def exchange_piece(i, target, phase):
        return pltpu.make_async_remote_copy(
            src_ref=o_out.at[i],
            dst_ref=target.at[mine],
            send_sem=o_send.at[i],
            recv_sem=o_recv.at[phase, mine],
            device_id={"section": i % 2, "tensor": 2 * (i // 2) + x},
            device_id_type=MESH,
        )

    def send_piece(i, target, phase):
        @pl.when(mine == i)
        def _():
            target[mine] = o_out[i]

        @pl.when(mine != i)
        def _():
            exchange_piece(i, target, phase).start()

    def wait_pieces(target, phase):
        for i in range(4):

            @pl.when(mine != i)
            def _():
                exchange_piece(i, target, phase).wait_send()
                pltpu.make_async_copy(o_out.at[i], target.at[i], o_recv.at[phase, i]).wait()

    def hidden_half(layer, who, source, q):
        total = None
        for cut in range(2):
            lanes = slice(cut * model // 2, (cut + 1) * model // 2)
            made = dot_nn(source, ff[layer, 0, q, :, lanes])
            pre[layer, who, q, :, lanes] = made.astype(BF16)
            term = dot_nn(gelu_tanh(made).astype(BF16), ff[layer, 1, q, lanes, :])
            total = term if total is None else total + term
        return total

    def hidden_back(layer, who, upstream, q):
        total = None
        for cut in range(2):
            lanes = slice(cut * model // 2, (cut + 1) * model // 2)
            grad_hidden = dot_nt(upstream, ff[layer, 1, q, lanes, :])
            slope = gelu_slope(pre[layer, who, q, :, lanes].astype(F32))
            term = dot_nt((grad_hidden * slope).astype(BF16), ff[layer, 0, q, :, lanes])
            total = term if total is None else total + term
        return total

    pltpu.make_async_copy(x_rows.at[x], xb, row_recv.at[0]).wait()
    small_copy.wait_recv()
    cot_copies = [
        row_copy(cot_rows.at[1 - x], cb.at[0], 1),
        row_copy(cot_rows.at[x], cb.at[1], 2),
    ]

    cot_local = [
        pltpu.make_async_copy(cot_rows.at[x], cb.at[0], row_recv.at[1]),
        pltpu.make_async_copy(cot_rows.at[1 - x], cb.at[1], row_recv.at[2]),
    ]

    for layer in range(2):
        source = xb if layer == 0 else act.at[0]
        unit, _ = norm_stats(source[...].astype(F32))
        rows[layer, mine] = (unit * sm[layer, 0:1, :]).astype(BF16)
        row_y = wires.copy(rows.at[layer, mine], rows.at[layer, mine], to_y)
        row_c = wires.copy(rows.at[layer, mine], rows.at[layer, mine], to_c)
        row_yc = wires.copy(rows.at[layer, far], rows.at[layer, far], to_c)
        row_y.start()
        row_c.start()
        if layer == 0:
            pass_wq(0)
            pass_wo(0, 0)
        else:
            place(0, 0, act.at[0], act_out)

            @pl.when(here)
            def _():
                for copy in cot_copies:
                    copy.start()
                for copy in cot_local:
                    copy.start()

            pass_ff_z(1, 0)
            pass_wo(1, 2)
        arrived_wq(layer)
        if layer == 0:
            pl.when(c == 1)(send_wq)
        qkv_block(layer, mine)
        row_c.wait_recv()
        qkv_block(layer, twin)
        if layer == 0:
            pass_ff_y(0, 0)
        row_y.wait_recv()
        row_yc.start()
        qkv_block(layer, far)
        row_yc.wait_recv()
        qkv_block(layer, far_twin)
        if layer == 0:
            pass_wo(0, 1)
        for i in range(4):
            attend(layer, i)
            send_piece(i, o_in, layer)
            if layer == 0 and i == 0:
                pass_ff_y(0, 1)
            if layer == 0 and i == 2:
                pass_ff_z(0, 0)
                pass_wo(0, 2)
        if layer == 0:
            pass_wq(1)
        else:
            pass_ff_z(1, 1)
        arrived_wo(layer)
        wait_pieces(o_in, layer)
        stream = source[...].astype(F32)
        for q in range(4):
            stream = stream + dot_nn(both_halves(o_in, q), wo_all[layer, q])
        middle[layer] = stream
        unit, _ = norm_stats(stream)
        norm2[0] = (unit * sm[layer, 8:9, :]).astype(BF16)
        norm_x = wires.copy(norm2.at[0], norm2.at[1], to_x)
        norm_x.start()
        if layer == 0:
            start_ff(1)
            start_wo(1)
            pass_ff_z(0, 1)
            for copy in locals_[:2]:
                copy.wait()
            for copy in ff_twin:
                copy.wait_recv()
        own_sum[...] = hidden_half(layer, 0, norm2[0], 0)
        arrived_ff(layer)
        own_sum[...] += hidden_half(layer, 0, norm2[0], 1)
        norm_x.wait_recv()
        away = hidden_half(layer, 1, norm2[1], 0) + hidden_half(layer, 1, norm2[1], 1)
        part_out[...] = away.astype(BF16)
        part_x = wires.copy(part_out, part_in.at[0], to_x)
        part_x.start()
        if layer == 0:
            pass_ff_y(1, 0)
            pass_wo(1, 0)
        stream = middle[layer] + own_sum[...]
        if layer == 0:
            pass_ff_y(1, 1)
            pass_wo(1, 1)
        part_x.wait()
        wires.forget(part_x)
        norm_x.wait_send()
        wires.forget(norm_x)
        act[layer] = (stream + part_in[0].astype(F32)).astype(BF16)

    for copy in cot_local:
        copy.wait()

    for layer in (1, 0):
        upstream = cb[0] if layer == 1 else grad[1]
        if layer == 1:
            away = hidden_back(layer, 1, cb[1], 0) + hidden_back(layer, 1, cb[1], 1)
        else:
            up_x = wires.copy(grad.at[1], norm2.at[1], to_x)
            up_x.start()
            own_sum[...] = hidden_back(layer, 0, upstream, 0) + hidden_back(layer, 0, upstream, 1)
            up_x.wait_recv()
            away = hidden_back(layer, 1, norm2[1], 0) + hidden_back(layer, 1, norm2[1], 1)
        part_out[...] = away.astype(BF16)
        part_x = wires.copy(part_out, part_in.at[1], to_x)
        part_x.start()
        if layer == 1:
            place(0, 1, act.at[1], act_out)
            own_sum[...] = hidden_back(layer, 0, upstream, 0) + hidden_back(layer, 0, upstream, 1)
        unit, inverse = norm_stats(middle[layer])
        part_x.wait()
        wires.forget(part_x)
        grad_norm = own_sum[...] + part_in[1].astype(F32)
        grad_middle = upstream.astype(F32) + normalize_back(
            grad_norm, unit, inverse, sm[layer, 8:9, :]
        )
        own_sum[...] = grad_middle
        grad_b = grad_middle.astype(BF16)
        for q in range(4):
            made = dot_nt(grad_b, wo_all[layer, q]).astype(BF16)
            o_out[q, 0] = made[:, :128]
            o_out[q, 1] = made[:, 128:]
            send_piece(q, do_in, 2 + layer)
        if layer == 0:
            place(1, 1, grad.at[1], grad_out)
        wait_pieces(do_in, 2 + layer)

        def back_pair(pair, carry):
            dk_acc[...] = jnp.zeros_like(dk_acc)
            dv_acc[...] = jnp.zeros_like(dv_acc)
            for i in range(4):
                low, high = key_span(i, block)
                at = slice(i * block, (i + 1) * block)
                allowed = allowed_keys(i, block, seg_col, seg_row)
                queries = qkv[layer, 0, pair, at, :] * BF16(HEAD_DIM**-0.5)
                keys = qkv[layer, 1, pair, low:high, :]
                values = qkv[layer, 2, pair, low:high, :]
                grads = do_in[i, pair]
                parts = []
                for h in range(2):
                    lanes = head_lanes(block, h)
                    picked = jnp.where(lanes, queries, BF16(0))
                    given = jnp.where(lanes, grads, BF16(0))
                    scores = jnp.where(allowed, dot_nt(picked, keys), MASKED)
                    exponent = jnp.exp(scores - jnp.max(scores, axis=-1, keepdims=True))
                    soft = exponent * (1.0 / jnp.sum(exponent, axis=-1, keepdims=True))
                    weighted = soft * dot_nt(given, values)
                    grad_scores = (
                        weighted - soft * jnp.sum(weighted, axis=-1, keepdims=True)
                    ).astype(BF16)
                    parts.append(dot_nn(grad_scores, keys))
                    dk_acc[low:high, :] += dot_tn(grad_scores, picked)
                    dv_acc[low:high, :] += dot_tn(soft.astype(BF16), given)
                dqkv[0, pair, at, :] = (
                    jnp.where(head_lanes(block, 0), parts[0], parts[1]) * HEAD_DIM**-0.5
                ).astype(BF16)
            dqkv[1, pair] = dk_acc[...].astype(BF16)
            dqkv[2, pair] = dv_acc[...].astype(BF16)
            return carry

        lax.fori_loop(0, 2, back_pair, 0)
        down = sm[layer, 16:32, :].astype(BF16)

        def block_grad(b, first):
            at = pl.ds(pl.multiple_of(b * block, block), block)
            parts = [
                jnp.concatenate([dqkv[k, 0, at, :], dqkv[k, 1, at, :]], axis=1) for k in range(3)
            ]
            low = factor * (
                dot_nt(parts[0], up_all[layer, 0]) + dot_nt(parts[2], up_all[layer, 1])
            )
            low_b = low.astype(BF16)
            term = dot_nn(low_b, down)
            for k in range(3):
                term = term + dot_nt(parts[k], wq_all[layer, k])
            kept = thin[layer, b]
            to_down = dot_tn(low_b, rows[layer, b])
            to_up = [factor * dot_tn(kept, parts[0]), factor * dot_tn(kept, parts[2])]
            if first:
                down_sums[...] = to_down
                up_sums[0], up_sums[1] = to_up
            else:
                down_sums[...] += to_down
                up_sums[0] += to_up[0]
                up_sums[1] += to_up[1]
            return term

        c_far = wires.copy(c_out.at[0], c_in.at[0], to_c)
        c_near = wires.copy(c_out.at[1], c_in.at[1], to_c)
        y_far = wires.copy(y_out, y_in, to_y)
        c_out[0] = block_grad(far_twin, True).astype(BF16)
        c_far.start()
        term = block_grad(far, False)
        c_far.wait_recv()
        y_out[...] = (term + c_in[0].astype(F32)).astype(BF16)
        y_far.start()
        c_out[1] = block_grad(twin, False).astype(BF16)
        c_near.start()
        term = block_grad(mine, False)
        total_out[layer, 0, 0:8] = down_sums[0:8]
        total_out[layer, 0, 8:16] = jnp.zeros((8, model), F32)
        low_rows = lax.broadcasted_iota(jnp.int32, (8, width), 0) < 4
        total_out[
            layer, 0, 8:16, pl.ds(pl.multiple_of(mine * width, width), width)
        ] = jnp.where(low_rows, up_sums[0, 0:8], up_sums[1, 0:8])
        hops = [to_c, to_x, to_y, *to_zs]
        for k, peer in enumerate(hops):
            hop = wires.copy(total_out.at[layer, k], total_in.at[layer, k], peer)
            hop.start()
            if k == 0:
                c_near.wait_recv()
                term = term + c_in[1].astype(F32)
                source = xb if layer == 0 else act.at[0]
                unit, inverse = norm_stats(source[...].astype(F32))
            hop.wait_recv()
            summed = total_out[layer, k] + total_in[layer, k]
            if k + 1 < len(hops):
                total_out[layer, k + 1] = summed
            else:

                @pl.when(c == layer)
                def _():
                    sums_out[...] = summed

        y_far.wait_recv()
        grad_norm = term + y_in[...].astype(F32)
        grad[layer] = (
            own_sum[...] + normalize_back(grad_norm, unit, inverse, sm[layer, 0:1, :])
        ).astype(BF16)
        for copy in (c_far, c_near, y_far):
            copy.wait_send()
            wires.forget(copy)

    @pl.when(here)
    def _():
        x_copy.wait_send()
        for copy in cot_copies:
            copy.wait_send()

    place(1, 0, grad.at[0], grad_out)
    sent_wq()
    for copy in wires.sent:
        copy.wait_send()
    placed(0, act, act_out)
    placed(1, grad, grad_out)


def step_call(block, model, width, planes, operands):
    slots = 4 * block
    hops = 3 + (planes - 1).bit_length()
    in_vmem = pl.BlockSpec(memory_space=pltpu.VMEM)
    in_hbm = pl.BlockSpec(memory_space=pl.ANY)
    return pl.pallas_call(
        functools.partial(step_kernel, block, model, planes),
        out_shape=(
            jax.ShapeDtypeStruct((2, block, model), BF16),
            jax.ShapeDtypeStruct((2, block, model), BF16),
            jax.ShapeDtypeStruct((16, model), F32),
        ),
        in_specs=[in_hbm] * 2 + [in_vmem] * 7 + [in_hbm] * 4,
        out_specs=[in_vmem] * 3,
        scratch_shapes=[
            pltpu.VMEM((2, block, model), BF16),
            pltpu.VMEM((2, block, model), BF16),
            pltpu.VMEM((block, model), BF16),
            pltpu.VMEM((2, block, model), BF16),
            pltpu.VMEM((slots, 1), jnp.int32),
            pltpu.VMEM((1, slots), jnp.int32),
            pltpu.VMEM((2, 32, model), F32),
            pltpu.VMEM((2, 16, width), BF16),
            pltpu.VMEM((16, width), F32),
            pltpu.VMEM((2, 3, model, width), BF16),
            pltpu.VMEM((2, 2, 16, width), BF16),
            pltpu.VMEM((2, 4, width, model), BF16),
            pltpu.VMEM((2, 2, 2, model, model), BF16),
            pltpu.VMEM((2, 4, block, model), BF16),
            pltpu.VMEM((2, 4, block, 16), BF16),
            pltpu.VMEM((2, 3, 2, slots, 128), BF16),
            pltpu.VMEM((4, 2, block, 128), BF16),
            pltpu.VMEM((4, 2, block, 128), BF16),
            pltpu.VMEM((2, block, model), F32),
            pltpu.VMEM((2, block, model), BF16),
            pltpu.VMEM((2, 2, 2, block, model), BF16),
            pltpu.VMEM((block, model), BF16),
            pltpu.VMEM((2, block, model), BF16),
            pltpu.VMEM((block, model), F32),
            pltpu.VMEM((4, 2, block, 128), BF16),
            pltpu.VMEM((3, 2, slots, 128), BF16),
            pltpu.VMEM((slots, 128), F32),
            pltpu.VMEM((slots, 128), F32),
            pltpu.VMEM((2, block, model), BF16),
            pltpu.VMEM((2, block, model), BF16),
            pltpu.VMEM((block, model), BF16),
            pltpu.VMEM((block, model), BF16),
            pltpu.VMEM((16, model), F32),
            pltpu.VMEM((2, 16, width), F32),
            pltpu.VMEM((2, hops, 16, model), F32),
            pltpu.VMEM((2, hops, 16, model), F32),
            pltpu.SemaphoreType.DMA((WIRES,)),
            pltpu.SemaphoreType.DMA((WIRES,)),
            pltpu.SemaphoreType.DMA((3,)),
            pltpu.SemaphoreType.DMA((3,)),
            pltpu.SemaphoreType.DMA((3, 2)),
            pltpu.SemaphoreType.DMA((2, 2)),
            pltpu.SemaphoreType.DMA((2, 2)),
            pltpu.SemaphoreType.DMA((3,)),
            pltpu.SemaphoreType.DMA((4,)),
            pltpu.SemaphoreType.DMA((4, 4)),
            pltpu.SemaphoreType.DMA((2, 2)),
            pltpu.SemaphoreType.DMA((2, 2)),
        ],
        compiler_params=pltpu.CompilerParams(
            collective_id=0, has_side_effects=True, vmem_limit_bytes=62 * 1024 * 1024
        ),
    )(*operands)


def fast_body(
    planes,
    inputs,
    segments,
    cotangent,
    gain_attn,
    joint_projection_weight,
    query_down_factor,
    query_up_factor,
    value_down_factor,
    value_up_factor,
    w_out,
    gain_mlp,
    w_fc,
    w_proj,
):
    block, _, model = inputs.shape
    width = joint_projection_weight.shape[3]
    rank = query_down_factor.shape[2]
    downs = jnp.concatenate([query_down_factor[0], value_down_factor[0]], axis=1)
    acts, grads, total = step_call(
        block,
        model,
        width,
        planes,
        (
            jnp.swapaxes(inputs, 0, 1),
            jnp.swapaxes(cotangent, 0, 1),
            segments.T,
            segments,
            gain_attn,
            gain_mlp,
            downs.T,
            query_up_factor[0],
            value_up_factor[0],
            jnp.swapaxes(joint_projection_weight[0], 0, 1),
            w_out[0],
            w_fc[0],
            w_proj[0],
        ),
    )
    return (
        jnp.swapaxes(acts, 0, 1)[None],
        jnp.swapaxes(grads, 0, 1)[None],
        total[:rank].T[None],
        total[2 * rank : 3 * rank][None],
        total[rank : 2 * rank].T[None],
        total[3 * rank :][None],
    )


def fits_fast(mesh, shapes):
    planes = mesh.shape["dp"]
    slots, rows_all, model = shapes[0]
    return (
        mesh.shape["section"] == 2
        and mesh.shape["tensor"] == 4
        and planes > 1
        and planes & (planes - 1) == 0
        and rows_all == 2 * planes
        and slots == 1024
        and model == 1024
        and shapes[4][3] == 1024
        and shapes[5][2] == 4
        and shapes[11][2] == 4096
    )


def solution(mesh):
    placed = (
        P("tensor", "dp", None),
        P("dp", None),
        P("tensor", "dp", None),
        P("section", None),
        P("section", None, None, "tensor"),
        P("section", None, None),
        P("section", None, "tensor"),
        P("section", None, None),
        P("section", None, "tensor"),
        P("section", "tensor", None),
        P("section", None),
        P("section", None, "tensor"),
        P("section", "tensor", None),
    )

    def mapped(picked):
        return jax.shard_map(
            picked,
            mesh=mesh,
            in_specs=placed,
            out_specs=(
                P("section", "tensor", "dp", None),
                P("section", "tensor", "dp", None),
                P("section", None, None),
                P("section", None, None),
                P("section", None, None),
                P("section", None, None),
            ),
            check_vma=False,
        )

    def choose(*args):
        if fits_fast(mesh, [a.shape for a in args]):
            return mapped(functools.partial(fast_body, mesh.shape["dp"]))(*args)
        return mapped(body)(*args)

    return choose
```

```python
import functools

import jax
import jax.numpy as jnp
from jax import lax
from jax.experimental import pallas as pl
from jax.experimental.pallas import tpu as pltpu
from jax.sharding import PartitionSpec as P

HEAD_DIM = 64
MICRO = 2


EPSILON = 1e-05
PRECISE = lax.Precision.HIGHEST
MASKED = -1000000000.0
CUBIC_TERM = 0.044715
TANH_SCALE = 0.7978845608028654


def passed_along(block, axis, distance):
    devices = range(lax.axis_size(axis))
    route = [(i - distance, i) for i in devices if i - distance in devices]
    return lax.ppermute(block, axis, route)


def gelu_tanh(value):
    return 0.5 * value * (1.0 + jnp.tanh(TANH_SCALE * (value + CUBIC_TERM * value * value * value)))


def normalize(residual_stream, gain):
    middle = jnp.mean(residual_stream, axis=-1, keepdims=True)
    centred = residual_stream - middle
    inverse = lax.rsqrt(jnp.mean(centred * centred, axis=-1, keepdims=True) + EPSILON)
    unit_rows = centred * inverse
    return (unit_rows * gain, unit_rows, inverse)


def normalize_back(grad_norm, unit_rows, inverse, gain):
    scaled = grad_norm * gain
    return inverse * (
        scaled
        - jnp.mean(scaled, axis=-1, keepdims=True)
        - unit_rows * jnp.mean(scaled * unit_rows, axis=-1, keepdims=True)
    )


def block_mask(segment_row_span, first_row, block):
    length = segment_row_span.shape[1]
    segment_part = lax.dynamic_slice_in_dim(segment_row_span, first_row, block, 1)
    query_places = first_row + jnp.arange(block)
    key_places = jnp.arange(length)
    same_doc = segment_part[:, :, None] == segment_row_span[:, None, :]
    return same_doc & (key_places[None, None, :] <= query_places[None, :, None])


def projected_rows(row_portion, joint_projection_weight, adapter_pair):
    query_down_factor, query_up_factor, value_down_factor, value_up_factor = adapter_pair
    factor = 32.0 / query_down_factor.shape[-1]
    joined = jnp.einsum(
        "srd,dcf->srcf", row_portion, joint_projection_weight, preferred_element_type=jnp.float32
    )
    narrow_query_rows = jnp.einsum(
        "srd,dk->srk", row_portion, query_down_factor, preferred_element_type=jnp.float32
    )
    narrow_value_rows = jnp.einsum(
        "srd,dk->srk", row_portion, value_down_factor, preferred_element_type=jnp.float32
    )
    queries = joined[:, :, 0] + factor * jnp.einsum(
        "srk,kf->srf", narrow_query_rows, query_up_factor.astype(jnp.float32), precision=PRECISE
    )
    values_all = joined[:, :, 2] + factor * jnp.einsum(
        "srk,kf->srf", narrow_value_rows, value_up_factor.astype(jnp.float32), precision=PRECISE
    )
    stacked_weights = jnp.stack([queries, joined[:, :, 1], values_all], axis=2).astype(jnp.bfloat16)
    return (stacked_weights, narrow_query_rows, narrow_value_rows)


def attention_forward(queries, keys_all, values_all, segment_row_span):
    length, row_count, head_count, width = queries.shape
    block = min(512, length)
    factor = width ** (-0.5)

    def one_block(block_index):
        first_row = block_index * block
        query_part = lax.dynamic_slice_in_dim(queries, first_row, block, 0)
        scores = (
            jnp.einsum("qrhe,krhe->rhqk", query_part, keys_all, preferred_element_type=jnp.float32)
            * factor
        )
        allowed = block_mask(segment_row_span, first_row, block)
        scores = jnp.where(allowed[:, None], scores, MASKED)
        row_max = jnp.max(scores, axis=-1, keepdims=True)
        exponent = jnp.exp(scores - row_max)
        total = jnp.sum(exponent, axis=-1, keepdims=True)
        weights_soft = (exponent / total).astype(jnp.bfloat16)
        attended = jnp.einsum(
            "rhqk,krhe->qrhe", weights_soft, values_all, preferred_element_type=jnp.float32
        )
        return (attended, (row_max + jnp.log(total))[..., 0])

    attended, log_sums = lax.map(one_block, jnp.arange(length // block))
    attended = attended.reshape(length, row_count, head_count, width)
    log_sums = jnp.moveaxis(log_sums, 0, 2).reshape(row_count, head_count, length)
    return (attended, log_sums)


def attention_backward(queries, keys_all, values_all, segment_row_span, log_sums, grad_heads):
    length = queries.shape[0]
    block = min(512, length)
    factor = queries.shape[-1] ** (-0.5)

    def one_block(carry, block_index):
        grad_keys, grad_values = carry
        first_row = block_index * block
        query_part = lax.dynamic_slice_in_dim(queries, first_row, block, 0)
        grad_part = lax.dynamic_slice_in_dim(grad_heads, first_row, block, 0)
        sums_part = lax.dynamic_slice_in_dim(log_sums, first_row, block, 2)
        scores = (
            jnp.einsum("qrhe,krhe->rhqk", query_part, keys_all, preferred_element_type=jnp.float32)
            * factor
        )
        allowed = block_mask(segment_row_span, first_row, block)
        scores = jnp.where(allowed[:, None], scores, MASKED)
        weights_soft = jnp.exp(scores - sums_part[..., None])
        grad_soft = jnp.einsum(
            "qrhe,krhe->rhqk", grad_part, values_all, preferred_element_type=jnp.float32
        )
        grad_scores = weights_soft * (
            grad_soft - jnp.sum(weights_soft * grad_soft, axis=-1, keepdims=True)
        )
        grad_scores = grad_scores.astype(jnp.bfloat16)
        grad_query = (
            jnp.einsum("rhqk,krhe->qrhe", grad_scores, keys_all, preferred_element_type=jnp.float32)
            * factor
        )
        grad_keys = (
            grad_keys
            + jnp.einsum(
                "rhqk,qrhe->krhe", grad_scores, query_part, preferred_element_type=jnp.float32
            )
            * factor
        )
        grad_values = grad_values + jnp.einsum(
            "rhqk,qrhe->krhe",
            weights_soft.astype(jnp.bfloat16),
            grad_part,
            preferred_element_type=jnp.float32,
        )
        return ((grad_keys, grad_values), grad_query)

    start_state = (jnp.zeros(keys_all.shape, jnp.float32), jnp.zeros(values_all.shape, jnp.float32))
    (grad_keys, grad_values), grad_blocks = lax.scan(
        one_block, start_state, jnp.arange(length // block)
    )
    return (grad_blocks.reshape(queries.shape), grad_keys, grad_values)


def attend_all(stacked_weights, segment_row_span):
    length, row_count = (stacked_weights.shape[0], stacked_weights.shape[1])
    head_view = stacked_weights.reshape(length, row_count, 3, -1, HEAD_DIM)
    queries, keys_all, values_all = (head_view[:, :, 0], head_view[:, :, 1], head_view[:, :, 2])
    attended, log_sums = attention_forward(queries, keys_all, values_all, segment_row_span)
    return (
        attended.reshape(length, row_count, -1).astype(jnp.bfloat16),
        log_sums,
        (queries, keys_all, values_all),
    )


def attention_project(attended_b, w_out):
    return lax.psum_scatter(
        jnp.einsum("srf,fd->srd", attended_b, w_out, preferred_element_type=jnp.float32).astype(
            jnp.bfloat16
        ),
        "tensor",
        scatter_dimension=0,
        tiled=True,
    ).astype(jnp.float32)


def attention_grad_heads(grad_middle_b, w_out):
    grad_attended = jnp.einsum(
        "srd,fd->srf",
        lax.all_gather(grad_middle_b, "tensor", axis=0, tiled=True),
        w_out,
        preferred_element_type=jnp.float32,
    )
    return grad_attended.astype(jnp.bfloat16)


def mlp_pre(normed_b, w_fc):
    return jnp.einsum(
        "srd,df->srf",
        lax.all_gather(normed_b, "tensor", axis=0, tiled=True),
        w_fc,
        preferred_element_type=jnp.float32,
    )


def mlp_out(hidden_b, w_proj):
    return lax.psum_scatter(
        jnp.einsum("srf,fd->srd", hidden_b, w_proj, preferred_element_type=jnp.float32).astype(
            jnp.bfloat16
        ),
        "tensor",
        scatter_dimension=0,
        tiled=True,
    ).astype(jnp.float32)


def mlp_back(grad_mlp, pre_act, w_fc, w_proj):
    grad_hidden = jnp.einsum(
        "srd,fd->srf",
        lax.all_gather(grad_mlp, "tensor", axis=0, tiled=True),
        w_proj,
        preferred_element_type=jnp.float32,
    )
    activated, slope = jax.vjp(gelu_tanh, pre_act)
    grad_pre = slope(grad_hidden)[0].astype(jnp.bfloat16)
    return lax.psum_scatter(
        jnp.einsum("srf,df->srd", grad_pre, w_fc, preferred_element_type=jnp.float32).astype(
            jnp.bfloat16
        ),
        "tensor",
        scatter_dimension=0,
        tiled=True,
    ).astype(jnp.float32)


def forward_layer_step(layer_input_rows, segment_row_span, fixed_weights, adapter_pair):
    norm_rows = normalize(layer_input_rows, fixed_weights[0])[0].astype(jnp.bfloat16)
    stacked_weights = projected_rows(
        lax.all_gather(norm_rows, "tensor", axis=0, tiled=True), fixed_weights[1], adapter_pair
    )[0]
    attended_b = attend_all(stacked_weights, segment_row_span)[0]
    middle = layer_input_rows + attention_project(attended_b, fixed_weights[2])
    normed_mlp = normalize(middle, fixed_weights[3])[0].astype(jnp.bfloat16)
    pre_act = mlp_pre(normed_mlp, fixed_weights[4])
    hidden_b = gelu_tanh(pre_act).astype(jnp.bfloat16)
    return middle + mlp_out(hidden_b, fixed_weights[5])


def backward_layer_step(
    layer_input_rows, segment_row_span, upstream_gradient, fixed_weights, adapter_pair
):
    gain_a, joint_projection_weight, w_out, gain_m, w_fc, w_proj = fixed_weights
    query_down_factor, query_up_factor, value_down_factor, value_up_factor = adapter_pair
    factor = 32.0 / query_down_factor.shape[-1]
    norm_rows, unit_first, inverse_first = normalize(layer_input_rows, gain_a)
    collected_rows = lax.all_gather(norm_rows.astype(jnp.bfloat16), "tensor", axis=0, tiled=True)
    stacked_weights, narrow_query_rows, narrow_value_rows = projected_rows(
        collected_rows, joint_projection_weight, adapter_pair
    )
    length, row_count = (collected_rows.shape[0], collected_rows.shape[1])
    attended_b, log_sums, head_views = attend_all(stacked_weights, segment_row_span)
    queries, keys_all, values_all = head_views
    middle = layer_input_rows + attention_project(attended_b, w_out)
    normed_mlp, unit_second, inverse_second = normalize(middle, gain_m)
    pre_act = mlp_pre(normed_mlp.astype(jnp.bfloat16), w_fc)
    grad_norm_mlp = mlp_back(upstream_gradient.astype(jnp.bfloat16), pre_act, w_fc, w_proj)
    grad_middle = upstream_gradient + normalize_back(
        grad_norm_mlp, unit_second, inverse_second, gain_m
    )
    grad_attended = attention_grad_heads(grad_middle.astype(jnp.bfloat16), w_out)
    grad_heads = grad_attended.reshape(queries.shape)
    grad_queries, grad_keys, grad_values = attention_backward(
        queries, keys_all, values_all, segment_row_span, log_sums, grad_heads
    )
    grad_stack = (
        jnp.stack([grad_queries, grad_keys, grad_values], axis=2)
        .astype(jnp.bfloat16)
        .reshape(length, row_count, 3, -1)
    )
    grad_query_rows = grad_stack[:, :, 0]
    grad_value_rows = grad_stack[:, :, 2]
    thin_grad_query = factor * jnp.einsum(
        "srf,kf->srk", grad_query_rows, query_up_factor, preferred_element_type=jnp.float32
    )
    thin_grad_value = factor * jnp.einsum(
        "srf,kf->srk", grad_value_rows, value_up_factor, preferred_element_type=jnp.float32
    )
    grad_bq = factor * jnp.einsum(
        "srk,srf->kf", narrow_query_rows, grad_query_rows.astype(jnp.float32), precision=PRECISE
    )
    grad_bv = factor * jnp.einsum(
        "srk,srf->kf", narrow_value_rows, grad_value_rows.astype(jnp.float32), precision=PRECISE
    )
    gathered_wide = collected_rows.astype(jnp.float32)
    grad_aq = jnp.einsum("srd,srk->dk", gathered_wide, thin_grad_query, precision=PRECISE)
    grad_av = jnp.einsum("srd,srk->dk", gathered_wide, thin_grad_value, precision=PRECISE)
    a_query_wide = query_down_factor.astype(jnp.float32)
    a_value_wide = value_down_factor.astype(jnp.float32)
    term = jnp.einsum(
        "srcf,dcf->srd", grad_stack, joint_projection_weight, preferred_element_type=jnp.float32
    )
    term = term + jnp.einsum("srk,dk->srd", thin_grad_query, a_query_wide, precision=PRECISE)
    grad_norm_attn = lax.psum_scatter(
        (term + jnp.einsum("srk,dk->srd", thin_grad_value, a_value_wide, precision=PRECISE)).astype(
            jnp.bfloat16
        ),
        "tensor",
        scatter_dimension=0,
        tiled=True,
    ).astype(jnp.float32)
    layer_output_rows = grad_middle + normalize_back(
        grad_norm_attn, unit_first, inverse_first, gain_a
    )
    return (layer_output_rows, (grad_aq, grad_bq, grad_av, grad_bv))


def body(
    inputs,
    segments,
    cotangent,
    gain_attn,
    joint_projection_weight,
    query_down_factor,
    query_up_factor,
    value_down_factor,
    value_up_factor,
    w_out,
    gain_mlp,
    w_fc,
    w_proj,
):
    fixed_weights = (
        gain_attn[0],
        joint_projection_weight[0],
        w_out[0],
        gain_mlp[0],
        w_fc[0],
        w_proj[0],
    )
    adapter_pair = (
        query_down_factor[0],
        query_up_factor[0],
        value_down_factor[0],
        value_up_factor[0],
    )
    sections = lax.axis_size("section")
    section_index = lax.axis_index("section")
    is_first = section_index == 0
    is_last = section_index == sections - 1
    rows_mb = inputs.shape[1] // MICRO
    ticks = MICRO + sections - 1
    block_shape = (inputs.shape[0], rows_mb, inputs.shape[2])
    activations = jnp.zeros_like(inputs)
    kept_inputs = jnp.zeros((MICRO,) + block_shape, jnp.bfloat16)
    arriving = jnp.zeros(block_shape, jnp.bfloat16)
    for tick_index in range(ticks):
        own_index = min(tick_index, MICRO - 1)
        mb_slot = tick_index - section_index
        is_valid = (mb_slot >= 0) & (mb_slot < MICRO)
        mb_slot = jnp.clip(mb_slot, 0, MICRO - 1)
        fresh = lax.slice_in_dim(inputs, own_index * rows_mb, (own_index + 1) * rows_mb, axis=1)
        layer_input_rows = jnp.where(is_first, fresh, arriving)
        segment_row_span = lax.dynamic_slice_in_dim(segments, mb_slot * rows_mb, rows_mb, 0)
        layer_output_rows = forward_layer_step(
            layer_input_rows.astype(jnp.float32), segment_row_span, fixed_weights, adapter_pair
        ).astype(jnp.bfloat16)
        activations = jnp.where(
            is_valid,
            lax.dynamic_update_slice_in_dim(activations, layer_output_rows, mb_slot * rows_mb, 1),
            activations,
        )
        kept_inputs = jnp.where(
            is_valid, kept_inputs.at[mb_slot].set(layer_input_rows), kept_inputs
        )
        if tick_index < ticks - 1:
            arriving = passed_along(layer_output_rows, "section", 1)
    input_grads = jnp.zeros_like(inputs)
    gradient_totals = tuple(
        (jnp.zeros(factor_tensor.shape, jnp.float32) for factor_tensor in adapter_pair)
    )
    arriving = jnp.zeros(block_shape, jnp.bfloat16)
    for tick_index in range(ticks):
        own_index = min(tick_index, MICRO - 1)
        mb_slot = tick_index - (sections - 1 - section_index)
        is_valid = (mb_slot >= 0) & (mb_slot < MICRO)
        mb_slot = jnp.clip(mb_slot, 0, MICRO - 1)
        given = lax.slice_in_dim(cotangent, own_index * rows_mb, (own_index + 1) * rows_mb, axis=1)
        upstream_gradient = jnp.where(is_last, given, arriving).astype(jnp.float32)
        layer_input_rows = kept_inputs[mb_slot].astype(jnp.float32)
        segment_row_span = lax.dynamic_slice_in_dim(segments, mb_slot * rows_mb, rows_mb, 0)
        layer_output_rows, row_pieces = backward_layer_step(
            layer_input_rows, segment_row_span, upstream_gradient, fixed_weights, adapter_pair
        )
        leaving_b = layer_output_rows.astype(jnp.bfloat16)
        input_grads = jnp.where(
            is_valid,
            lax.dynamic_update_slice_in_dim(input_grads, leaving_b, mb_slot * rows_mb, 1),
            input_grads,
        )
        gradient_totals = tuple(
            (
                running + jnp.where(is_valid, piece_grad, 0.0)
                for running, piece_grad in zip(gradient_totals, row_pieces)
            )
        )
        if tick_index < ticks - 1:
            arriving = passed_along(leaving_b, "section", -1)
    adapter_rank = adapter_pair[1].shape[0]
    model_width = inputs.shape[2]
    column_total = adapter_pair[1].shape[1]
    offset = lax.axis_index("tensor") * column_total
    full_query = lax.dynamic_update_slice_in_dim(
        jnp.zeros((adapter_rank, model_width), jnp.float32), gradient_totals[1], offset, 1
    )
    full_value = lax.dynamic_update_slice_in_dim(
        jnp.zeros((adapter_rank, model_width), jnp.float32), gradient_totals[3], offset, 1
    )
    summed = lax.psum(
        (gradient_totals[0], full_query, gradient_totals[2], full_value), ("dp", "tensor")
    )
    return (
        activations[None],
        input_grads[None],
        summed[0][None],
        summed[1][None],
        summed[2][None],
        summed[3][None],
    )


REACH = 512
BF16 = jnp.bfloat16
F32 = jnp.float32
MESH = pl.DeviceIdType.MESH


def dot_nn(a, b):
    return lax.dot_general(a, b, (((1,), (0,)), ((), ())), preferred_element_type=F32)


def dot_nt(a, b):
    return lax.dot_general(a, b, (((1,), (1,)), ((), ())), preferred_element_type=F32)


def dot_tn(a, b):
    return lax.dot_general(a, b, (((0,), (0,)), ((), ())), preferred_element_type=F32)


def norm_stats(rows):
    middle = jnp.mean(rows, axis=-1, keepdims=True)
    centred = rows - middle
    inverse = lax.rsqrt(jnp.mean(centred * centred, axis=-1, keepdims=True) + EPSILON)
    return centred * inverse, inverse


def gelu_slope(pre):
    square = pre * pre
    bent = jnp.tanh(TANH_SCALE * (pre + CUBIC_TERM * square * pre))
    return 0.5 * (1.0 + bent) + (0.5 * TANH_SCALE) * pre * (1.0 - bent * bent) * (
        1.0 + (3.0 * CUBIC_TERM) * square
    )


def key_span(i, block):
    return max(0, i - REACH // block) * block, (i + 1) * block


def allowed_keys(i, block, seg_col_ref, seg_row_ref):
    low, high = key_span(i, block)
    seg_k = seg_col_ref[low:high, :]
    seg_q = seg_row_ref[:, i * block : (i + 1) * block]
    places_k = low + lax.broadcasted_iota(jnp.int32, (high - low, block), 0)
    places_q = i * block + lax.broadcasted_iota(jnp.int32, (high - low, block), 1)
    return (seg_q == seg_k) & (places_k <= places_q)


def head_lanes(rows, h):
    lane = lax.broadcasted_iota(jnp.int32, (rows, 128), 1)
    return (lane < HEAD_DIM) if h == 0 else (lane >= HEAD_DIM)


def both_halves(ref, *index):
    return jnp.concatenate([ref[(*index, 0)], ref[(*index, 1)]], axis=1)


class Wires:
    def __init__(self, send, recv):
        self.send, self.recv, self.count, self.sent = send, recv, 0, []

    def copy(self, source, target, where):
        k = self.count
        self.count += 1
        made = pltpu.make_async_remote_copy(
            src_ref=source,
            dst_ref=target,
            send_sem=self.send.at[k],
            recv_sem=self.recv.at[k],
            device_id=where,
            device_id_type=MESH,
        )
        self.sent.append(made)
        return made

    def forget(self, copy):
        self.sent = [one for one in self.sent if one is not copy]


class Totals:
    def __init__(self, wires, layer, out_ref, in_ref, hops):
        self.out_ref, self.in_ref, self.layer, self.at = out_ref, in_ref, layer, 0
        self.hops = [
            wires.copy(out_ref.at[layer, k], in_ref.at[layer, k], peer)
            for k, peer in enumerate(hops)
        ]
        self.wires = wires
        self.hops[0].start()

    def step(self):
        k, layer = self.at, self.layer
        self.hops[k].wait_recv()
        summed = self.out_ref[layer, k] + self.in_ref[layer, k]
        self.at = k + 1
        if self.at < len(self.hops):
            self.out_ref[layer, self.at] = summed
            self.hops[self.at].start()
        else:
            self.hops[0].wait_send()
            self.wires.forget(self.hops[0])
            self.out_ref[layer, 0] = summed

    def finish(self):
        while self.at < len(self.hops):
            self.step()


WIRES = 96


def step_kernel(
    block,
    model,
    planes,
    x_rows,
    cot_rows,
    seg_cols,
    seg_rows,
    gain_a,
    gain_m,
    downs_t,
    up_q,
    up_v,
    wq,
    wo,
    fc,
    proj,
    act_out,
    grad_out,
    sums_out,
    act,
    grad,
    xb,
    cb,
    seg_col,
    seg_row,
    sm,
    up,
    pad,
    wq_all,
    up_all,
    wo_all,
    ff,
    rows,
    thin,
    qkv,
    o_out,
    o_in,
    middle,
    norm2,
    pre,
    part_out,
    part_in,
    own_sum,
    do_in,
    dqkv,
    dk_acc,
    dv_acc,
    c_out,
    c_in,
    y_out,
    y_in,
    down_sums,
    up_sums,
    total_out,
    total_in,
    wire_send,
    wire_recv,
    row_send,
    row_recv,
    wq_send,
    wq_recv,
    wq_half,
    local_sem,
    o_send,
    o_recv,
    place_send,
    place_recv,
):
    c = lax.axis_index("section")
    z = lax.axis_index("dp")
    t = lax.axis_index("tensor")
    y, x = lax.div(t, 2), lax.rem(t, 2)
    over_x, over_y = 2 * y + (1 - x), 2 * (1 - y) + x
    mine, twin = 2 * y + c, 2 * y + (1 - c)
    far, far_twin = 2 * (1 - y) + c, 2 * (1 - y) + (1 - c)
    to_c, to_x, to_y = {"section": 1 - c}, {"tensor": over_x}, {"tensor": over_y}
    to_xc = {"section": 1 - c, "tensor": over_x}
    to_yc = {"section": 1 - c, "tensor": over_y}
    to_zs = []
    bit = 1
    while bit < planes:
        up_bit = lax.rem(lax.div(z, bit), 2)
        to_zs.append({"dp": z + bit - 2 * bit * up_bit})
        bit *= 2
    to_z = to_zs[0]
    odd = lax.rem(z, 2)
    here = c == x
    wires = Wires(wire_send, wire_recv)
    width = wq.shape[2]
    factor = 8.0

    barrier = pltpu.get_barrier_semaphore()
    peers = [to_c, to_x, to_y, to_xc, to_yc, *to_zs]
    for peer in peers:
        pl.semaphore_signal(barrier, inc=1, device_id=peer, device_id_type=MESH)
    pl.semaphore_wait(barrier, len(peers))

    def part(which, count):
        first = odd if which == 0 else 1 - odd
        return pl.ds(pl.multiple_of(first * (count // 2), count // 2), count // 2)

    def row_copy(source, target, k):
        return pltpu.make_async_remote_copy(
            src_ref=source,
            dst_ref=target,
            send_sem=row_send.at[k],
            recv_sem=row_recv.at[k],
            device_id=to_x,
            device_id_type=MESH,
        )

    x_copy = row_copy(x_rows.at[1 - x], xb, 0)

    @pl.when(here)
    def _():
        x_copy.start()
        pltpu.make_async_copy(x_rows.at[x], xb, row_recv.at[0]).start()

    pad[...] = jnp.zeros_like(pad)
    pad[0:4] = up_q[...].astype(F32)
    up[0] = pad[...].astype(BF16)
    pad[0:4] = jnp.zeros((4, width), F32)
    pad[4:8] = up_v[...].astype(F32)
    up[1] = pad[...].astype(BF16)

    def wq_twin():
        return [
            pltpu.make_async_remote_copy(
                src_ref=source,
                dst_ref=target.at[c],
                send_sem=wq_send.at[0, j],
                recv_sem=wq_recv.at[c, j],
                device_id=to_c,
                device_id_type=MESH,
            )
            for j, (source, target) in enumerate(((wq, wq_all), (up, up_all)))
        ]

    def wq_over_x():
        cut = part(0, model)
        where = {"section": x, "tensor": over_x}
        made = [
            pltpu.make_async_remote_copy(
                src_ref=wq.at[k, cut],
                dst_ref=wq_all.at[c, k, cut],
                send_sem=wq_send.at[1, k],
                recv_sem=wq_half.at[c, 0, k],
                device_id=where,
                device_id_type=MESH,
            )
            for k in range(3)
        ]
        made.append(
            pltpu.make_async_remote_copy(
                src_ref=up,
                dst_ref=up_all.at[c],
                send_sem=wq_send.at[0, 2],
                recv_sem=wq_recv.at[c, 1],
                device_id=where,
                device_id_type=MESH,
            )
        )
        return made

    def wq_over_z(layer):
        cut = part(0, model)
        return [
            pltpu.make_async_remote_copy(
                src_ref=wq_all.at[layer, k, cut],
                dst_ref=wq_all.at[layer, k, cut],
                send_sem=wq_send.at[2 + layer, k],
                recv_sem=wq_half.at[layer, 1, k],
                device_id=to_z,
                device_id_type=MESH,
            )
            for k in range(3)
        ]

    def wq_local(layer):
        return [
            pltpu.make_async_copy(source, target.at[layer], wq_recv.at[layer, j])
            for j, (source, target) in enumerate(((wq, wq_all), (up, up_all)))
        ]

    def send_wq_far(layer, pieces):
        @pl.when(c == layer)
        def _():
            copies = wq_over_x()
            for k in pieces:
                copies[k].start()

    def send_wq_near():
        @pl.when(here)
        def _():
            for copy in wq_local(c):
                copy.start()

        @pl.when(jnp.logical_not(here))
        def _():
            for copy in wq_twin():
                copy.start()

    def half_wait(layer, which, k):
        cut = part(which, model)
        pltpu.make_async_copy(
            wq.at[k, cut], wq_all.at[layer, k, cut], wq_half.at[layer, which, k]
        ).wait()

    def pass_wq(layer):
        @pl.when(jnp.logical_not(here))
        def _():
            for k, copy in enumerate(wq_over_z(layer)):
                half_wait(layer, 0, k)
                copy.start()

    def arrived_wq(layer):
        whole, small = wq_local(layer)
        small.wait()
        pl.when(here)(whole.wait)

        @pl.when(jnp.logical_not(here))
        def _():
            for k in range(3):
                half_wait(layer, 1, k)

    def sent_wq():
        for copy in wq_over_x():
            copy.wait_send()

        @pl.when(jnp.logical_not(here))
        def _():
            for copy in wq_twin():
                copy.wait_send()
            for layer in range(2):
                for copy in wq_over_z(layer):
                    copy.wait_send()

    send_wq_far(0, (3, 0, 1, 2))
    pl.when(c == 0)(send_wq_near)

    sm[c, 0:1] = gain_a[...]
    sm[c, 8:9] = gain_m[...]
    sm[c, 16:24] = downs_t[...].astype(F32)
    sm[c, 24:32] = jnp.zeros((8, model), F32)
    small_copy = wires.copy(sm.at[c], sm.at[c], to_c)
    small_copy.start()
    seg_row[...] = seg_rows[pl.ds(x, 1), :]
    seg_col[...] = jnp.where(x == 0, seg_cols[:, 0:1], seg_cols[:, 1:2])

    locals_ = [
        pltpu.make_async_copy(source, target, local_sem.at[k])
        for k, (source, target) in enumerate(
            ((fc, ff.at[c, 0, 0]), (proj, ff.at[c, 1, 0]), (wo, wo_all.at[c, t]))
        )
    ]
    piece = model // 4

    def ff_rows(p, which):
        first = odd if which == 0 else 1 - odd
        return pl.ds(pl.multiple_of(first * (model // 2) + (p % 2) * piece, piece), piece)

    def ff_same(p, which, where):
        at = ff.at[c, p // 2, 1, ff_rows(p, which)]
        return wires.copy(at, at, where)

    ff_twin = [wires.copy(one, ff.at[c, k, 0], to_c) for k, one in enumerate((fc, proj))]
    ff_x = [
        wires.copy(
            (fc, proj)[p // 2].at[ff_rows(p, 0)], ff.at[c, p // 2, 1, ff_rows(p, 0)], to_x
        )
        for p in range(4)
    ]
    ff_z = [ff_same(p, 0, to_z) for p in range(4)]
    ff_c = [[ff_same(p, which, to_c) for which in range(2)] for p in range(4)]

    def start_ff(layer):
        @pl.when(c == layer)
        def _():
            for copy in ff_x:
                copy.start()

    def pass_ff_x(layer, p):
        @pl.when(c == layer)
        def _():
            ff_x[p].wait_recv()
            ff_z[p].start()
            ff_c[p][0].start()

    def pass_ff_z(layer, p):
        @pl.when(c == layer)
        def _():
            ff_z[p].wait_recv()
            ff_c[p][1].start()

    def arrived_ff(layer):
        @pl.when(c != layer)
        def _():
            for pair in ff_c:
                for copy in pair:
                    copy.wait_recv()

    corner = 2 * (1 - y) + (1 - x)
    wo_cut = part(0, width)
    quart = width // 4
    wo_low = pl.ds(pl.multiple_of(odd * (width // 2), quart), quart)
    wo_high = pl.ds(pl.multiple_of(odd * (width // 2) + quart, quart), quart)

    def wo_same(q, cut, where):
        if cut is None:
            return wires.copy(wo_all.at[c, q], wo_all.at[c, q], where)
        return wires.copy(wo_all.at[c, q, cut], wo_all.at[c, q, cut], where)

    wo_twin = wires.copy(wo, wo_all.at[c, t], to_c)
    wo_x = wires.copy(wo.at[wo_cut], wo_all.at[c, t, wo_cut], to_x)
    wo_y = wires.copy(wo.at[wo_cut], wo_all.at[c, t, wo_cut], to_y)
    wo_dy = wo_same(over_x, wo_low, to_y)
    wo_dx = wo_same(over_y, wo_high, to_x)
    wo_z = [wo_same(q, wo_cut, to_z) for q in (over_x, over_y, corner)]
    wo_c = [wo_same(q, None, to_c) for q in (over_x, over_y, corner)]

    def start_wo_x(layer):
        pl.when(c == layer)(wo_x.start)

    def start_wo_y(layer):
        pl.when(c == layer)(wo_y.start)

    def pass_wo(layer, stage):
        @pl.when(c == layer)
        def _():
            if stage == 0:
                wo_x.wait_recv()
                wo_dy.start()
                wo_z[0].start()
                wo_y.wait_recv()
                wo_dx.start()
                wo_z[1].start()
            if stage == 1:
                wo_dy.wait_recv()
                wo_dx.wait_recv()
                wo_z[2].start()
            if stage == 2:
                for came, onward in zip(wo_z, wo_c):
                    came.wait_recv()
                    onward.start()

    def arrived_wo(layer):
        @pl.when(c == layer)
        def _():
            locals_[2].wait()

        @pl.when(c != layer)
        def _():
            wo_twin.wait_recv()
            for copy in wo_c:
                copy.wait_recv()

    for copy in locals_:
        copy.start()
    for copy in ff_twin + [wo_twin]:
        copy.start()
    start_wo_x(0)
    start_ff(0)

    def place_copy(kind, layer, source, target):
        return pltpu.make_async_remote_copy(
            src_ref=source,
            dst_ref=target.at[x],
            send_sem=place_send.at[kind, layer],
            recv_sem=place_recv.at[kind, x],
            device_id={"section": layer, "tensor": mine},
            device_id_type=MESH,
        )

    def place(kind, layer, source, target):
        stays = jnp.logical_and(here, c == layer)

        @pl.when(stays)
        def _():
            target[x] = source[...]

        @pl.when(jnp.logical_not(stays))
        def _():
            place_copy(kind, layer, source, target).start()

    def placed(kind, source, target):
        for layer in range(2):
            stays = jnp.logical_and(here, c == layer)

            @pl.when(jnp.logical_not(stays))
            def _():
                place_copy(kind, layer, source.at[layer], target).wait_send()

        for slot in range(2):
            came = jnp.logical_not(jnp.logical_and(here, x == slot))

            @pl.when(came)
            def _():
                pltpu.make_async_copy(
                    source.at[0], target.at[slot], place_recv.at[kind, slot]
                ).wait()

    def qkv_block(layer, b):
        normed = rows[layer, b]
        down = sm[layer, 16:32, :].astype(BF16)
        low = dot_nt(normed, down)
        low_b = low.astype(BF16)
        thin[layer, b] = low_b
        at = pl.ds(pl.multiple_of(b * block, block), block)
        for k in range(3):
            made = dot_nn(normed, wq_all[layer, k])
            if k == 0:
                made = made + factor * dot_nn(low_b, up_all[layer, 0])
            if k == 2:
                made = made + factor * dot_nn(low_b, up_all[layer, 1])
            made = made.astype(BF16)
            qkv[layer, k, 0, at, :] = made[:, :128]
            qkv[layer, k, 1, at, :] = made[:, 128:]

    def attend(layer, i):
        low, high = key_span(i, block)
        at = slice(i * block, (i + 1) * block)
        allowed = allowed_keys(i, block, seg_col, seg_row)

        def one_pair(pair, carry):
            queries = qkv[layer, 0, pair, at, :] * BF16(HEAD_DIM**-0.5)
            keys = qkv[layer, 1, pair, low:high, :]
            values = qkv[layer, 2, pair, low:high, :]
            parts = []
            for h in range(2):
                picked = jnp.where(head_lanes(block, h), queries, BF16(0))
                scores = jnp.where(allowed, dot_nt(keys, picked), MASKED)
                exponent = jnp.exp(scores - jnp.max(scores, axis=0, keepdims=True))
                total = jnp.sum(exponent, axis=0, keepdims=True)
                made = dot_tn(values, exponent.astype(BF16))
                parts.append(made[h * HEAD_DIM : (h + 1) * HEAD_DIM] / total)
            o_out[i, pair] = jnp.concatenate(parts, axis=0).T.astype(BF16)
            return carry

        lax.fori_loop(0, 2, one_pair, 0)

    def exchange_piece(i, target, phase):
        return pltpu.make_async_remote_copy(
            src_ref=o_out.at[i],
            dst_ref=target.at[mine],
            send_sem=o_send.at[i],
            recv_sem=o_recv.at[phase, mine],
            device_id={"section": i % 2, "tensor": 2 * (i // 2) + x},
            device_id_type=MESH,
        )

    def send_piece(i, target, phase):
        @pl.when(mine == i)
        def _():
            target[mine] = o_out[i]

        @pl.when(mine != i)
        def _():
            exchange_piece(i, target, phase).start()

    def wait_pieces(target, phase):
        for i in range(4):

            @pl.when(mine != i)
            def _():
                exchange_piece(i, target, phase).wait_send()
                pltpu.make_async_copy(o_out.at[i], target.at[i], o_recv.at[phase, i]).wait()

    def hidden_half(layer, who, source, q):
        total = None
        for cut in range(2):
            lanes = slice(cut * model // 2, (cut + 1) * model // 2)
            made = dot_nn(source, ff[layer, 0, q, :, lanes])
            pre[layer, who, q, :, lanes] = made.astype(BF16)
            term = dot_nn(gelu_tanh(made).astype(BF16), ff[layer, 1, q, lanes, :])
            total = term if total is None else total + term
        return total

    def hidden_back(layer, who, upstream, q):
        total = None
        for cut in range(2):
            lanes = slice(cut * model // 2, (cut + 1) * model // 2)
            grad_hidden = dot_nt(upstream, ff[layer, 1, q, lanes, :])
            slope = gelu_slope(pre[layer, who, q, :, lanes].astype(F32))
            term = dot_nt((grad_hidden * slope).astype(BF16), ff[layer, 0, q, :, lanes])
            total = term if total is None else total + term
        return total

    pltpu.make_async_copy(x_rows.at[x], xb, row_recv.at[0]).wait()
    small_copy.wait_recv()
    cot_x = row_copy(cot_rows.at[1 - x], cb.at[0], 1)
    cot_local = pltpu.make_async_copy(cot_rows.at[x], cb.at[0], row_recv.at[1])
    cot_y = wires.copy(cb.at[0], cb.at[1], to_y)

    for layer in range(2):
        source = xb if layer == 0 else act.at[0]
        unit, _ = norm_stats(source[...].astype(F32))
        rows[layer, mine] = (unit * sm[layer, 0:1, :]).astype(BF16)
        row_y = wires.copy(rows.at[layer, mine], rows.at[layer, mine], to_y)
        row_c = wires.copy(rows.at[layer, mine], rows.at[layer, mine], to_c)
        row_yc = wires.copy(rows.at[layer, far], rows.at[layer, far], to_c)
        row_y.start()
        row_c.start()
        if layer == 0:
            pass_wq(0)
        else:
            pass_wo(1, 1)
            pass_ff_x(1, 2)
        arrived_wq(layer)
        qkv_block(layer, mine)
        if layer == 1:
            pass_ff_x(1, 3)
            pass_wo(1, 2)
            place(0, 0, act.at[0], act_out)
        row_c.wait_recv()
        qkv_block(layer, twin)
        row_y.wait_recv()
        row_yc.start()
        if layer == 0:
            start_wo_y(0)
        else:
            cot_local.wait()
            cot_y.start()
        qkv_block(layer, far)
        row_yc.wait_recv()
        qkv_block(layer, far_twin)
        if layer == 0:
            pass_ff_x(0, 0)
        for i in range(4):
            attend(layer, i)
            send_piece(i, o_in, layer)
            if layer == 0 and i == 0:
                pass_wo(0, 0)
            if layer == 0 and i == 2:
                pass_wo(0, 1)
                pass_ff_x(0, 1)
            if layer == 0 and i == 3:
                pass_wo(0, 2)
            if layer == 1 and i >= 2:
                pass_ff_z(1, i - 2)
        arrived_wo(layer)
        wait_pieces(o_in, layer)
        if layer == 0:
            pass_ff_x(0, 2)
        else:
            pass_ff_z(1, 2)
        stream = source[...].astype(F32)
        for q in range(4):
            stream = stream + dot_nn(both_halves(o_in, q), wo_all[layer, q])
        middle[layer] = stream
        unit, _ = norm_stats(stream)
        norm2[0] = (unit * sm[layer, 8:9, :]).astype(BF16)
        norm_y = wires.copy(norm2.at[0], norm2.at[1], to_y)
        norm_y.start()
        if layer == 0:
            for copy in locals_[:2]:
                copy.wait()
            for copy in ff_twin:
                copy.wait_recv()
            pass_ff_z(0, 0)
            pass_ff_x(0, 3)
            pl.when(c == 1)(send_wq_near)
            send_wq_far(1, (3, 0, 1, 2))
            start_wo_x(1)
            start_wo_y(1)
            start_ff(1)
            pass_ff_z(0, 1)
        else:
            pass_ff_z(1, 3)
        own_sum[...] = hidden_half(layer, 0, norm2[0], 0)
        if layer == 0:
            pass_ff_z(0, 2)
            pass_ff_z(0, 3)
            pass_wq(1)
        arrived_ff(layer)
        own_sum[...] += hidden_half(layer, 0, norm2[0], 1)
        if layer == 1:
            grad[0] = own_sum[...].astype(BF16)
            own_sum[...] = hidden_back(1, 0, cb[0], 0) + hidden_back(1, 0, cb[0], 1)
        norm_y.wait_recv()
        away = hidden_half(layer, 1, norm2[1], 0) + hidden_half(layer, 1, norm2[1], 1)
        if layer == 1:
            y_out[...] = away.astype(BF16)
            cot_y.wait_recv()
            away = hidden_back(1, 1, cb[1], 0) + hidden_back(1, 1, cb[1], 1)
        part_out[...] = away.astype(BF16)
        part_y = wires.copy(part_out, part_in.at[layer], to_y)
        part_y.start()
        if layer == 0:
            stream = middle[layer] + own_sum[...]
            pass_wo(1, 0)
            pass_ff_x(1, 0)
            pass_ff_x(1, 1)

            @pl.when(here)
            def _():
                cot_x.start()
                cot_local.start()

            part_y.wait()
            wires.forget(part_y)
            norm_y.wait_send()
            wires.forget(norm_y)
            act[layer] = (stream + part_in[0].astype(F32)).astype(BF16)

    for layer in (1, 0):
        upstream = cb[0] if layer == 1 else grad[1]
        if layer == 0:
            up_y = wires.copy(grad.at[1], norm2.at[1], to_y)
            up_y.start()
            own_sum[...] = hidden_back(layer, 0, upstream, 0) + hidden_back(layer, 0, upstream, 1)
            up_y.wait_recv()
            totals.step()
            away = hidden_back(layer, 1, norm2[1], 0) + hidden_back(layer, 1, norm2[1], 1)
            part_out[...] = away.astype(BF16)
            part_y = wires.copy(part_out, part_in.at[1], to_y)
            part_y.start()
        unit, inverse = norm_stats(middle[layer])
        part_y.wait()
        wires.forget(part_y)
        if layer == 0:
            totals.step()
        grad_norm = own_sum[...] + part_in[1].astype(F32)
        grad_middle = upstream.astype(F32) + normalize_back(
            grad_norm, unit, inverse, sm[layer, 8:9, :]
        )
        own_sum[...] = grad_middle
        grad_b = grad_middle.astype(BF16)
        for q in range(4):
            made = dot_nt(grad_b, wo_all[layer, q]).astype(BF16)
            o_out[q, 0] = made[:, :128]
            o_out[q, 1] = made[:, 128:]
            send_piece(q, do_in, 2 + layer)
        if layer == 0:
            place(1, 1, grad.at[1], grad_out)
        else:
            late_y = wires.copy(y_out, part_in.at[0], to_y)
            late_y.start()
        wait_pieces(do_in, 2 + layer)
        if layer == 0:
            totals.step()

        def back_pair(pair, carry):
            dk_acc[...] = jnp.zeros_like(dk_acc)
            dv_acc[...] = jnp.zeros_like(dv_acc)
            for i in range(4):
                low, high = key_span(i, block)
                at = slice(i * block, (i + 1) * block)
                allowed = allowed_keys(i, block, seg_col, seg_row)
                queries = qkv[layer, 0, pair, at, :] * BF16(HEAD_DIM**-0.5)
                keys = qkv[layer, 1, pair, low:high, :]
                values = qkv[layer, 2, pair, low:high, :]
                grads = do_in[i, pair]
                parts = []
                for h in range(2):
                    lanes = head_lanes(block, h)
                    picked = jnp.where(lanes, queries, BF16(0))
                    given = jnp.where(lanes, grads, BF16(0))
                    scores = jnp.where(allowed, dot_nt(keys, picked), MASKED)
                    exponent = jnp.exp(scores - jnp.max(scores, axis=0, keepdims=True))
                    soft = exponent * (1.0 / jnp.sum(exponent, axis=0, keepdims=True))
                    weighted = soft * dot_nt(values, given)
                    grad_scores = (
                        weighted - soft * jnp.sum(weighted, axis=0, keepdims=True)
                    ).astype(BF16)
                    made = dot_tn(keys, grad_scores)
                    parts.append(made[h * HEAD_DIM : (h + 1) * HEAD_DIM])
                    dk_acc[low:high, :] += dot_nn(grad_scores, picked)
                    dv_acc[low:high, :] += dot_nn(soft.astype(BF16), given)
                dqkv[0, pair, at, :] = (
                    jnp.concatenate(parts, axis=0).T * HEAD_DIM**-0.5
                ).astype(BF16)
            dqkv[1, pair] = dk_acc[...].astype(BF16)
            dqkv[2, pair] = dv_acc[...].astype(BF16)
            return carry

        lax.fori_loop(0, 2, back_pair, 0)
        if layer == 1:
            late_y.wait()
            wires.forget(late_y)
            act[1] = (
                middle[1] + grad[0].astype(F32) + part_in[0].astype(F32)
            ).astype(BF16)
            place(0, 1, act.at[1], act_out)
        down = sm[layer, 16:32, :].astype(BF16)
        if layer == 0:
            totals.finish()

        def block_grad(b, first):
            at = pl.ds(pl.multiple_of(b * block, block), block)
            parts = [
                jnp.concatenate([dqkv[k, 0, at, :], dqkv[k, 1, at, :]], axis=1) for k in range(3)
            ]
            low = factor * (
                dot_nt(parts[0], up_all[layer, 0]) + dot_nt(parts[2], up_all[layer, 1])
            )
            low_b = low.astype(BF16)
            term = dot_nn(low_b, down)
            for k in range(3):
                term = term + dot_nt(parts[k], wq_all[layer, k])
            kept = thin[layer, b]
            to_down = dot_tn(low_b, rows[layer, b])
            to_up = [factor * dot_tn(kept, parts[0]), factor * dot_tn(kept, parts[2])]
            if first:
                down_sums[...] = to_down
                up_sums[0], up_sums[1] = to_up
            else:
                down_sums[...] += to_down
                up_sums[0] += to_up[0]
                up_sums[1] += to_up[1]
            return term

        c_far = wires.copy(c_out.at[0], c_in.at[0], to_c)
        c_near = wires.copy(c_out.at[1], c_in.at[1], to_c)
        y_far = wires.copy(y_out, y_in, to_y)
        c_out[0] = block_grad(far_twin, True).astype(BF16)
        c_far.start()
        term = block_grad(far, False)
        c_far.wait_recv()
        y_out[...] = (term + c_in[0].astype(F32)).astype(BF16)
        y_far.start()
        c_out[1] = block_grad(twin, False).astype(BF16)
        c_near.start()
        term = block_grad(mine, False)
        total_out[layer, 0, 0:8] = down_sums[0:8]
        total_out[layer, 0, 8:16] = jnp.zeros((8, model), F32)
        low_rows = lax.broadcasted_iota(jnp.int32, (8, width), 0) < 4
        total_out[
            layer, 0, 8:16, pl.ds(pl.multiple_of(mine * width, width), width)
        ] = jnp.where(low_rows, up_sums[0, 0:8], up_sums[1, 0:8])
        totals = Totals(wires, layer, total_out, total_in, [to_c, to_x, to_y, *to_zs])
        c_near.wait_recv()
        term = term + c_in[1].astype(F32)
        source = xb if layer == 0 else act.at[0]
        unit, inverse = norm_stats(source[...].astype(F32))
        if layer == 0:
            totals.step()
            totals.step()
        y_far.wait_recv()
        grad_norm = term + y_in[...].astype(F32)
        grad[layer] = (
            own_sum[...] + normalize_back(grad_norm, unit, inverse, sm[layer, 0:1, :])
        ).astype(BF16)
        for copy in (c_far, c_near, y_far):
            copy.wait_send()
            wires.forget(copy)

    @pl.when(here)
    def _():
        x_copy.wait_send()
        cot_x.wait_send()


    place(1, 0, grad.at[0], grad_out)
    totals.finish()
    sums_out[...] = jnp.where(c == 0, total_out[0, 0], total_out[1, 0])
    sent_wq()
    for copy in wires.sent:
        copy.wait_send()
    placed(0, act, act_out)
    placed(1, grad, grad_out)


def step_call(block, model, width, planes, operands):
    slots = 4 * block
    hops = 3 + (planes - 1).bit_length()
    in_vmem = pl.BlockSpec(memory_space=pltpu.VMEM)
    in_hbm = pl.BlockSpec(memory_space=pl.ANY)
    return pl.pallas_call(
        functools.partial(step_kernel, block, model, planes),
        out_shape=(
            jax.ShapeDtypeStruct((2, block, model), BF16),
            jax.ShapeDtypeStruct((2, block, model), BF16),
            jax.ShapeDtypeStruct((16, model), F32),
        ),
        in_specs=[in_hbm] * 2 + [in_vmem] * 7 + [in_hbm] * 4,
        out_specs=[in_vmem] * 3,
        scratch_shapes=[
            pltpu.VMEM((2, block, model), BF16),
            pltpu.VMEM((2, block, model), BF16),
            pltpu.VMEM((block, model), BF16),
            pltpu.VMEM((2, block, model), BF16),
            pltpu.VMEM((slots, 1), jnp.int32),
            pltpu.VMEM((1, slots), jnp.int32),
            pltpu.VMEM((2, 32, model), F32),
            pltpu.VMEM((2, 16, width), BF16),
            pltpu.VMEM((16, width), F32),
            pltpu.VMEM((2, 3, model, width), BF16),
            pltpu.VMEM((2, 2, 16, width), BF16),
            pltpu.VMEM((2, 4, width, model), BF16),
            pltpu.VMEM((2, 2, 2, model, model), BF16),
            pltpu.VMEM((2, 4, block, model), BF16),
            pltpu.VMEM((2, 4, block, 16), BF16),
            pltpu.VMEM((2, 3, 2, slots, 128), BF16),
            pltpu.VMEM((4, 2, block, 128), BF16),
            pltpu.VMEM((4, 2, block, 128), BF16),
            pltpu.VMEM((2, block, model), F32),
            pltpu.VMEM((2, block, model), BF16),
            pltpu.VMEM((2, 2, 2, block, model), BF16),
            pltpu.VMEM((block, model), BF16),
            pltpu.VMEM((2, block, model), BF16),
            pltpu.VMEM((block, model), F32),
            pltpu.VMEM((4, 2, block, 128), BF16),
            pltpu.VMEM((3, 2, slots, 128), BF16),
            pltpu.VMEM((slots, 128), F32),
            pltpu.VMEM((slots, 128), F32),
            pltpu.VMEM((2, block, model), BF16),
            pltpu.VMEM((2, block, model), BF16),
            pltpu.VMEM((block, model), BF16),
            pltpu.VMEM((block, model), BF16),
            pltpu.VMEM((16, model), F32),
            pltpu.VMEM((2, 16, width), F32),
            pltpu.VMEM((2, hops, 16, model), F32),
            pltpu.VMEM((2, hops, 16, model), F32),
            pltpu.SemaphoreType.DMA((WIRES,)),
            pltpu.SemaphoreType.DMA((WIRES,)),
            pltpu.SemaphoreType.DMA((3,)),
            pltpu.SemaphoreType.DMA((3,)),
            pltpu.SemaphoreType.DMA((4, 3)),
            pltpu.SemaphoreType.DMA((2, 2)),
            pltpu.SemaphoreType.DMA((2, 2, 3)),
            pltpu.SemaphoreType.DMA((3,)),
            pltpu.SemaphoreType.DMA((4,)),
            pltpu.SemaphoreType.DMA((4, 4)),
            pltpu.SemaphoreType.DMA((2, 2)),
            pltpu.SemaphoreType.DMA((2, 2)),
        ],
        compiler_params=pltpu.CompilerParams(
            collective_id=0, has_side_effects=True, vmem_limit_bytes=62 * 1024 * 1024
        ),
    )(*operands)


def fast_body(
    planes,
    inputs,
    segments,
    cotangent,
    gain_attn,
    joint_projection_weight,
    query_down_factor,
    query_up_factor,
    value_down_factor,
    value_up_factor,
    w_out,
    gain_mlp,
    w_fc,
    w_proj,
):
    block, _, model = inputs.shape
    width = joint_projection_weight.shape[3]
    rank = query_down_factor.shape[2]
    downs = jnp.concatenate([query_down_factor[0], value_down_factor[0]], axis=1)
    acts, grads, total = step_call(
        block,
        model,
        width,
        planes,
        (
            jnp.swapaxes(inputs, 0, 1),
            jnp.swapaxes(cotangent, 0, 1),
            segments.T,
            segments,
            gain_attn,
            gain_mlp,
            downs.T,
            query_up_factor[0],
            value_up_factor[0],
            jnp.swapaxes(joint_projection_weight[0], 0, 1),
            w_out[0],
            w_fc[0],
            w_proj[0],
        ),
    )
    return (
        jnp.swapaxes(acts, 0, 1)[None],
        jnp.swapaxes(grads, 0, 1)[None],
        total[:rank].T[None],
        total[2 * rank : 3 * rank][None],
        total[rank : 2 * rank].T[None],
        total[3 * rank :][None],
    )


def fits_fast(mesh, shapes):
    planes = mesh.shape["dp"]
    slots, rows_all, model = shapes[0]
    return (
        mesh.shape["section"] == 2
        and mesh.shape["tensor"] == 4
        and planes > 1
        and planes & (planes - 1) == 0
        and rows_all == 2 * planes
        and slots == 1024
        and model == 1024
        and shapes[4][3] == 1024
        and shapes[5][2] == 4
        and shapes[11][2] == 4096
    )


def solution(mesh):
    placed = (
        P("tensor", "dp", None),
        P("dp", None),
        P("tensor", "dp", None),
        P("section", None),
        P("section", None, None, "tensor"),
        P("section", None, None),
        P("section", None, "tensor"),
        P("section", None, None),
        P("section", None, "tensor"),
        P("section", "tensor", None),
        P("section", None),
        P("section", None, "tensor"),
        P("section", "tensor", None),
    )

    def mapped(picked):
        return jax.shard_map(
            picked,
            mesh=mesh,
            in_specs=placed,
            out_specs=(
                P("section", "tensor", "dp", None),
                P("section", "tensor", "dp", None),
                P("section", None, None),
                P("section", None, None),
                P("section", None, None),
                P("section", None, None),
            ),
            check_vma=False,
        )

    def choose(*args):
        if fits_fast(mesh, [a.shape for a in args]):
            return mapped(functools.partial(fast_body, mesh.shape["dp"]))(*args)
        return mapped(body)(*args)

    return choose
```

```python
import functools

import jax
import jax.numpy as jnp
from jax import lax
from jax.experimental import pallas as pl
from jax.experimental.pallas import tpu as pltpu
from jax.sharding import PartitionSpec as P

HEAD_DIM = 64
MICRO = 2


EPSILON = 1e-05
PRECISE = lax.Precision.HIGHEST
MASKED = -1000000000.0
CUBIC_TERM = 0.044715
TANH_SCALE = 0.7978845608028654


def passed_along(block, axis, distance):
    devices = range(lax.axis_size(axis))
    route = [(i - distance, i) for i in devices if i - distance in devices]
    return lax.ppermute(block, axis, route)


def gelu_tanh(value):
    return 0.5 * value * (1.0 + jnp.tanh(TANH_SCALE * (value + CUBIC_TERM * value * value * value)))


def normalize(residual_stream, gain):
    middle = jnp.mean(residual_stream, axis=-1, keepdims=True)
    centred = residual_stream - middle
    inverse = lax.rsqrt(jnp.mean(centred * centred, axis=-1, keepdims=True) + EPSILON)
    unit_rows = centred * inverse
    return (unit_rows * gain, unit_rows, inverse)


def normalize_back(grad_norm, unit_rows, inverse, gain):
    scaled = grad_norm * gain
    return inverse * (
        scaled
        - jnp.mean(scaled, axis=-1, keepdims=True)
        - unit_rows * jnp.mean(scaled * unit_rows, axis=-1, keepdims=True)
    )


def block_mask(segment_row_span, first_row, block):
    length = segment_row_span.shape[1]
    segment_part = lax.dynamic_slice_in_dim(segment_row_span, first_row, block, 1)
    query_places = first_row + jnp.arange(block)
    key_places = jnp.arange(length)
    same_doc = segment_part[:, :, None] == segment_row_span[:, None, :]
    return same_doc & (key_places[None, None, :] <= query_places[None, :, None])


def projected_rows(row_portion, joint_projection_weight, adapter_pair):
    query_down_factor, query_up_factor, value_down_factor, value_up_factor = adapter_pair
    factor = 32.0 / query_down_factor.shape[-1]
    joined = jnp.einsum(
        "srd,dcf->srcf", row_portion, joint_projection_weight, preferred_element_type=jnp.float32
    )
    narrow_query_rows = jnp.einsum(
        "srd,dk->srk", row_portion, query_down_factor, preferred_element_type=jnp.float32
    )
    narrow_value_rows = jnp.einsum(
        "srd,dk->srk", row_portion, value_down_factor, preferred_element_type=jnp.float32
    )
    queries = joined[:, :, 0] + factor * jnp.einsum(
        "srk,kf->srf", narrow_query_rows, query_up_factor.astype(jnp.float32), precision=PRECISE
    )
    values_all = joined[:, :, 2] + factor * jnp.einsum(
        "srk,kf->srf", narrow_value_rows, value_up_factor.astype(jnp.float32), precision=PRECISE
    )
    stacked_weights = jnp.stack([queries, joined[:, :, 1], values_all], axis=2).astype(jnp.bfloat16)
    return (stacked_weights, narrow_query_rows, narrow_value_rows)


def attention_forward(queries, keys_all, values_all, segment_row_span):
    length, row_count, head_count, width = queries.shape
    block = min(512, length)
    factor = width ** (-0.5)

    def one_block(block_index):
        first_row = block_index * block
        query_part = lax.dynamic_slice_in_dim(queries, first_row, block, 0)
        scores = (
            jnp.einsum("qrhe,krhe->rhqk", query_part, keys_all, preferred_element_type=jnp.float32)
            * factor
        )
        allowed = block_mask(segment_row_span, first_row, block)
        scores = jnp.where(allowed[:, None], scores, MASKED)
        row_max = jnp.max(scores, axis=-1, keepdims=True)
        exponent = jnp.exp(scores - row_max)
        total = jnp.sum(exponent, axis=-1, keepdims=True)
        weights_soft = (exponent / total).astype(jnp.bfloat16)
        attended = jnp.einsum(
            "rhqk,krhe->qrhe", weights_soft, values_all, preferred_element_type=jnp.float32
        )
        return (attended, (row_max + jnp.log(total))[..., 0])

    attended, log_sums = lax.map(one_block, jnp.arange(length // block))
    attended = attended.reshape(length, row_count, head_count, width)
    log_sums = jnp.moveaxis(log_sums, 0, 2).reshape(row_count, head_count, length)
    return (attended, log_sums)


def attention_backward(queries, keys_all, values_all, segment_row_span, log_sums, grad_heads):
    length = queries.shape[0]
    block = min(512, length)
    factor = queries.shape[-1] ** (-0.5)

    def one_block(carry, block_index):
        grad_keys, grad_values = carry
        first_row = block_index * block
        query_part = lax.dynamic_slice_in_dim(queries, first_row, block, 0)
        grad_part = lax.dynamic_slice_in_dim(grad_heads, first_row, block, 0)
        sums_part = lax.dynamic_slice_in_dim(log_sums, first_row, block, 2)
        scores = (
            jnp.einsum("qrhe,krhe->rhqk", query_part, keys_all, preferred_element_type=jnp.float32)
            * factor
        )
        allowed = block_mask(segment_row_span, first_row, block)
        scores = jnp.where(allowed[:, None], scores, MASKED)
        weights_soft = jnp.exp(scores - sums_part[..., None])
        grad_soft = jnp.einsum(
            "qrhe,krhe->rhqk", grad_part, values_all, preferred_element_type=jnp.float32
        )
        grad_scores = weights_soft * (
            grad_soft - jnp.sum(weights_soft * grad_soft, axis=-1, keepdims=True)
        )
        grad_scores = grad_scores.astype(jnp.bfloat16)
        grad_query = (
            jnp.einsum("rhqk,krhe->qrhe", grad_scores, keys_all, preferred_element_type=jnp.float32)
            * factor
        )
        grad_keys = (
            grad_keys
            + jnp.einsum(
                "rhqk,qrhe->krhe", grad_scores, query_part, preferred_element_type=jnp.float32
            )
            * factor
        )
        grad_values = grad_values + jnp.einsum(
            "rhqk,qrhe->krhe",
            weights_soft.astype(jnp.bfloat16),
            grad_part,
            preferred_element_type=jnp.float32,
        )
        return ((grad_keys, grad_values), grad_query)

    start_state = (jnp.zeros(keys_all.shape, jnp.float32), jnp.zeros(values_all.shape, jnp.float32))
    (grad_keys, grad_values), grad_blocks = lax.scan(
        one_block, start_state, jnp.arange(length // block)
    )
    return (grad_blocks.reshape(queries.shape), grad_keys, grad_values)


def attend_all(stacked_weights, segment_row_span):
    length, row_count = (stacked_weights.shape[0], stacked_weights.shape[1])
    head_view = stacked_weights.reshape(length, row_count, 3, -1, HEAD_DIM)
    queries, keys_all, values_all = (head_view[:, :, 0], head_view[:, :, 1], head_view[:, :, 2])
    attended, log_sums = attention_forward(queries, keys_all, values_all, segment_row_span)
    return (
        attended.reshape(length, row_count, -1).astype(jnp.bfloat16),
        log_sums,
        (queries, keys_all, values_all),
    )


def attention_project(attended_b, w_out):
    return lax.psum_scatter(
        jnp.einsum("srf,fd->srd", attended_b, w_out, preferred_element_type=jnp.float32).astype(
            jnp.bfloat16
        ),
        "tensor",
        scatter_dimension=0,
        tiled=True,
    ).astype(jnp.float32)


def attention_grad_heads(grad_middle_b, w_out):
    grad_attended = jnp.einsum(
        "srd,fd->srf",
        lax.all_gather(grad_middle_b, "tensor", axis=0, tiled=True),
        w_out,
        preferred_element_type=jnp.float32,
    )
    return grad_attended.astype(jnp.bfloat16)


def mlp_pre(normed_b, w_fc):
    return jnp.einsum(
        "srd,df->srf",
        lax.all_gather(normed_b, "tensor", axis=0, tiled=True),
        w_fc,
        preferred_element_type=jnp.float32,
    )


def mlp_out(hidden_b, w_proj):
    return lax.psum_scatter(
        jnp.einsum("srf,fd->srd", hidden_b, w_proj, preferred_element_type=jnp.float32).astype(
            jnp.bfloat16
        ),
        "tensor",
        scatter_dimension=0,
        tiled=True,
    ).astype(jnp.float32)


def mlp_back(grad_mlp, pre_act, w_fc, w_proj):
    grad_hidden = jnp.einsum(
        "srd,fd->srf",
        lax.all_gather(grad_mlp, "tensor", axis=0, tiled=True),
        w_proj,
        preferred_element_type=jnp.float32,
    )
    activated, slope = jax.vjp(gelu_tanh, pre_act)
    grad_pre = slope(grad_hidden)[0].astype(jnp.bfloat16)
    return lax.psum_scatter(
        jnp.einsum("srf,df->srd", grad_pre, w_fc, preferred_element_type=jnp.float32).astype(
            jnp.bfloat16
        ),
        "tensor",
        scatter_dimension=0,
        tiled=True,
    ).astype(jnp.float32)


def forward_layer_step(layer_input_rows, segment_row_span, fixed_weights, adapter_pair):
    norm_rows = normalize(layer_input_rows, fixed_weights[0])[0].astype(jnp.bfloat16)
    stacked_weights = projected_rows(
        lax.all_gather(norm_rows, "tensor", axis=0, tiled=True), fixed_weights[1], adapter_pair
    )[0]
    attended_b = attend_all(stacked_weights, segment_row_span)[0]
    middle = layer_input_rows + attention_project(attended_b, fixed_weights[2])
    normed_mlp = normalize(middle, fixed_weights[3])[0].astype(jnp.bfloat16)
    pre_act = mlp_pre(normed_mlp, fixed_weights[4])
    hidden_b = gelu_tanh(pre_act).astype(jnp.bfloat16)
    return middle + mlp_out(hidden_b, fixed_weights[5])


def backward_layer_step(
    layer_input_rows, segment_row_span, upstream_gradient, fixed_weights, adapter_pair
):
    gain_a, joint_projection_weight, w_out, gain_m, w_fc, w_proj = fixed_weights
    query_down_factor, query_up_factor, value_down_factor, value_up_factor = adapter_pair
    factor = 32.0 / query_down_factor.shape[-1]
    norm_rows, unit_first, inverse_first = normalize(layer_input_rows, gain_a)
    collected_rows = lax.all_gather(norm_rows.astype(jnp.bfloat16), "tensor", axis=0, tiled=True)
    stacked_weights, narrow_query_rows, narrow_value_rows = projected_rows(
        collected_rows, joint_projection_weight, adapter_pair
    )
    length, row_count = (collected_rows.shape[0], collected_rows.shape[1])
    attended_b, log_sums, head_views = attend_all(stacked_weights, segment_row_span)
    queries, keys_all, values_all = head_views
    middle = layer_input_rows + attention_project(attended_b, w_out)
    normed_mlp, unit_second, inverse_second = normalize(middle, gain_m)
    pre_act = mlp_pre(normed_mlp.astype(jnp.bfloat16), w_fc)
    grad_norm_mlp = mlp_back(upstream_gradient.astype(jnp.bfloat16), pre_act, w_fc, w_proj)
    grad_middle = upstream_gradient + normalize_back(
        grad_norm_mlp, unit_second, inverse_second, gain_m
    )
    grad_attended = attention_grad_heads(grad_middle.astype(jnp.bfloat16), w_out)
    grad_heads = grad_attended.reshape(queries.shape)
    grad_queries, grad_keys, grad_values = attention_backward(
        queries, keys_all, values_all, segment_row_span, log_sums, grad_heads
    )
    grad_stack = (
        jnp.stack([grad_queries, grad_keys, grad_values], axis=2)
        .astype(jnp.bfloat16)
        .reshape(length, row_count, 3, -1)
    )
    grad_query_rows = grad_stack[:, :, 0]
    grad_value_rows = grad_stack[:, :, 2]
    thin_grad_query = factor * jnp.einsum(
        "srf,kf->srk", grad_query_rows, query_up_factor, preferred_element_type=jnp.float32
    )
    thin_grad_value = factor * jnp.einsum(
        "srf,kf->srk", grad_value_rows, value_up_factor, preferred_element_type=jnp.float32
    )
    grad_bq = factor * jnp.einsum(
        "srk,srf->kf", narrow_query_rows, grad_query_rows.astype(jnp.float32), precision=PRECISE
    )
    grad_bv = factor * jnp.einsum(
        "srk,srf->kf", narrow_value_rows, grad_value_rows.astype(jnp.float32), precision=PRECISE
    )
    gathered_wide = collected_rows.astype(jnp.float32)
    grad_aq = jnp.einsum("srd,srk->dk", gathered_wide, thin_grad_query, precision=PRECISE)
    grad_av = jnp.einsum("srd,srk->dk", gathered_wide, thin_grad_value, precision=PRECISE)
    a_query_wide = query_down_factor.astype(jnp.float32)
    a_value_wide = value_down_factor.astype(jnp.float32)
    term = jnp.einsum(
        "srcf,dcf->srd", grad_stack, joint_projection_weight, preferred_element_type=jnp.float32
    )
    term = term + jnp.einsum("srk,dk->srd", thin_grad_query, a_query_wide, precision=PRECISE)
    grad_norm_attn = lax.psum_scatter(
        (term + jnp.einsum("srk,dk->srd", thin_grad_value, a_value_wide, precision=PRECISE)).astype(
            jnp.bfloat16
        ),
        "tensor",
        scatter_dimension=0,
        tiled=True,
    ).astype(jnp.float32)
    layer_output_rows = grad_middle + normalize_back(
        grad_norm_attn, unit_first, inverse_first, gain_a
    )
    return (layer_output_rows, (grad_aq, grad_bq, grad_av, grad_bv))


def body(
    inputs,
    segments,
    cotangent,
    gain_attn,
    joint_projection_weight,
    query_down_factor,
    query_up_factor,
    value_down_factor,
    value_up_factor,
    w_out,
    gain_mlp,
    w_fc,
    w_proj,
):
    fixed_weights = (
        gain_attn[0],
        joint_projection_weight[0],
        w_out[0],
        gain_mlp[0],
        w_fc[0],
        w_proj[0],
    )
    adapter_pair = (
        query_down_factor[0],
        query_up_factor[0],
        value_down_factor[0],
        value_up_factor[0],
    )
    sections = lax.axis_size("section")
    section_index = lax.axis_index("section")
    is_first = section_index == 0
    is_last = section_index == sections - 1
    rows_mb = inputs.shape[1] // MICRO
    ticks = MICRO + sections - 1
    block_shape = (inputs.shape[0], rows_mb, inputs.shape[2])
    activations = jnp.zeros_like(inputs)
    kept_inputs = jnp.zeros((MICRO,) + block_shape, jnp.bfloat16)
    arriving = jnp.zeros(block_shape, jnp.bfloat16)
    for tick_index in range(ticks):
        own_index = min(tick_index, MICRO - 1)
        mb_slot = tick_index - section_index
        is_valid = (mb_slot >= 0) & (mb_slot < MICRO)
        mb_slot = jnp.clip(mb_slot, 0, MICRO - 1)
        fresh = lax.slice_in_dim(inputs, own_index * rows_mb, (own_index + 1) * rows_mb, axis=1)
        layer_input_rows = jnp.where(is_first, fresh, arriving)
        segment_row_span = lax.dynamic_slice_in_dim(segments, mb_slot * rows_mb, rows_mb, 0)
        layer_output_rows = forward_layer_step(
            layer_input_rows.astype(jnp.float32), segment_row_span, fixed_weights, adapter_pair
        ).astype(jnp.bfloat16)
        activations = jnp.where(
            is_valid,
            lax.dynamic_update_slice_in_dim(activations, layer_output_rows, mb_slot * rows_mb, 1),
            activations,
        )
        kept_inputs = jnp.where(
            is_valid, kept_inputs.at[mb_slot].set(layer_input_rows), kept_inputs
        )
        if tick_index < ticks - 1:
            arriving = passed_along(layer_output_rows, "section", 1)
    input_grads = jnp.zeros_like(inputs)
    gradient_totals = tuple(
        (jnp.zeros(factor_tensor.shape, jnp.float32) for factor_tensor in adapter_pair)
    )
    arriving = jnp.zeros(block_shape, jnp.bfloat16)
    for tick_index in range(ticks):
        own_index = min(tick_index, MICRO - 1)
        mb_slot = tick_index - (sections - 1 - section_index)
        is_valid = (mb_slot >= 0) & (mb_slot < MICRO)
        mb_slot = jnp.clip(mb_slot, 0, MICRO - 1)
        given = lax.slice_in_dim(cotangent, own_index * rows_mb, (own_index + 1) * rows_mb, axis=1)
        upstream_gradient = jnp.where(is_last, given, arriving).astype(jnp.float32)
        layer_input_rows = kept_inputs[mb_slot].astype(jnp.float32)
        segment_row_span = lax.dynamic_slice_in_dim(segments, mb_slot * rows_mb, rows_mb, 0)
        layer_output_rows, row_pieces = backward_layer_step(
            layer_input_rows, segment_row_span, upstream_gradient, fixed_weights, adapter_pair
        )
        leaving_b = layer_output_rows.astype(jnp.bfloat16)
        input_grads = jnp.where(
            is_valid,
            lax.dynamic_update_slice_in_dim(input_grads, leaving_b, mb_slot * rows_mb, 1),
            input_grads,
        )
        gradient_totals = tuple(
            (
                running + jnp.where(is_valid, piece_grad, 0.0)
                for running, piece_grad in zip(gradient_totals, row_pieces)
            )
        )
        if tick_index < ticks - 1:
            arriving = passed_along(leaving_b, "section", -1)
    adapter_rank = adapter_pair[1].shape[0]
    model_width = inputs.shape[2]
    column_total = adapter_pair[1].shape[1]
    offset = lax.axis_index("tensor") * column_total
    full_query = lax.dynamic_update_slice_in_dim(
        jnp.zeros((adapter_rank, model_width), jnp.float32), gradient_totals[1], offset, 1
    )
    full_value = lax.dynamic_update_slice_in_dim(
        jnp.zeros((adapter_rank, model_width), jnp.float32), gradient_totals[3], offset, 1
    )
    summed = lax.psum(
        (gradient_totals[0], full_query, gradient_totals[2], full_value), ("dp", "tensor")
    )
    return (
        activations[None],
        input_grads[None],
        summed[0][None],
        summed[1][None],
        summed[2][None],
        summed[3][None],
    )


REACH = 512
BF16 = jnp.bfloat16
F32 = jnp.float32
MESH = pl.DeviceIdType.MESH


def dot_nn(a, b):
    return lax.dot_general(a, b, (((1,), (0,)), ((), ())), preferred_element_type=F32)


def dot_nt(a, b):
    return lax.dot_general(a, b, (((1,), (1,)), ((), ())), preferred_element_type=F32)


def dot_tn(a, b):
    return lax.dot_general(a, b, (((0,), (0,)), ((), ())), preferred_element_type=F32)


def norm_stats(rows):
    middle = jnp.mean(rows, axis=-1, keepdims=True)
    centred = rows - middle
    inverse = lax.rsqrt(jnp.mean(centred * centred, axis=-1, keepdims=True) + EPSILON)
    return centred * inverse, inverse


def gelu_slope(pre):
    square = pre * pre
    bent = jnp.tanh(TANH_SCALE * (pre + CUBIC_TERM * square * pre))
    return 0.5 * (1.0 + bent) + (0.5 * TANH_SCALE) * pre * (1.0 - bent * bent) * (
        1.0 + (3.0 * CUBIC_TERM) * square
    )


def key_span(i, block):
    return max(0, i - REACH // block) * block, (i + 1) * block


def allowed_keys(i, block, seg_col_ref, seg_row_ref):
    low, high = key_span(i, block)
    seg_k = seg_col_ref[low:high, :]
    seg_q = seg_row_ref[:, i * block : (i + 1) * block]
    places_k = low + lax.broadcasted_iota(jnp.int32, (high - low, block), 0)
    places_q = i * block + lax.broadcasted_iota(jnp.int32, (high - low, block), 1)
    return (seg_q == seg_k) & (places_k <= places_q)


def head_lanes(rows, h):
    lane = lax.broadcasted_iota(jnp.int32, (rows, 128), 1)
    return (lane < HEAD_DIM) if h == 0 else (lane >= HEAD_DIM)


def both_halves(ref, *index):
    return jnp.concatenate([ref[(*index, 0)], ref[(*index, 1)]], axis=1)


class Wires:
    def __init__(self, send, recv):
        self.send, self.recv, self.count, self.sent = send, recv, 0, []

    def copy(self, source, target, where):
        k = self.count
        self.count += 1
        made = pltpu.make_async_remote_copy(
            src_ref=source,
            dst_ref=target,
            send_sem=self.send.at[k],
            recv_sem=self.recv.at[k],
            device_id=where,
            device_id_type=MESH,
        )
        self.sent.append(made)
        return made

    def forget(self, copy):
        self.sent = [one for one in self.sent if one is not copy]


class Totals:
    def __init__(self, wires, layer, out_ref, in_ref, hops):
        self.out_ref, self.in_ref, self.layer, self.at = out_ref, in_ref, layer, 0
        self.hops = [
            wires.copy(out_ref.at[layer, k], in_ref.at[layer, k], peer)
            for k, peer in enumerate(hops)
        ]
        self.wires = wires
        self.hops[0].start()

    def step(self):
        k, layer = self.at, self.layer
        self.hops[k].wait_recv()
        summed = self.out_ref[layer, k] + self.in_ref[layer, k]
        self.at = k + 1
        if self.at < len(self.hops):
            self.out_ref[layer, self.at] = summed
            self.hops[self.at].start()
        else:
            self.hops[0].wait_send()
            self.wires.forget(self.hops[0])
            self.out_ref[layer, 0] = summed

    def finish(self):
        while self.at < len(self.hops):
            self.step()


WIRES = 128


def step_kernel(
    block,
    model,
    planes,
    x_rows,
    cot_rows,
    seg_rows,
    gain_a,
    gain_m,
    downs_t,
    up_q,
    up_v,
    wq,
    wo,
    fc,
    proj,
    act_out,
    grad_out,
    sums_out,
    act,
    grad,
    xb,
    cb,
    seg_col,
    seg_row,
    sm,
    up,
    pad,
    wq_all,
    up_all,
    wo_all,
    ff,
    rows,
    thin,
    qkv,
    o_out,
    o_in,
    middle,
    norm2,
    pre,
    part_out,
    part_in,
    own_sum,
    do_in,
    dqkv,
    dk_acc,
    dv_acc,
    c_out,
    c_in,
    y_out,
    y_in,
    down_sums,
    up_sums,
    total_out,
    total_in,
    wire_send,
    wire_recv,
    row_send,
    row_recv,
    wq_send,
    wq_recv,
    wq_half,
    local_sem,
    o_send,
    o_recv,
    place_send,
    place_recv,
):
    c = lax.axis_index("section")
    z = lax.axis_index("dp")
    t = lax.axis_index("tensor")
    y, x = lax.div(t, 2), lax.rem(t, 2)
    over_x, over_y = 2 * y + (1 - x), 2 * (1 - y) + x
    mine, twin = 2 * y + c, 2 * y + (1 - c)
    far, far_twin = 2 * (1 - y) + c, 2 * (1 - y) + (1 - c)
    to_c, to_x, to_y = {"section": 1 - c}, {"tensor": over_x}, {"tensor": over_y}
    to_xc = {"section": 1 - c, "tensor": over_x}
    to_yc = {"section": 1 - c, "tensor": over_y}
    to_zs = []
    bit = 1
    while bit < planes:
        up_bit = lax.rem(lax.div(z, bit), 2)
        to_zs.append({"dp": z + bit - 2 * bit * up_bit})
        bit *= 2
    to_z = to_zs[0]
    odd = lax.rem(z, 2)
    here = c == x
    wires = Wires(wire_send, wire_recv)
    width = wq.shape[2]
    factor = 8.0

    barrier = pltpu.get_barrier_semaphore()
    peers = [to_c, to_x, to_y, to_xc, to_yc, *to_zs]
    for peer in peers:
        pl.semaphore_signal(barrier, inc=1, device_id=peer, device_id_type=MESH)
    pl.semaphore_wait(barrier, len(peers))

    def part(which, count):
        first = odd if which == 0 else 1 - odd
        return pl.ds(pl.multiple_of(first * (count // 2), count // 2), count // 2)

    def row_copy(source, target, k):
        return pltpu.make_async_remote_copy(
            src_ref=source,
            dst_ref=target,
            send_sem=row_send.at[k],
            recv_sem=row_recv.at[k],
            device_id=to_x,
            device_id_type=MESH,
        )

    x_copy = row_copy(x_rows.at[1 - x], xb, 0)
    cot_local = pltpu.make_async_copy(cot_rows.at[x], cb.at[0], row_recv.at[1])

    @pl.when(here)
    def _():
        x_copy.start()
        cot_local.start()
        pltpu.make_async_copy(x_rows.at[x], xb, row_recv.at[0]).start()

    pad[...] = jnp.zeros_like(pad)
    pad[0:4] = up_q[...].astype(F32)
    up[0] = pad[...].astype(BF16)
    pad[0:4] = jnp.zeros((4, width), F32)
    pad[4:8] = up_v[...].astype(F32)
    up[1] = pad[...].astype(BF16)

    def wq_twin():
        return [
            pltpu.make_async_remote_copy(
                src_ref=source,
                dst_ref=target.at[c],
                send_sem=wq_send.at[0, j],
                recv_sem=wq_recv.at[c, j],
                device_id=to_c,
                device_id_type=MESH,
            )
            for j, (source, target) in enumerate(((wq, wq_all), (up, up_all)))
        ]

    def wq_over_x():
        cut = part(0, model)
        where = {"section": x, "tensor": over_x}
        made = [
            pltpu.make_async_remote_copy(
                src_ref=wq.at[k, cut],
                dst_ref=wq_all.at[c, k, cut],
                send_sem=wq_send.at[1, k],
                recv_sem=wq_half.at[c, 0, k],
                device_id=where,
                device_id_type=MESH,
            )
            for k in range(3)
        ]
        made.append(
            pltpu.make_async_remote_copy(
                src_ref=up,
                dst_ref=up_all.at[c],
                send_sem=wq_send.at[0, 2],
                recv_sem=wq_recv.at[c, 1],
                device_id=where,
                device_id_type=MESH,
            )
        )
        return made

    def wq_over_z(layer):
        cut = part(0, model)
        return [
            pltpu.make_async_remote_copy(
                src_ref=wq_all.at[layer, k, cut],
                dst_ref=wq_all.at[layer, k, cut],
                send_sem=wq_send.at[2 + layer, k],
                recv_sem=wq_half.at[layer, 1, k],
                device_id=to_z,
                device_id_type=MESH,
            )
            for k in range(3)
        ]

    def wq_local(layer):
        return [
            pltpu.make_async_copy(source, target.at[layer], wq_recv.at[layer, j])
            for j, (source, target) in enumerate(((wq, wq_all), (up, up_all)))
        ]

    def send_wq_far(layer, pieces):
        @pl.when(c == layer)
        def _():
            copies = wq_over_x()
            for k in pieces:
                copies[k].start()

    def send_wq_near():
        @pl.when(here)
        def _():
            for copy in wq_local(c):
                copy.start()

        @pl.when(jnp.logical_not(here))
        def _():
            for copy in wq_twin():
                copy.start()

    def half_wait(layer, which, k):
        cut = part(which, model)
        pltpu.make_async_copy(
            wq.at[k, cut], wq_all.at[layer, k, cut], wq_half.at[layer, which, k]
        ).wait()

    def pass_wq(layer):
        @pl.when(jnp.logical_not(here))
        def _():
            for k, copy in enumerate(wq_over_z(layer)):
                half_wait(layer, 0, k)
                copy.start()

    def arrived_wq(layer):
        whole, small = wq_local(layer)
        small.wait()
        pl.when(here)(whole.wait)

        @pl.when(jnp.logical_not(here))
        def _():
            for k in range(3):
                half_wait(layer, 1, k)

    def sent_wq():
        for copy in wq_over_x():
            copy.wait_send()

        @pl.when(jnp.logical_not(here))
        def _():
            for copy in wq_twin():
                copy.wait_send()
            for layer in range(2):
                for copy in wq_over_z(layer):
                    copy.wait_send()

    send_wq_far(0, (3, 0, 1, 2))
    pl.when(c == 0)(send_wq_near)

    sm[c, 0:1] = gain_a[...]
    sm[c, 8:9] = gain_m[...]
    sm[c, 16:24] = downs_t[...].astype(F32)
    sm[c, 24:32] = jnp.zeros((8, model), F32)
    small_copy = wires.copy(sm.at[c], sm.at[c], to_c)
    small_copy.start()
    seg_row[...] = seg_rows[pl.ds(x, 1), :]
    same = lax.broadcasted_iota(jnp.int32, (128, 128), 0) == lax.broadcasted_iota(
        jnp.int32, (128, 128), 1
    )
    for k in range(4 * block // 128):
        lanes = slice(k * 128, (k + 1) * 128)
        seg_col[lanes, :] = jnp.sum(
            jnp.where(same, seg_row[:, lanes], 0), axis=1, keepdims=True
        )

    locals_ = [
        pltpu.make_async_copy(source, target, local_sem.at[k])
        for k, (source, target) in enumerate(
            ((fc, ff.at[c, 0, 0]), (proj, ff.at[c, 1, 0]), (wo, wo_all.at[c, t]))
        )
    ]
    piece = model // 4

    def ff_rows(p, which):
        first = odd if which == 0 else 1 - odd
        return pl.ds(pl.multiple_of(first * (model // 2) + (p % 2) * piece, piece), piece)

    def ff_same(p, which, where):
        at = ff.at[c, p // 2, 1, ff_rows(p, which)]
        return wires.copy(at, at, where)

    ff_twin = [wires.copy(one, ff.at[c, k, 0], to_c) for k, one in enumerate((fc, proj))]
    ff_x = [
        wires.copy(
            (fc, proj)[p // 2].at[ff_rows(p, 0)], ff.at[c, p // 2, 1, ff_rows(p, 0)], to_x
        )
        for p in range(4)
    ]
    ff_z = [ff_same(p, 0, to_z) for p in range(4)]
    ff_c = [[ff_same(p, which, to_c) for which in range(2)] for p in range(4)]

    def start_ff(layer):
        @pl.when(c == layer)
        def _():
            for copy in ff_x:
                copy.start()

    def pass_ff_x(layer, p):
        @pl.when(c == layer)
        def _():
            ff_x[p].wait_recv()
            ff_z[p].start()
            ff_c[p][0].start()

    def pass_ff_z(layer, p):
        @pl.when(c == layer)
        def _():
            ff_z[p].wait_recv()
            ff_c[p][1].start()

    def arrived_ff(layer):
        @pl.when(c != layer)
        def _():
            for pair in ff_c:
                for copy in pair:
                    copy.wait_recv()

    corner = 2 * (1 - y) + (1 - x)
    wo_cut = part(0, width)
    quart = width // 4
    wo_low = pl.ds(pl.multiple_of(odd * (width // 2), quart), quart)
    wo_high = pl.ds(pl.multiple_of(odd * (width // 2) + quart, quart), quart)

    def wo_same(q, cut, where):
        if cut is None:
            return wires.copy(wo_all.at[c, q], wo_all.at[c, q], where)
        return wires.copy(wo_all.at[c, q, cut], wo_all.at[c, q, cut], where)

    wo_twin = wires.copy(wo, wo_all.at[c, t], to_c)
    wo_x = wires.copy(wo.at[wo_cut], wo_all.at[c, t, wo_cut], to_x)
    wo_y = wires.copy(wo.at[wo_cut], wo_all.at[c, t, wo_cut], to_y)
    wo_dy = wo_same(over_x, wo_low, to_y)
    wo_dx = wo_same(over_y, wo_high, to_x)
    wo_z = [wo_same(q, wo_cut, to_z) for q in (over_x, over_y, corner)]
    wo_c = [wo_same(q, None, to_c) for q in (over_x, over_y, corner)]

    def start_wo_x(layer):
        pl.when(c == layer)(wo_x.start)

    def start_wo_y(layer):
        pl.when(c == layer)(wo_y.start)

    def pass_wo(layer, stage):
        @pl.when(c == layer)
        def _():
            if stage == 0:
                wo_x.wait_recv()
                wo_dy.start()
                wo_z[0].start()
                wo_y.wait_recv()
                wo_dx.start()
                wo_z[1].start()
            if stage == 1:
                wo_dy.wait_recv()
                wo_dx.wait_recv()
                wo_z[2].start()
            if stage == 2:
                for came, onward in zip(wo_z, wo_c):
                    came.wait_recv()
                    onward.start()

    def arrived_wo(layer):
        @pl.when(c == layer)
        def _():
            locals_[2].wait()

        @pl.when(c != layer)
        def _():
            wo_twin.wait_recv()
            for copy in wo_c:
                copy.wait_recv()

    for copy in locals_:
        copy.start()
    for copy in ff_twin + [wo_twin]:
        copy.start()
    start_wo_x(0)
    start_ff(0)

    def place_copy(kind, layer, source, target, at=slice(None)):
        return pltpu.make_async_remote_copy(
            src_ref=source.at[at],
            dst_ref=target.at[x, at],
            send_sem=place_send.at[kind, layer],
            recv_sem=place_recv.at[kind, x],
            device_id={"section": layer, "tensor": mine},
            device_id_type=MESH,
        )

    def place(kind, layer, source, target, at=slice(None)):
        stays = jnp.logical_and(here, c == layer)

        @pl.when(stays)
        def _():
            target[x, at] = source[at]

        @pl.when(jnp.logical_not(stays))
        def _():
            place_copy(kind, layer, source, target, at).start()

    def placed(kind, source, target):
        for layer in range(2):
            stays = jnp.logical_and(here, c == layer)

            @pl.when(jnp.logical_not(stays))
            def _():
                place_copy(kind, layer, source.at[layer], target).wait_send()

        for slot in range(2):
            came = jnp.logical_not(jnp.logical_and(here, x == slot))

            @pl.when(came)
            def _():
                pltpu.make_async_copy(
                    source.at[0], target.at[slot], place_recv.at[kind, slot]
                ).wait()

    def qkv_block(layer, b):
        normed = rows[layer, b]
        down = sm[layer, 16:32, :].astype(BF16)
        low = dot_nt(normed, down)
        low_b = low.astype(BF16)
        thin[layer, b] = low_b
        at = pl.ds(pl.multiple_of(b * block, block), block)
        for k in range(3):
            made = dot_nn(normed, wq_all[layer, k])
            if k == 0:
                made = made + factor * dot_nn(low_b, up_all[layer, 0])
            if k == 2:
                made = made + factor * dot_nn(low_b, up_all[layer, 1])
            made = made.astype(BF16)
            qkv[layer, k, 0, at, :] = made[:, :128]
            qkv[layer, k, 1, at, :] = made[:, 128:]

    def attend(layer, i):
        low, high = key_span(i, block)
        at = slice(i * block, (i + 1) * block)
        allowed = allowed_keys(i, block, seg_col, seg_row)

        def one_pair(pair, carry):
            queries = qkv[layer, 0, pair, at, :] * BF16(HEAD_DIM**-0.5)
            keys = qkv[layer, 1, pair, low:high, :]
            values = qkv[layer, 2, pair, low:high, :]
            parts = []
            for h in range(2):
                picked = jnp.where(head_lanes(block, h), queries, BF16(0))
                scores = jnp.where(allowed, dot_nt(keys, picked), MASKED)
                exponent = jnp.exp(scores - jnp.max(scores, axis=0, keepdims=True))
                total = jnp.sum(exponent, axis=0, keepdims=True)
                made = dot_tn(values, exponent.astype(BF16))
                parts.append(made[h * HEAD_DIM : (h + 1) * HEAD_DIM] / total)
            o_out[i, pair] = jnp.concatenate(parts, axis=0).T.astype(BF16)
            return carry

        lax.fori_loop(0, 2, one_pair, 0)

    def exchange_piece(i, target, phase):
        return pltpu.make_async_remote_copy(
            src_ref=o_out.at[i],
            dst_ref=target.at[mine],
            send_sem=o_send.at[i],
            recv_sem=o_recv.at[phase, mine],
            device_id={"section": i % 2, "tensor": 2 * (i // 2) + x},
            device_id_type=MESH,
        )

    def send_piece(i, target, phase):
        @pl.when(mine == i)
        def _():
            target[mine] = o_out[i]

        @pl.when(mine != i)
        def _():
            exchange_piece(i, target, phase).start()

    def wait_pieces(target, phase):
        for i in range(4):

            @pl.when(mine != i)
            def _():
                exchange_piece(i, target, phase).wait_send()
                pltpu.make_async_copy(o_out.at[i], target.at[i], o_recv.at[phase, i]).wait()

    def hidden_half(layer, who, source, q):
        total = None
        for cut in range(2):
            lanes = slice(cut * model // 2, (cut + 1) * model // 2)
            made = dot_nn(source, ff[layer, 0, q, :, lanes])
            pre[layer, who, q, :, lanes] = made.astype(BF16)
            term = dot_nn(gelu_tanh(made).astype(BF16), ff[layer, 1, q, lanes, :])
            total = term if total is None else total + term
        return total

    def hidden_back(layer, who, upstream, q):
        total = None
        for cut in range(2):
            lanes = slice(cut * model // 2, (cut + 1) * model // 2)
            grad_hidden = dot_nt(upstream, ff[layer, 1, q, lanes, :])
            slope = gelu_slope(pre[layer, who, q, :, lanes].astype(F32))
            term = dot_nt((grad_hidden * slope).astype(BF16), ff[layer, 0, q, :, lanes])
            total = term if total is None else total + term
        return total

    half_rows = [slice(h * block // 2, (h + 1) * block // 2) for h in range(2)]

    def in_halves(source, target, where):
        return [wires.copy(source(at), target(at), where) for at in half_rows]

    def give_rows(layer, h, source):
        at = half_rows[h]
        unit, _ = norm_stats(source[at, :].astype(F32))
        rows[layer, mine, at] = (unit * sm[layer, 0:1, :]).astype(BF16)
        row_y[layer][h].start()
        row_c[layer][h].start()

    row_y, row_c, row_yc = [], [], []
    for layer in range(2):
        for store, b, where in ((row_y, mine, to_y), (row_c, mine, to_c), (row_yc, far, to_c)):
            store.append(
                in_halves(
                    lambda at: rows.at[layer, b, at], lambda at: rows.at[layer, b, at], where
                )
            )

    pltpu.make_async_copy(x_rows.at[x], xb, row_recv.at[0]).wait()
    small_copy.wait_recv()
    cot_x = row_copy(cot_rows.at[1 - x], cb.at[0], 1)
    cot_y = wires.copy(cb.at[0], cb.at[1], to_y)

    for layer in range(2):
        source = xb if layer == 0 else act.at[0]
        if layer == 0:
            for h in range(2):
                give_rows(0, h, xb)
            pass_wq(0)
        else:
            pass_wo(1, 1)
            pass_ff_x(1, 2)
        arrived_wq(layer)
        qkv_block(layer, mine)
        if layer == 1:
            pass_ff_x(1, 3)
            pass_wo(1, 2)
            place(0, 0, act.at[0], act_out)
        for copy in row_c[layer]:
            copy.wait_recv()
        qkv_block(layer, twin)
        for copy, onward in zip(row_y[layer], row_yc[layer]):
            copy.wait_recv()
            onward.start()
        if layer == 0:
            start_wo_y(0)

            @pl.when(here)
            def _():
                cot_local.wait()
                cot_y.start()
        else:

            @pl.when(jnp.logical_not(here))
            def _():
                cot_local.wait()
                cot_y.start()
        qkv_block(layer, far)
        for copy in row_yc[layer]:
            copy.wait_recv()
        qkv_block(layer, far_twin)
        if layer == 0:
            pass_ff_x(0, 0)
        for i in range(4):
            attend(layer, i)
            send_piece(i, o_in, layer)
            if layer == 0 and i == 0:
                pass_wo(0, 0)
            if layer == 0 and i == 2:
                pass_wo(0, 1)
                pass_ff_x(0, 1)
            if layer == 0 and i == 3:
                pass_wo(0, 2)
            if layer == 1 and i >= 2:
                pass_ff_z(1, i - 2)
        arrived_wo(layer)
        wait_pieces(o_in, layer)
        if layer == 0:
            pass_ff_x(0, 2)
        else:
            pass_ff_z(1, 2)
        stream = source[...].astype(F32)
        for q in range(4):
            stream = stream + dot_nn(both_halves(o_in, q), wo_all[layer, q])
        middle[layer] = stream
        unit, _ = norm_stats(stream)
        norm2[0] = (unit * sm[layer, 8:9, :]).astype(BF16)
        norm_y = wires.copy(norm2.at[0], norm2.at[1], to_y)
        norm_y.start()
        if layer == 0:
            for copy in locals_[:2]:
                copy.wait()
            for copy in ff_twin:
                copy.wait_recv()
            pass_ff_z(0, 0)
            pass_ff_x(0, 3)
            pl.when(c == 1)(send_wq_near)
            send_wq_far(1, (3, 0, 1, 2))
            start_wo_x(1)
            start_wo_y(1)
            start_ff(1)
            pass_ff_z(0, 1)
        else:
            pass_ff_z(1, 3)
        own_sum[...] = hidden_half(layer, 0, norm2[0], 0)
        if layer == 0:
            pass_ff_z(0, 2)
            pass_ff_z(0, 3)
            pass_wq(1)
        arrived_ff(layer)
        own_sum[...] += hidden_half(layer, 0, norm2[0], 1)
        if layer == 1:
            grad[0] = own_sum[...].astype(BF16)
            own_sum[...] = hidden_back(1, 0, cb[0], 0) + hidden_back(1, 0, cb[0], 1)
        norm_y.wait_recv()
        away = hidden_half(layer, 1, norm2[1], 0) + hidden_half(layer, 1, norm2[1], 1)
        if layer == 1:
            y_out[...] = away.astype(BF16)
            cot_y.wait_recv()
            away = hidden_back(1, 1, cb[1], 0) + hidden_back(1, 1, cb[1], 1)
        part_out[...] = away.astype(BF16)
        part_y = in_halves(
            lambda at: part_out.at[at], lambda at: part_in.at[layer, at], to_y
        )
        for copy in part_y:
            copy.start()
        if layer == 0:
            stream = middle[layer] + own_sum[...]
            pass_wo(1, 0)
            pass_ff_x(1, 0)
            pass_ff_x(1, 1)

            pl.when(here)(cot_x.start)
            for h, at in enumerate(half_rows):
                part_y[h].wait()
                wires.forget(part_y[h])
                act[0, at] = (stream[at] + part_in[0, at].astype(F32)).astype(BF16)
                give_rows(1, h, act.at[0])
            norm_y.wait_send()
            wires.forget(norm_y)

    for layer in (1, 0):
        upstream = cb[0] if layer == 1 else grad[1]
        if layer == 0:
            own_sum[...] = hidden_back(layer, 0, upstream, 0) + hidden_back(layer, 0, upstream, 1)
            for copy in up_y:
                copy.wait_recv()
            totals.step()
            away = hidden_back(layer, 1, norm2[1], 0) + hidden_back(layer, 1, norm2[1], 1)
            part_out[...] = away.astype(BF16)
            part_y = in_halves(
                lambda at: part_out.at[at], lambda at: part_in.at[1, at], to_y
            )
            for copy in part_y:
                copy.start()
        unit, inverse = norm_stats(middle[layer])
        for copy in part_y:
            copy.wait()
            wires.forget(copy)
        if layer == 0:
            totals.step()
        grad_norm = own_sum[...] + part_in[1].astype(F32)
        grad_middle = upstream.astype(F32) + normalize_back(
            grad_norm, unit, inverse, sm[layer, 8:9, :]
        )
        own_sum[...] = grad_middle
        grad_b = grad_middle.astype(BF16)
        for q in range(4):
            made = dot_nt(grad_b, wo_all[layer, q]).astype(BF16)
            o_out[q, 0] = made[:, :128]
            o_out[q, 1] = made[:, 128:]
            send_piece(q, do_in, 2 + layer)
        if layer == 0:
            place(1, 1, grad.at[1], grad_out)
        else:
            late_y = wires.copy(y_out, part_in.at[0], to_y)
            late_y.start()
        wait_pieces(do_in, 2 + layer)
        if layer == 0:
            totals.step()

        def back_pair(pair, carry):
            dk_acc[...] = jnp.zeros_like(dk_acc)
            dv_acc[...] = jnp.zeros_like(dv_acc)
            for i in range(4):
                low, high = key_span(i, block)
                at = slice(i * block, (i + 1) * block)
                allowed = allowed_keys(i, block, seg_col, seg_row)
                queries = qkv[layer, 0, pair, at, :] * BF16(HEAD_DIM**-0.5)
                keys = qkv[layer, 1, pair, low:high, :]
                values = qkv[layer, 2, pair, low:high, :]
                grads = do_in[i, pair]
                parts = []
                for h in range(2):
                    lanes = head_lanes(block, h)
                    picked = jnp.where(lanes, queries, BF16(0))
                    given = jnp.where(lanes, grads, BF16(0))
                    scores = jnp.where(allowed, dot_nt(keys, picked), MASKED)
                    exponent = jnp.exp(scores - jnp.max(scores, axis=0, keepdims=True))
                    soft = exponent * (1.0 / jnp.sum(exponent, axis=0, keepdims=True))
                    weighted = soft * dot_nt(values, given)
                    grad_scores = (
                        weighted - soft * jnp.sum(weighted, axis=0, keepdims=True)
                    ).astype(BF16)
                    made = dot_tn(keys, grad_scores)
                    parts.append(made[h * HEAD_DIM : (h + 1) * HEAD_DIM])
                    dk_acc[low:high, :] += dot_nn(grad_scores, picked)
                    dv_acc[low:high, :] += dot_nn(soft.astype(BF16), given)
                dqkv[0, pair, at, :] = (
                    jnp.concatenate(parts, axis=0).T * HEAD_DIM**-0.5
                ).astype(BF16)
            dqkv[1, pair] = dk_acc[...].astype(BF16)
            dqkv[2, pair] = dv_acc[...].astype(BF16)
            return carry

        lax.fori_loop(0, 2, back_pair, 0)
        if layer == 1:
            late_y.wait()
            wires.forget(late_y)
            act[1] = (
                middle[1] + grad[0].astype(F32) + part_in[0].astype(F32)
            ).astype(BF16)
            place(0, 1, act.at[1], act_out)
        down = sm[layer, 16:32, :].astype(BF16)
        if layer == 0:
            totals.finish()

        def block_grad(b, first):
            at = pl.ds(pl.multiple_of(b * block, block), block)
            parts = [
                jnp.concatenate([dqkv[k, 0, at, :], dqkv[k, 1, at, :]], axis=1) for k in range(3)
            ]
            low = factor * (
                dot_nt(parts[0], up_all[layer, 0]) + dot_nt(parts[2], up_all[layer, 1])
            )
            low_b = low.astype(BF16)
            term = dot_nn(low_b, down)
            for k in range(3):
                term = term + dot_nt(parts[k], wq_all[layer, k])
            kept = thin[layer, b]
            to_down = dot_tn(low_b, rows[layer, b])
            to_up = [factor * dot_tn(kept, parts[0]), factor * dot_tn(kept, parts[2])]
            if first:
                down_sums[...] = to_down
                up_sums[0], up_sums[1] = to_up
            else:
                down_sums[...] += to_down
                up_sums[0] += to_up[0]
                up_sums[1] += to_up[1]
            return term

        c_far = wires.copy(c_out.at[0], c_in.at[0], to_c)
        c_near = wires.copy(c_out.at[1], c_in.at[1], to_c)
        y_far = in_halves(lambda at: y_out.at[at], lambda at: y_in.at[at], to_y)
        c_out[0] = block_grad(far_twin, True).astype(BF16)
        c_far.start()
        term = block_grad(far, False)
        c_far.wait_recv()
        y_out[...] = (term + c_in[0].astype(F32)).astype(BF16)
        for copy in y_far:
            copy.start()
        c_out[1] = block_grad(twin, False).astype(BF16)
        c_near.start()
        term = block_grad(mine, False)
        total_out[layer, 0, 0:8] = down_sums[0:8]
        total_out[layer, 0, 8:16] = jnp.zeros((8, model), F32)
        low_rows = lax.broadcasted_iota(jnp.int32, (8, width), 0) < 4
        total_out[
            layer, 0, 8:16, pl.ds(pl.multiple_of(mine * width, width), width)
        ] = jnp.where(low_rows, up_sums[0, 0:8], up_sums[1, 0:8])
        totals = Totals(wires, layer, total_out, total_in, [to_c, to_x, to_y, *to_zs])
        c_near.wait_recv()
        term = term + c_in[1].astype(F32)
        source = xb if layer == 0 else act.at[0]
        unit, inverse = norm_stats(source[...].astype(F32))
        if layer == 0:
            totals.step()
            totals.step()
        if layer == 1:
            up_y = in_halves(lambda at: grad.at[1, at], lambda at: norm2.at[1, at], to_y)
        for h, at in enumerate(half_rows):
            y_far[h].wait_recv()
            grad_norm = term[at] + y_in[at].astype(F32)
            grad[layer, at] = (
                own_sum[at]
                + normalize_back(grad_norm, unit[at], inverse[at], sm[layer, 0:1, :])
            ).astype(BF16)
            if layer == 1:
                up_y[h].start()
            else:
                place(1, 0, grad.at[0], grad_out, at)
        for copy in (c_far, c_near, *y_far):
            copy.wait_send()
            wires.forget(copy)

    @pl.when(here)
    def _():
        x_copy.wait_send()
        cot_x.wait_send()


    totals.finish()
    sums_out[...] = jnp.where(c == 0, total_out[0, 0], total_out[1, 0])
    sent_wq()
    for copy in wires.sent:
        copy.wait_send()
    placed(0, act, act_out)
    placed(1, grad, grad_out)


def step_call(block, model, width, planes, operands):
    slots = 4 * block
    hops = 3 + (planes - 1).bit_length()
    in_vmem = pl.BlockSpec(memory_space=pltpu.VMEM)
    in_hbm = pl.BlockSpec(memory_space=pl.ANY)
    return pl.pallas_call(
        functools.partial(step_kernel, block, model, planes),
        out_shape=(
            jax.ShapeDtypeStruct((2, block, model), BF16),
            jax.ShapeDtypeStruct((2, block, model), BF16),
            jax.ShapeDtypeStruct((16, model), F32),
        ),
        in_specs=[in_hbm] * 2 + [in_vmem] * 6 + [in_hbm] * 4,
        out_specs=[in_vmem] * 3,
        scratch_shapes=[
            pltpu.VMEM((2, block, model), BF16),
            pltpu.VMEM((2, block, model), BF16),
            pltpu.VMEM((block, model), BF16),
            pltpu.VMEM((2, block, model), BF16),
            pltpu.VMEM((slots, 1), jnp.int32),
            pltpu.VMEM((1, slots), jnp.int32),
            pltpu.VMEM((2, 32, model), F32),
            pltpu.VMEM((2, 16, width), BF16),
            pltpu.VMEM((16, width), F32),
            pltpu.VMEM((2, 3, model, width), BF16),
            pltpu.VMEM((2, 2, 16, width), BF16),
            pltpu.VMEM((2, 4, width, model), BF16),
            pltpu.VMEM((2, 2, 2, model, model), BF16),
            pltpu.VMEM((2, 4, block, model), BF16),
            pltpu.VMEM((2, 4, block, 16), BF16),
            pltpu.VMEM((2, 3, 2, slots, 128), BF16),
            pltpu.VMEM((4, 2, block, 128), BF16),
            pltpu.VMEM((4, 2, block, 128), BF16),
            pltpu.VMEM((2, block, model), F32),
            pltpu.VMEM((2, block, model), BF16),
            pltpu.VMEM((2, 2, 2, block, model), BF16),
            pltpu.VMEM((block, model), BF16),
            pltpu.VMEM((2, block, model), BF16),
            pltpu.VMEM((block, model), F32),
            pltpu.VMEM((4, 2, block, 128), BF16),
            pltpu.VMEM((3, 2, slots, 128), BF16),
            pltpu.VMEM((slots, 128), F32),
            pltpu.VMEM((slots, 128), F32),
            pltpu.VMEM((2, block, model), BF16),
            pltpu.VMEM((2, block, model), BF16),
            pltpu.VMEM((block, model), BF16),
            pltpu.VMEM((block, model), BF16),
            pltpu.VMEM((16, model), F32),
            pltpu.VMEM((2, 16, width), F32),
            pltpu.VMEM((2, hops, 16, model), F32),
            pltpu.VMEM((2, hops, 16, model), F32),
            pltpu.SemaphoreType.DMA((WIRES,)),
            pltpu.SemaphoreType.DMA((WIRES,)),
            pltpu.SemaphoreType.DMA((3,)),
            pltpu.SemaphoreType.DMA((3,)),
            pltpu.SemaphoreType.DMA((4, 3)),
            pltpu.SemaphoreType.DMA((2, 2)),
            pltpu.SemaphoreType.DMA((2, 2, 3)),
            pltpu.SemaphoreType.DMA((3,)),
            pltpu.SemaphoreType.DMA((4,)),
            pltpu.SemaphoreType.DMA((4, 4)),
            pltpu.SemaphoreType.DMA((2, 2)),
            pltpu.SemaphoreType.DMA((2, 2)),
        ],
        compiler_params=pltpu.CompilerParams(
            collective_id=0, has_side_effects=True, vmem_limit_bytes=62 * 1024 * 1024
        ),
    )(*operands)


def fast_body(
    planes,
    inputs,
    segments,
    cotangent,
    gain_attn,
    joint_projection_weight,
    query_down_factor,
    query_up_factor,
    value_down_factor,
    value_up_factor,
    w_out,
    gain_mlp,
    w_fc,
    w_proj,
):
    block, _, model = inputs.shape
    width = joint_projection_weight.shape[3]
    rank = query_down_factor.shape[2]
    downs = jnp.concatenate([query_down_factor[0], value_down_factor[0]], axis=1)
    acts, grads, total = step_call(
        block,
        model,
        width,
        planes,
        (
            jnp.swapaxes(inputs, 0, 1),
            jnp.swapaxes(cotangent, 0, 1),
            segments,
            gain_attn,
            gain_mlp,
            downs.T,
            query_up_factor[0],
            value_up_factor[0],
            jnp.swapaxes(joint_projection_weight[0], 0, 1),
            w_out[0],
            w_fc[0],
            w_proj[0],
        ),
    )
    return (
        jnp.swapaxes(acts, 0, 1)[None],
        jnp.swapaxes(grads, 0, 1)[None],
        total[:rank].T[None],
        total[2 * rank : 3 * rank][None],
        total[rank : 2 * rank].T[None],
        total[3 * rank :][None],
    )


def fits_fast(mesh, shapes):
    planes = mesh.shape["dp"]
    slots, rows_all, model = shapes[0]
    return (
        mesh.shape["section"] == 2
        and mesh.shape["tensor"] == 4
        and planes > 1
        and planes & (planes - 1) == 0
        and rows_all == 2 * planes
        and slots == 1024
        and model == 1024
        and shapes[4][3] == 1024
        and shapes[5][2] == 4
        and shapes[11][2] == 4096
    )


def solution(mesh):
    placed = (
        P("tensor", "dp", None),
        P("dp", None),
        P("tensor", "dp", None),
        P("section", None),
        P("section", None, None, "tensor"),
        P("section", None, None),
        P("section", None, "tensor"),
        P("section", None, None),
        P("section", None, "tensor"),
        P("section", "tensor", None),
        P("section", None),
        P("section", None, "tensor"),
        P("section", "tensor", None),
    )

    def mapped(picked):
        return jax.shard_map(
            picked,
            mesh=mesh,
            in_specs=placed,
            out_specs=(
                P("section", "tensor", "dp", None),
                P("section", "tensor", "dp", None),
                P("section", None, None),
                P("section", None, None),
                P("section", None, None),
                P("section", None, None),
            ),
            check_vma=False,
        )

    def choose(*args):
        if fits_fast(mesh, [a.shape for a in args]):
            return mapped(functools.partial(fast_body, mesh.shape["dp"]))(*args)
        return mapped(body)(*args)

    return choose
```

```python
import functools

import jax
import jax.numpy as jnp
from jax import lax
from jax.experimental import pallas as pl
from jax.experimental.pallas import tpu as pltpu
from jax.sharding import PartitionSpec as P

HEAD_DIM = 64
MICRO = 2


EPSILON = 1e-05
PRECISE = lax.Precision.HIGHEST
MASKED = -1000000000.0
CUBIC_TERM = 0.044715
TANH_SCALE = 0.7978845608028654


def passed_along(block, axis, distance):
    devices = range(lax.axis_size(axis))
    route = [(i - distance, i) for i in devices if i - distance in devices]
    return lax.ppermute(block, axis, route)


def gelu_tanh(value):
    return 0.5 * value * (1.0 + jnp.tanh(TANH_SCALE * (value + CUBIC_TERM * value * value * value)))


def normalize(residual_stream, gain):
    middle = jnp.mean(residual_stream, axis=-1, keepdims=True)
    centred = residual_stream - middle
    inverse = lax.rsqrt(jnp.mean(centred * centred, axis=-1, keepdims=True) + EPSILON)
    unit_rows = centred * inverse
    return (unit_rows * gain, unit_rows, inverse)


def normalize_back(grad_norm, unit_rows, inverse, gain):
    scaled = grad_norm * gain
    return inverse * (
        scaled
        - jnp.mean(scaled, axis=-1, keepdims=True)
        - unit_rows * jnp.mean(scaled * unit_rows, axis=-1, keepdims=True)
    )


def block_mask(segment_row_span, first_row, block):
    length = segment_row_span.shape[1]
    segment_part = lax.dynamic_slice_in_dim(segment_row_span, first_row, block, 1)
    query_places = first_row + jnp.arange(block)
    key_places = jnp.arange(length)
    same_doc = segment_part[:, :, None] == segment_row_span[:, None, :]
    return same_doc & (key_places[None, None, :] <= query_places[None, :, None])


def projected_rows(row_portion, joint_projection_weight, adapter_pair):
    query_down_factor, query_up_factor, value_down_factor, value_up_factor = adapter_pair
    factor = 32.0 / query_down_factor.shape[-1]
    joined = jnp.einsum(
        "srd,dcf->srcf", row_portion, joint_projection_weight, preferred_element_type=jnp.float32
    )
    narrow_query_rows = jnp.einsum(
        "srd,dk->srk", row_portion, query_down_factor, preferred_element_type=jnp.float32
    )
    narrow_value_rows = jnp.einsum(
        "srd,dk->srk", row_portion, value_down_factor, preferred_element_type=jnp.float32
    )
    queries = joined[:, :, 0] + factor * jnp.einsum(
        "srk,kf->srf", narrow_query_rows, query_up_factor.astype(jnp.float32), precision=PRECISE
    )
    values_all = joined[:, :, 2] + factor * jnp.einsum(
        "srk,kf->srf", narrow_value_rows, value_up_factor.astype(jnp.float32), precision=PRECISE
    )
    stacked_weights = jnp.stack([queries, joined[:, :, 1], values_all], axis=2).astype(jnp.bfloat16)
    return (stacked_weights, narrow_query_rows, narrow_value_rows)


def attention_forward(queries, keys_all, values_all, segment_row_span):
    length, row_count, head_count, width = queries.shape
    block = min(512, length)
    factor = width ** (-0.5)

    def one_block(block_index):
        first_row = block_index * block
        query_part = lax.dynamic_slice_in_dim(queries, first_row, block, 0)
        scores = (
            jnp.einsum("qrhe,krhe->rhqk", query_part, keys_all, preferred_element_type=jnp.float32)
            * factor
        )
        allowed = block_mask(segment_row_span, first_row, block)
        scores = jnp.where(allowed[:, None], scores, MASKED)
        row_max = jnp.max(scores, axis=-1, keepdims=True)
        exponent = jnp.exp(scores - row_max)
        total = jnp.sum(exponent, axis=-1, keepdims=True)
        weights_soft = (exponent / total).astype(jnp.bfloat16)
        attended = jnp.einsum(
            "rhqk,krhe->qrhe", weights_soft, values_all, preferred_element_type=jnp.float32
        )
        return (attended, (row_max + jnp.log(total))[..., 0])

    attended, log_sums = lax.map(one_block, jnp.arange(length // block))
    attended = attended.reshape(length, row_count, head_count, width)
    log_sums = jnp.moveaxis(log_sums, 0, 2).reshape(row_count, head_count, length)
    return (attended, log_sums)


def attention_backward(queries, keys_all, values_all, segment_row_span, log_sums, grad_heads):
    length = queries.shape[0]
    block = min(512, length)
    factor = queries.shape[-1] ** (-0.5)

    def one_block(carry, block_index):
        grad_keys, grad_values = carry
        first_row = block_index * block
        query_part = lax.dynamic_slice_in_dim(queries, first_row, block, 0)
        grad_part = lax.dynamic_slice_in_dim(grad_heads, first_row, block, 0)
        sums_part = lax.dynamic_slice_in_dim(log_sums, first_row, block, 2)
        scores = (
            jnp.einsum("qrhe,krhe->rhqk", query_part, keys_all, preferred_element_type=jnp.float32)
            * factor
        )
        allowed = block_mask(segment_row_span, first_row, block)
        scores = jnp.where(allowed[:, None], scores, MASKED)
        weights_soft = jnp.exp(scores - sums_part[..., None])
        grad_soft = jnp.einsum(
            "qrhe,krhe->rhqk", grad_part, values_all, preferred_element_type=jnp.float32
        )
        grad_scores = weights_soft * (
            grad_soft - jnp.sum(weights_soft * grad_soft, axis=-1, keepdims=True)
        )
        grad_scores = grad_scores.astype(jnp.bfloat16)
        grad_query = (
            jnp.einsum("rhqk,krhe->qrhe", grad_scores, keys_all, preferred_element_type=jnp.float32)
            * factor
        )
        grad_keys = (
            grad_keys
            + jnp.einsum(
                "rhqk,qrhe->krhe", grad_scores, query_part, preferred_element_type=jnp.float32
            )
            * factor
        )
        grad_values = grad_values + jnp.einsum(
            "rhqk,qrhe->krhe",
            weights_soft.astype(jnp.bfloat16),
            grad_part,
            preferred_element_type=jnp.float32,
        )
        return ((grad_keys, grad_values), grad_query)

    start_state = (jnp.zeros(keys_all.shape, jnp.float32), jnp.zeros(values_all.shape, jnp.float32))
    (grad_keys, grad_values), grad_blocks = lax.scan(
        one_block, start_state, jnp.arange(length // block)
    )
    return (grad_blocks.reshape(queries.shape), grad_keys, grad_values)


def attend_all(stacked_weights, segment_row_span):
    length, row_count = (stacked_weights.shape[0], stacked_weights.shape[1])
    head_view = stacked_weights.reshape(length, row_count, 3, -1, HEAD_DIM)
    queries, keys_all, values_all = (head_view[:, :, 0], head_view[:, :, 1], head_view[:, :, 2])
    attended, log_sums = attention_forward(queries, keys_all, values_all, segment_row_span)
    return (
        attended.reshape(length, row_count, -1).astype(jnp.bfloat16),
        log_sums,
        (queries, keys_all, values_all),
    )


def attention_project(attended_b, w_out):
    return lax.psum_scatter(
        jnp.einsum("srf,fd->srd", attended_b, w_out, preferred_element_type=jnp.float32).astype(
            jnp.bfloat16
        ),
        "tensor",
        scatter_dimension=0,
        tiled=True,
    ).astype(jnp.float32)


def attention_grad_heads(grad_middle_b, w_out):
    grad_attended = jnp.einsum(
        "srd,fd->srf",
        lax.all_gather(grad_middle_b, "tensor", axis=0, tiled=True),
        w_out,
        preferred_element_type=jnp.float32,
    )
    return grad_attended.astype(jnp.bfloat16)


def mlp_pre(normed_b, w_fc):
    return jnp.einsum(
        "srd,df->srf",
        lax.all_gather(normed_b, "tensor", axis=0, tiled=True),
        w_fc,
        preferred_element_type=jnp.float32,
    )


def mlp_out(hidden_b, w_proj):
    return lax.psum_scatter(
        jnp.einsum("srf,fd->srd", hidden_b, w_proj, preferred_element_type=jnp.float32).astype(
            jnp.bfloat16
        ),
        "tensor",
        scatter_dimension=0,
        tiled=True,
    ).astype(jnp.float32)


def mlp_back(grad_mlp, pre_act, w_fc, w_proj):
    grad_hidden = jnp.einsum(
        "srd,fd->srf",
        lax.all_gather(grad_mlp, "tensor", axis=0, tiled=True),
        w_proj,
        preferred_element_type=jnp.float32,
    )
    activated, slope = jax.vjp(gelu_tanh, pre_act)
    grad_pre = slope(grad_hidden)[0].astype(jnp.bfloat16)
    return lax.psum_scatter(
        jnp.einsum("srf,df->srd", grad_pre, w_fc, preferred_element_type=jnp.float32).astype(
            jnp.bfloat16
        ),
        "tensor",
        scatter_dimension=0,
        tiled=True,
    ).astype(jnp.float32)


def forward_layer_step(layer_input_rows, segment_row_span, fixed_weights, adapter_pair):
    norm_rows = normalize(layer_input_rows, fixed_weights[0])[0].astype(jnp.bfloat16)
    stacked_weights = projected_rows(
        lax.all_gather(norm_rows, "tensor", axis=0, tiled=True), fixed_weights[1], adapter_pair
    )[0]
    attended_b = attend_all(stacked_weights, segment_row_span)[0]
    middle = layer_input_rows + attention_project(attended_b, fixed_weights[2])
    normed_mlp = normalize(middle, fixed_weights[3])[0].astype(jnp.bfloat16)
    pre_act = mlp_pre(normed_mlp, fixed_weights[4])
    hidden_b = gelu_tanh(pre_act).astype(jnp.bfloat16)
    return middle + mlp_out(hidden_b, fixed_weights[5])


def backward_layer_step(
    layer_input_rows, segment_row_span, upstream_gradient, fixed_weights, adapter_pair
):
    gain_a, joint_projection_weight, w_out, gain_m, w_fc, w_proj = fixed_weights
    query_down_factor, query_up_factor, value_down_factor, value_up_factor = adapter_pair
    factor = 32.0 / query_down_factor.shape[-1]
    norm_rows, unit_first, inverse_first = normalize(layer_input_rows, gain_a)
    collected_rows = lax.all_gather(norm_rows.astype(jnp.bfloat16), "tensor", axis=0, tiled=True)
    stacked_weights, narrow_query_rows, narrow_value_rows = projected_rows(
        collected_rows, joint_projection_weight, adapter_pair
    )
    length, row_count = (collected_rows.shape[0], collected_rows.shape[1])
    attended_b, log_sums, head_views = attend_all(stacked_weights, segment_row_span)
    queries, keys_all, values_all = head_views
    middle = layer_input_rows + attention_project(attended_b, w_out)
    normed_mlp, unit_second, inverse_second = normalize(middle, gain_m)
    pre_act = mlp_pre(normed_mlp.astype(jnp.bfloat16), w_fc)
    grad_norm_mlp = mlp_back(upstream_gradient.astype(jnp.bfloat16), pre_act, w_fc, w_proj)
    grad_middle = upstream_gradient + normalize_back(
        grad_norm_mlp, unit_second, inverse_second, gain_m
    )
    grad_attended = attention_grad_heads(grad_middle.astype(jnp.bfloat16), w_out)
    grad_heads = grad_attended.reshape(queries.shape)
    grad_queries, grad_keys, grad_values = attention_backward(
        queries, keys_all, values_all, segment_row_span, log_sums, grad_heads
    )
    grad_stack = (
        jnp.stack([grad_queries, grad_keys, grad_values], axis=2)
        .astype(jnp.bfloat16)
        .reshape(length, row_count, 3, -1)
    )
    grad_query_rows = grad_stack[:, :, 0]
    grad_value_rows = grad_stack[:, :, 2]
    thin_grad_query = factor * jnp.einsum(
        "srf,kf->srk", grad_query_rows, query_up_factor, preferred_element_type=jnp.float32
    )
    thin_grad_value = factor * jnp.einsum(
        "srf,kf->srk", grad_value_rows, value_up_factor, preferred_element_type=jnp.float32
    )
    grad_bq = factor * jnp.einsum(
        "srk,srf->kf", narrow_query_rows, grad_query_rows.astype(jnp.float32), precision=PRECISE
    )
    grad_bv = factor * jnp.einsum(
        "srk,srf->kf", narrow_value_rows, grad_value_rows.astype(jnp.float32), precision=PRECISE
    )
    gathered_wide = collected_rows.astype(jnp.float32)
    grad_aq = jnp.einsum("srd,srk->dk", gathered_wide, thin_grad_query, precision=PRECISE)
    grad_av = jnp.einsum("srd,srk->dk", gathered_wide, thin_grad_value, precision=PRECISE)
    a_query_wide = query_down_factor.astype(jnp.float32)
    a_value_wide = value_down_factor.astype(jnp.float32)
    term = jnp.einsum(
        "srcf,dcf->srd", grad_stack, joint_projection_weight, preferred_element_type=jnp.float32
    )
    term = term + jnp.einsum("srk,dk->srd", thin_grad_query, a_query_wide, precision=PRECISE)
    grad_norm_attn = lax.psum_scatter(
        (term + jnp.einsum("srk,dk->srd", thin_grad_value, a_value_wide, precision=PRECISE)).astype(
            jnp.bfloat16
        ),
        "tensor",
        scatter_dimension=0,
        tiled=True,
    ).astype(jnp.float32)
    layer_output_rows = grad_middle + normalize_back(
        grad_norm_attn, unit_first, inverse_first, gain_a
    )
    return (layer_output_rows, (grad_aq, grad_bq, grad_av, grad_bv))


def body(
    inputs,
    segments,
    cotangent,
    gain_attn,
    joint_projection_weight,
    query_down_factor,
    query_up_factor,
    value_down_factor,
    value_up_factor,
    w_out,
    gain_mlp,
    w_fc,
    w_proj,
):
    fixed_weights = (
        gain_attn[0],
        joint_projection_weight[0],
        w_out[0],
        gain_mlp[0],
        w_fc[0],
        w_proj[0],
    )
    adapter_pair = (
        query_down_factor[0],
        query_up_factor[0],
        value_down_factor[0],
        value_up_factor[0],
    )
    sections = lax.axis_size("section")
    section_index = lax.axis_index("section")
    is_first = section_index == 0
    is_last = section_index == sections - 1
    rows_mb = inputs.shape[1] // MICRO
    ticks = MICRO + sections - 1
    block_shape = (inputs.shape[0], rows_mb, inputs.shape[2])
    activations = jnp.zeros_like(inputs)
    kept_inputs = jnp.zeros((MICRO,) + block_shape, jnp.bfloat16)
    arriving = jnp.zeros(block_shape, jnp.bfloat16)
    for tick_index in range(ticks):
        own_index = min(tick_index, MICRO - 1)
        mb_slot = tick_index - section_index
        is_valid = (mb_slot >= 0) & (mb_slot < MICRO)
        mb_slot = jnp.clip(mb_slot, 0, MICRO - 1)
        fresh = lax.slice_in_dim(inputs, own_index * rows_mb, (own_index + 1) * rows_mb, axis=1)
        layer_input_rows = jnp.where(is_first, fresh, arriving)
        segment_row_span = lax.dynamic_slice_in_dim(segments, mb_slot * rows_mb, rows_mb, 0)
        layer_output_rows = forward_layer_step(
            layer_input_rows.astype(jnp.float32), segment_row_span, fixed_weights, adapter_pair
        ).astype(jnp.bfloat16)
        activations = jnp.where(
            is_valid,
            lax.dynamic_update_slice_in_dim(activations, layer_output_rows, mb_slot * rows_mb, 1),
            activations,
        )
        kept_inputs = jnp.where(
            is_valid, kept_inputs.at[mb_slot].set(layer_input_rows), kept_inputs
        )
        if tick_index < ticks - 1:
            arriving = passed_along(layer_output_rows, "section", 1)
    input_grads = jnp.zeros_like(inputs)
    gradient_totals = tuple(
        (jnp.zeros(factor_tensor.shape, jnp.float32) for factor_tensor in adapter_pair)
    )
    arriving = jnp.zeros(block_shape, jnp.bfloat16)
    for tick_index in range(ticks):
        own_index = min(tick_index, MICRO - 1)
        mb_slot = tick_index - (sections - 1 - section_index)
        is_valid = (mb_slot >= 0) & (mb_slot < MICRO)
        mb_slot = jnp.clip(mb_slot, 0, MICRO - 1)
        given = lax.slice_in_dim(cotangent, own_index * rows_mb, (own_index + 1) * rows_mb, axis=1)
        upstream_gradient = jnp.where(is_last, given, arriving).astype(jnp.float32)
        layer_input_rows = kept_inputs[mb_slot].astype(jnp.float32)
        segment_row_span = lax.dynamic_slice_in_dim(segments, mb_slot * rows_mb, rows_mb, 0)
        layer_output_rows, row_pieces = backward_layer_step(
            layer_input_rows, segment_row_span, upstream_gradient, fixed_weights, adapter_pair
        )
        leaving_b = layer_output_rows.astype(jnp.bfloat16)
        input_grads = jnp.where(
            is_valid,
            lax.dynamic_update_slice_in_dim(input_grads, leaving_b, mb_slot * rows_mb, 1),
            input_grads,
        )
        gradient_totals = tuple(
            (
                running + jnp.where(is_valid, piece_grad, 0.0)
                for running, piece_grad in zip(gradient_totals, row_pieces)
            )
        )
        if tick_index < ticks - 1:
            arriving = passed_along(leaving_b, "section", -1)
    adapter_rank = adapter_pair[1].shape[0]
    model_width = inputs.shape[2]
    column_total = adapter_pair[1].shape[1]
    offset = lax.axis_index("tensor") * column_total
    full_query = lax.dynamic_update_slice_in_dim(
        jnp.zeros((adapter_rank, model_width), jnp.float32), gradient_totals[1], offset, 1
    )
    full_value = lax.dynamic_update_slice_in_dim(
        jnp.zeros((adapter_rank, model_width), jnp.float32), gradient_totals[3], offset, 1
    )
    summed = lax.psum(
        (gradient_totals[0], full_query, gradient_totals[2], full_value), ("dp", "tensor")
    )
    return (
        activations[None],
        input_grads[None],
        summed[0][None],
        summed[1][None],
        summed[2][None],
        summed[3][None],
    )


REACH = 512
BF16 = jnp.bfloat16
F32 = jnp.float32
MESH = pl.DeviceIdType.MESH


def dot_nn(a, b):
    return lax.dot_general(a, b, (((1,), (0,)), ((), ())), preferred_element_type=F32)


def dot_nt(a, b):
    return lax.dot_general(a, b, (((1,), (1,)), ((), ())), preferred_element_type=F32)


def dot_tn(a, b):
    return lax.dot_general(a, b, (((0,), (0,)), ((), ())), preferred_element_type=F32)


def norm_stats(rows):
    middle = jnp.mean(rows, axis=-1, keepdims=True)
    centred = rows - middle
    inverse = lax.rsqrt(jnp.mean(centred * centred, axis=-1, keepdims=True) + EPSILON)
    return centred * inverse, inverse


def gelu_slope(pre):
    square = pre * pre
    bent = jnp.tanh(TANH_SCALE * (pre + CUBIC_TERM * square * pre))
    return 0.5 * (1.0 + bent) + (0.5 * TANH_SCALE) * pre * (1.0 - bent * bent) * (
        1.0 + (3.0 * CUBIC_TERM) * square
    )


def key_span(i, block):
    return max(0, i - REACH // block) * block, (i + 1) * block


def allowed_keys(i, block, seg_col_ref, seg_row_ref):
    low, high = key_span(i, block)
    seg_k = seg_col_ref[low:high, :]
    seg_q = seg_row_ref[:, i * block : (i + 1) * block]
    places_k = low + lax.broadcasted_iota(jnp.int32, (high - low, block), 0)
    places_q = i * block + lax.broadcasted_iota(jnp.int32, (high - low, block), 1)
    return (seg_q == seg_k) & (places_k <= places_q)


def head_lanes(rows, h):
    lane = lax.broadcasted_iota(jnp.int32, (rows, 128), 1)
    return (lane < HEAD_DIM) if h == 0 else (lane >= HEAD_DIM)


def both_halves(ref, *index):
    return jnp.concatenate([ref[(*index, 0)], ref[(*index, 1)]], axis=1)


class Wires:
    def __init__(self, send, recv):
        self.send, self.recv, self.count, self.sent = send, recv, 0, []

    def copy(self, source, target, where):
        k = self.count
        self.count += 1
        made = pltpu.make_async_remote_copy(
            src_ref=source,
            dst_ref=target,
            send_sem=self.send.at[k],
            recv_sem=self.recv.at[k],
            device_id=where,
            device_id_type=MESH,
        )
        self.sent.append(made)
        return made

    def forget(self, copy):
        self.sent = [one for one in self.sent if one is not copy]


class Totals:
    def __init__(self, wires, layer, out_ref, in_ref, hops):
        self.out_ref, self.in_ref, self.layer, self.at = out_ref, in_ref, layer, 0
        self.hops = [
            wires.copy(out_ref.at[layer, k], in_ref.at[layer, k], peer)
            for k, peer in enumerate(hops)
        ]
        self.wires = wires
        self.hops[0].start()

    def step(self):
        k, layer = self.at, self.layer
        self.hops[k].wait_recv()
        summed = self.out_ref[layer, k] + self.in_ref[layer, k]
        self.at = k + 1
        if self.at < len(self.hops):
            self.out_ref[layer, self.at] = summed
            self.hops[self.at].start()
        else:
            self.hops[0].wait_send()
            self.wires.forget(self.hops[0])
            self.out_ref[layer, 0] = summed

    def finish(self):
        while self.at < len(self.hops):
            self.step()


WIRES = 128


def step_kernel(
    block,
    model,
    planes,
    x_rows,
    cot_rows,
    seg_rows,
    gain_a,
    gain_m,
    downs_t,
    up_q,
    up_v,
    wq,
    wo,
    fc,
    proj,
    act_out,
    grad_out,
    sums_out,
    act,
    grad,
    xb,
    cb,
    seg_col,
    seg_row,
    sm,
    up,
    pad,
    wq_all,
    up_all,
    wo_all,
    ff,
    rows,
    thin,
    qkv,
    o_out,
    o_in,
    middle,
    norm2,
    pre,
    part_out,
    part_in,
    own_sum,
    do_in,
    dqkv,
    dk_acc,
    dv_acc,
    c_out,
    c_in,
    y_out,
    y_in,
    down_sums,
    up_sums,
    total_out,
    total_in,
    wire_send,
    wire_recv,
    row_send,
    row_recv,
    wq_send,
    wq_recv,
    wq_half,
    local_sem,
    o_send,
    o_recv,
    place_send,
    place_recv,
):
    c = lax.axis_index("section")
    z = lax.axis_index("dp")
    t = lax.axis_index("tensor")
    y, x = lax.div(t, 2), lax.rem(t, 2)
    over_x, over_y = 2 * y + (1 - x), 2 * (1 - y) + x
    mine, twin = 2 * y + c, 2 * y + (1 - c)
    far, far_twin = 2 * (1 - y) + c, 2 * (1 - y) + (1 - c)
    to_c, to_x, to_y = {"section": 1 - c}, {"tensor": over_x}, {"tensor": over_y}
    to_xc = {"section": 1 - c, "tensor": over_x}
    to_yc = {"section": 1 - c, "tensor": over_y}
    to_zs = []
    bit = 1
    while bit < planes:
        up_bit = lax.rem(lax.div(z, bit), 2)
        to_zs.append({"dp": z + bit - 2 * bit * up_bit})
        bit *= 2
    to_z = to_zs[0]
    odd = lax.rem(z, 2)
    here = c == x
    wires = Wires(wire_send, wire_recv)
    width = wq.shape[2]
    factor = 8.0

    barrier = pltpu.get_barrier_semaphore()
    peers = [to_c, to_x, to_y, to_xc, to_yc, *to_zs]
    for peer in peers:
        pl.semaphore_signal(barrier, inc=1, device_id=peer, device_id_type=MESH)
    pl.semaphore_wait(barrier, len(peers))

    def part(which, count):
        first = odd if which == 0 else 1 - odd
        return pl.ds(pl.multiple_of(first * (count // 2), count // 2), count // 2)

    def row_copy(source, target, k):
        return pltpu.make_async_remote_copy(
            src_ref=source,
            dst_ref=target,
            send_sem=row_send.at[k],
            recv_sem=row_recv.at[k],
            device_id=to_x,
            device_id_type=MESH,
        )

    x_copy = row_copy(x_rows.at[1 - x], xb, 0)
    cot_local = pltpu.make_async_copy(cot_rows.at[x], cb.at[0], row_recv.at[1])

    @pl.when(here)
    def _():
        x_copy.start()
        cot_local.start()
        pltpu.make_async_copy(x_rows.at[x], xb, row_recv.at[0]).start()

    pad[...] = jnp.zeros_like(pad)
    pad[0:4] = up_q[...].astype(F32)
    up[0] = pad[...].astype(BF16)
    pad[0:4] = jnp.zeros((4, width), F32)
    pad[4:8] = up_v[...].astype(F32)
    up[1] = pad[...].astype(BF16)

    def wq_twin():
        return [
            pltpu.make_async_remote_copy(
                src_ref=source,
                dst_ref=target.at[c],
                send_sem=wq_send.at[0, j],
                recv_sem=wq_recv.at[c, j],
                device_id=to_c,
                device_id_type=MESH,
            )
            for j, (source, target) in enumerate(((wq, wq_all), (up, up_all)))
        ]

    def wq_over_x():
        cut = part(0, model)
        where = {"section": x, "tensor": over_x}
        made = [
            pltpu.make_async_remote_copy(
                src_ref=wq.at[k, cut],
                dst_ref=wq_all.at[c, k, cut],
                send_sem=wq_send.at[1, k],
                recv_sem=wq_half.at[c, 0, k],
                device_id=where,
                device_id_type=MESH,
            )
            for k in range(3)
        ]
        made.append(
            pltpu.make_async_remote_copy(
                src_ref=up,
                dst_ref=up_all.at[c],
                send_sem=wq_send.at[0, 2],
                recv_sem=wq_recv.at[c, 1],
                device_id=where,
                device_id_type=MESH,
            )
        )
        return made

    def wq_over_z(layer):
        cut = part(0, model)
        return [
            pltpu.make_async_remote_copy(
                src_ref=wq_all.at[layer, k, cut],
                dst_ref=wq_all.at[layer, k, cut],
                send_sem=wq_send.at[2 + layer, k],
                recv_sem=wq_half.at[layer, 1, k],
                device_id=to_z,
                device_id_type=MESH,
            )
            for k in range(3)
        ]

    def wq_local(layer):
        return [
            pltpu.make_async_copy(source, target.at[layer], wq_recv.at[layer, j])
            for j, (source, target) in enumerate(((wq, wq_all), (up, up_all)))
        ]

    def send_wq_far(layer, pieces):
        @pl.when(c == layer)
        def _():
            copies = wq_over_x()
            for k in pieces:
                copies[k].start()

    def send_wq_near():
        @pl.when(here)
        def _():
            for copy in wq_local(c):
                copy.start()

        @pl.when(jnp.logical_not(here))
        def _():
            for copy in wq_twin():
                copy.start()

    def half_wait(layer, which, k):
        cut = part(which, model)
        pltpu.make_async_copy(
            wq.at[k, cut], wq_all.at[layer, k, cut], wq_half.at[layer, which, k]
        ).wait()

    def pass_wq(layer):
        @pl.when(jnp.logical_not(here))
        def _():
            for k, copy in enumerate(wq_over_z(layer)):
                half_wait(layer, 0, k)
                copy.start()

    def arrived_wq(layer):
        whole, small = wq_local(layer)
        small.wait()
        pl.when(here)(whole.wait)

        @pl.when(jnp.logical_not(here))
        def _():
            for k in range(3):
                half_wait(layer, 1, k)

    def sent_wq():
        for copy in wq_over_x():
            copy.wait_send()

        @pl.when(jnp.logical_not(here))
        def _():
            for copy in wq_twin():
                copy.wait_send()
            for layer in range(2):
                for copy in wq_over_z(layer):
                    copy.wait_send()

    send_wq_far(0, (3, 0, 1, 2))
    pl.when(c == 0)(send_wq_near)

    sm[c, 0:1] = gain_a[...]
    sm[c, 8:9] = gain_m[...]
    sm[c, 16:24] = downs_t[...].astype(F32)
    sm[c, 24:32] = jnp.zeros((8, model), F32)
    small_copy = wires.copy(sm.at[c], sm.at[c], to_c)
    small_copy.start()
    seg_row[...] = seg_rows[pl.ds(x, 1), :]
    same = lax.broadcasted_iota(jnp.int32, (128, 128), 0) == lax.broadcasted_iota(
        jnp.int32, (128, 128), 1
    )
    for k in range(4 * block // 128):
        lanes = slice(k * 128, (k + 1) * 128)
        seg_col[lanes, :] = jnp.sum(
            jnp.where(same, seg_row[:, lanes], 0), axis=1, keepdims=True
        )

    locals_ = [
        pltpu.make_async_copy(source, target, local_sem.at[k])
        for k, (source, target) in enumerate(
            ((fc, ff.at[c, 0, 0]), (proj, ff.at[c, 1, 0]), (wo, wo_all.at[c, t]))
        )
    ]
    piece = model // 4

    def ff_rows(p, which):
        first = odd if which == 0 else 1 - odd
        return pl.ds(pl.multiple_of(first * (model // 2) + (p % 2) * piece, piece), piece)

    def ff_same(p, which, where):
        at = ff.at[c, p // 2, 1, ff_rows(p, which)]
        return wires.copy(at, at, where)

    ff_twin = [wires.copy(one, ff.at[c, k, 0], to_c) for k, one in enumerate((fc, proj))]
    ff_x = [
        wires.copy(
            (fc, proj)[p // 2].at[ff_rows(p, 0)], ff.at[c, p // 2, 1, ff_rows(p, 0)], to_x
        )
        for p in range(4)
    ]
    ff_z = [ff_same(p, 0, to_z) for p in range(4)]
    ff_c = [[ff_same(p, which, to_c) for which in range(2)] for p in range(4)]

    def start_ff(layer):
        @pl.when(c == layer)
        def _():
            for copy in ff_x:
                copy.start()

    def pass_ff_x(layer, p):
        @pl.when(c == layer)
        def _():
            ff_x[p].wait_recv()
            ff_z[p].start()
            ff_c[p][0].start()

    def pass_ff_z(layer, p):
        @pl.when(c == layer)
        def _():
            ff_z[p].wait_recv()
            ff_c[p][1].start()

    def arrived_ff(layer):
        @pl.when(c != layer)
        def _():
            for pair in ff_c:
                for copy in pair:
                    copy.wait_recv()

    corner = 2 * (1 - y) + (1 - x)
    wo_cut = part(0, width)
    quart = width // 4
    wo_low = pl.ds(pl.multiple_of(odd * (width // 2), quart), quart)
    wo_high = pl.ds(pl.multiple_of(odd * (width // 2) + quart, quart), quart)

    def wo_same(q, cut, where):
        if cut is None:
            return wires.copy(wo_all.at[c, q], wo_all.at[c, q], where)
        return wires.copy(wo_all.at[c, q, cut], wo_all.at[c, q, cut], where)

    wo_twin = wires.copy(wo, wo_all.at[c, t], to_c)
    wo_x = wires.copy(wo.at[wo_cut], wo_all.at[c, t, wo_cut], to_x)
    wo_y = wires.copy(wo.at[wo_cut], wo_all.at[c, t, wo_cut], to_y)
    wo_dy = wo_same(over_x, wo_low, to_y)
    wo_dx = wo_same(over_y, wo_high, to_x)
    wo_z = [wo_same(q, wo_cut, to_z) for q in (over_x, over_y, corner)]
    wo_c = [wo_same(q, None, to_c) for q in (over_x, over_y, corner)]

    def start_wo_x(layer):
        pl.when(c == layer)(wo_x.start)

    def start_wo_y(layer):
        pl.when(c == layer)(wo_y.start)

    def pass_wo(layer, stage):
        @pl.when(c == layer)
        def _():
            if stage == 0:
                wo_x.wait_recv()
                wo_dy.start()
                wo_z[0].start()
                wo_y.wait_recv()
                wo_dx.start()
                wo_z[1].start()
            if stage == 1:
                wo_dy.wait_recv()
                wo_dx.wait_recv()
                wo_z[2].start()
            if stage == 2:
                for came, onward in zip(wo_z, wo_c):
                    came.wait_recv()
                    onward.start()

    def arrived_wo(layer):
        @pl.when(c == layer)
        def _():
            locals_[2].wait()

        @pl.when(c != layer)
        def _():
            wo_twin.wait_recv()
            for copy in wo_c:
                copy.wait_recv()

    for copy in locals_:
        copy.start()
    for copy in ff_twin + [wo_twin]:
        copy.start()
    start_wo_x(0)
    start_ff(0)

    def place_copy(kind, layer, source, target, at=slice(None)):
        return pltpu.make_async_remote_copy(
            src_ref=source.at[at],
            dst_ref=target.at[x, at],
            send_sem=place_send.at[kind, layer],
            recv_sem=place_recv.at[kind, x],
            device_id={"section": layer, "tensor": mine},
            device_id_type=MESH,
        )

    def place(kind, layer, source, target, at=slice(None)):
        stays = jnp.logical_and(here, c == layer)

        @pl.when(stays)
        def _():
            target[x, at] = source[at]

        @pl.when(jnp.logical_not(stays))
        def _():
            place_copy(kind, layer, source, target, at).start()

    def placed(kind, source, target):
        for layer in range(2):
            stays = jnp.logical_and(here, c == layer)

            @pl.when(jnp.logical_not(stays))
            def _():
                place_copy(kind, layer, source.at[layer], target).wait_send()

        for slot in range(2):
            came = jnp.logical_not(jnp.logical_and(here, x == slot))

            @pl.when(came)
            def _():
                pltpu.make_async_copy(
                    source.at[0], target.at[slot], place_recv.at[kind, slot]
                ).wait()

    def qkv_block(layer, b):
        normed = rows[layer, b]
        down = sm[layer, 16:32, :].astype(BF16)
        low = dot_nt(normed, down)
        low_b = low.astype(BF16)
        thin[layer, b] = low_b
        at = pl.ds(pl.multiple_of(b * block, block), block)
        for k in range(3):
            made = dot_nn(normed, wq_all[layer, k])
            if k == 0:
                made = made + factor * dot_nn(low_b, up_all[layer, 0])
            if k == 2:
                made = made + factor * dot_nn(low_b, up_all[layer, 1])
            made = made.astype(BF16)
            qkv[layer, k, 0, at, :] = made[:, :128]
            qkv[layer, k, 1, at, :] = made[:, 128:]

    def attend(layer, i):
        low, high = key_span(i, block)
        at = slice(i * block, (i + 1) * block)
        allowed = allowed_keys(i, block, seg_col, seg_row)

        def one_pair(pair, carry):
            queries = qkv[layer, 0, pair, at, :] * BF16(HEAD_DIM**-0.5)
            keys = qkv[layer, 1, pair, low:high, :]
            values = qkv[layer, 2, pair, low:high, :]
            parts = []
            for h in range(2):
                picked = jnp.where(head_lanes(block, h), queries, BF16(0))
                scores = jnp.where(allowed, dot_nt(keys, picked), MASKED)
                exponent = jnp.exp(scores - jnp.max(scores, axis=0, keepdims=True))
                total = jnp.sum(exponent, axis=0, keepdims=True)
                made = dot_tn(values, exponent.astype(BF16))
                parts.append(made[h * HEAD_DIM : (h + 1) * HEAD_DIM] / total)
            o_out[i, pair] = jnp.concatenate(parts, axis=0).T.astype(BF16)
            return carry

        lax.fori_loop(0, 2, one_pair, 0)

    def exchange_piece(i, target, phase):
        return pltpu.make_async_remote_copy(
            src_ref=o_out.at[i],
            dst_ref=target.at[mine],
            send_sem=o_send.at[i],
            recv_sem=o_recv.at[phase, mine],
            device_id={"section": i % 2, "tensor": 2 * (i // 2) + x},
            device_id_type=MESH,
        )

    def send_piece(i, target, phase):
        @pl.when(mine == i)
        def _():
            target[mine] = o_out[i]

        @pl.when(mine != i)
        def _():
            exchange_piece(i, target, phase).start()

    def wait_pieces(target, phase):
        for i in range(4):

            @pl.when(mine != i)
            def _():
                exchange_piece(i, target, phase).wait_send()
                pltpu.make_async_copy(o_out.at[i], target.at[i], o_recv.at[phase, i]).wait()

    def hidden_half(layer, who, source, q):
        total = None
        for cut in range(2):
            lanes = slice(cut * model // 2, (cut + 1) * model // 2)
            made = dot_nn(source, ff[layer, 0, q, :, lanes])
            pre[layer, who, q, :, lanes] = made.astype(BF16)
            term = dot_nn(gelu_tanh(made).astype(BF16), ff[layer, 1, q, lanes, :])
            total = term if total is None else total + term
        return total

    def hidden_back(layer, who, upstream, q):
        total = None
        for cut in range(2):
            lanes = slice(cut * model // 2, (cut + 1) * model // 2)
            grad_hidden = dot_nt(upstream, ff[layer, 1, q, lanes, :])
            slope = gelu_slope(pre[layer, who, q, :, lanes].astype(F32))
            term = dot_nt((grad_hidden * slope).astype(BF16), ff[layer, 0, q, :, lanes])
            total = term if total is None else total + term
        return total

    cuts = [
        (q, slice(cut * model // 2, (cut + 1) * model // 2)) for q in range(2) for cut in range(2)
    ]
    half_rows = [slice(h * block // 2, (h + 1) * block // 2) for h in range(2)]

    def in_halves(source, target, where):
        return [wires.copy(source(at), target(at), where) for at in half_rows]

    def give_rows(layer, h, source):
        at = half_rows[h]
        unit, _ = norm_stats(source[at, :].astype(F32))
        rows[layer, mine, at] = (unit * sm[layer, 0:1, :]).astype(BF16)
        row_y[layer][h].start()
        row_c[layer][h].start()

    row_y, row_c, row_yc = [], [], []
    for layer in range(2):
        for store, b, where in ((row_y, mine, to_y), (row_c, mine, to_c), (row_yc, far, to_c)):
            store.append(
                in_halves(
                    lambda at: rows.at[layer, b, at], lambda at: rows.at[layer, b, at], where
                )
            )

    pltpu.make_async_copy(x_rows.at[x], xb, row_recv.at[0]).wait()
    small_copy.wait_recv()
    cot_x = row_copy(cot_rows.at[1 - x], cb.at[0], 1)
    cot_y = wires.copy(cb.at[0], cb.at[1], to_y)

    for layer in range(2):
        source = xb if layer == 0 else act.at[0]
        if layer == 0:
            for h in range(2):
                give_rows(0, h, xb)
            pass_wq(0)
        else:
            pass_wo(1, 1)
            pass_ff_x(1, 2)
        arrived_wq(layer)
        qkv_block(layer, mine)
        if layer == 1:
            pass_ff_x(1, 3)
            pass_wo(1, 2)
            place(0, 0, act.at[0], act_out)
        for copy in row_c[layer]:
            copy.wait_recv()
        qkv_block(layer, twin)
        for copy, onward in zip(row_y[layer], row_yc[layer]):
            copy.wait_recv()
            onward.start()
        if layer == 0:
            start_wo_y(0)

            @pl.when(here)
            def _():
                cot_local.wait()
                cot_y.start()
        else:

            @pl.when(jnp.logical_not(here))
            def _():
                cot_local.wait()
                cot_y.start()
        qkv_block(layer, far)
        for copy in row_yc[layer]:
            copy.wait_recv()
        qkv_block(layer, far_twin)
        if layer == 0:
            pass_ff_x(0, 0)
        for i in range(4):
            attend(layer, i)
            send_piece(i, o_in, layer)
            if layer == 0 and i == 0:
                pass_wo(0, 0)
            if layer == 0 and i == 2:
                pass_wo(0, 1)
                pass_ff_x(0, 1)
            if layer == 0 and i == 3:
                pass_wo(0, 2)
            if layer == 1 and i >= 2:
                pass_ff_z(1, i - 2)
        arrived_wo(layer)
        wait_pieces(o_in, layer)
        if layer == 0:
            pass_ff_x(0, 2)
        else:
            pass_ff_z(1, 2)
        stream = source[...].astype(F32)
        for q in range(4):
            stream = stream + dot_nn(both_halves(o_in, q), wo_all[layer, q])
        middle[layer] = stream
        unit, _ = norm_stats(stream)
        norm2[0] = (unit * sm[layer, 8:9, :]).astype(BF16)
        norm_y = wires.copy(norm2.at[0], norm2.at[1], to_y)
        norm_y.start()
        if layer == 0:
            for copy in locals_[:2]:
                copy.wait()
            for copy in ff_twin:
                copy.wait_recv()
            pass_ff_z(0, 0)
            pass_ff_x(0, 3)
            pl.when(c == 1)(send_wq_near)
            send_wq_far(1, (3, 0, 1, 2))
            start_wo_x(1)
            start_wo_y(1)
            start_ff(1)
            pass_ff_z(0, 1)
        else:
            pass_ff_z(1, 3)
        own_sum[...] = hidden_half(layer, 0, norm2[0], 0)
        if layer == 0:
            pass_ff_z(0, 2)
            pass_ff_z(0, 3)
            pass_wq(1)
        arrived_ff(layer)
        own_sum[...] += hidden_half(layer, 0, norm2[0], 1)
        if layer == 1:
            grad[0] = own_sum[...].astype(BF16)
            own_sum[...] = hidden_back(1, 0, cb[0], 0) + hidden_back(1, 0, cb[0], 1)
            cot_y.wait_recv()
            for q in range(2):
                c_out[q] = dot_nt(cb[1], ff[1, 1, q]).astype(BF16)
        norm_y.wait_recv()
        if layer == 0:
            away = hidden_half(0, 1, norm2[1], 0) + hidden_half(0, 1, norm2[1], 1)
        else:
            away = None
            for q, lanes in cuts:
                made = dot_nn(norm2[1], ff[1, 0, q, :, lanes])
                pre[1, 1, q, :, lanes] = made.astype(BF16)
                grad_pre = (c_out[q, :, lanes].astype(F32) * gelu_slope(made)).astype(BF16)
                term = dot_nt(grad_pre, ff[1, 0, q, :, lanes])
                away = term if away is None else away + term
        part_out[...] = away.astype(BF16)
        part_y = in_halves(
            lambda at: part_out.at[at], lambda at: part_in.at[layer, at], to_y
        )
        for copy in part_y:
            copy.start()
        if layer == 1:
            late = None
            for q, lanes in cuts:
                hidden = gelu_tanh(pre[1, 1, q, :, lanes].astype(F32)).astype(BF16)
                term = dot_nn(hidden, ff[1, 1, q, lanes, :])
                late = term if late is None else late + term
            y_out[...] = late.astype(BF16)
        if layer == 0:
            stream = middle[layer] + own_sum[...]
            pass_wo(1, 0)
            pass_ff_x(1, 0)
            pass_ff_x(1, 1)

            pl.when(here)(cot_x.start)
            for h, at in enumerate(half_rows):
                part_y[h].wait()
                wires.forget(part_y[h])
                act[0, at] = (stream[at] + part_in[0, at].astype(F32)).astype(BF16)
                give_rows(1, h, act.at[0])
            norm_y.wait_send()
            wires.forget(norm_y)

    for layer in (1, 0):
        upstream = cb[0] if layer == 1 else grad[1]
        if layer == 0:
            own_sum[...] = hidden_back(layer, 0, upstream, 0) + hidden_back(layer, 0, upstream, 1)
            for copy in up_y:
                copy.wait_recv()
            totals.step()
            away = hidden_back(layer, 1, norm2[1], 0) + hidden_back(layer, 1, norm2[1], 1)
            part_out[...] = away.astype(BF16)
            part_y = in_halves(
                lambda at: part_out.at[at], lambda at: part_in.at[1, at], to_y
            )
            for copy in part_y:
                copy.start()
        unit, inverse = norm_stats(middle[layer])
        for copy in part_y:
            copy.wait()
            wires.forget(copy)
        if layer == 0:
            totals.step()
        grad_norm = own_sum[...] + part_in[1].astype(F32)
        grad_middle = upstream.astype(F32) + normalize_back(
            grad_norm, unit, inverse, sm[layer, 8:9, :]
        )
        own_sum[...] = grad_middle
        grad_b = grad_middle.astype(BF16)
        for q in range(4):
            made = dot_nt(grad_b, wo_all[layer, q]).astype(BF16)
            o_out[q, 0] = made[:, :128]
            o_out[q, 1] = made[:, 128:]
            send_piece(q, do_in, 2 + layer)
        if layer == 0:
            place(1, 1, grad.at[1], grad_out)
        else:
            late_y = wires.copy(y_out, part_in.at[0], to_y)
            late_y.start()
        wait_pieces(do_in, 2 + layer)
        if layer == 0:
            totals.step()

        def back_pair(pair, carry):
            dk_acc[...] = jnp.zeros_like(dk_acc)
            dv_acc[...] = jnp.zeros_like(dv_acc)
            for i in range(4):
                low, high = key_span(i, block)
                at = slice(i * block, (i + 1) * block)
                allowed = allowed_keys(i, block, seg_col, seg_row)
                queries = qkv[layer, 0, pair, at, :] * BF16(HEAD_DIM**-0.5)
                keys = qkv[layer, 1, pair, low:high, :]
                values = qkv[layer, 2, pair, low:high, :]
                grads = do_in[i, pair]
                parts = []
                for h in range(2):
                    lanes = head_lanes(block, h)
                    picked = jnp.where(lanes, queries, BF16(0))
                    given = jnp.where(lanes, grads, BF16(0))
                    scores = jnp.where(allowed, dot_nt(keys, picked), MASKED)
                    exponent = jnp.exp(scores - jnp.max(scores, axis=0, keepdims=True))
                    soft = exponent * (1.0 / jnp.sum(exponent, axis=0, keepdims=True))
                    weighted = soft * dot_nt(values, given)
                    grad_scores = (
                        weighted - soft * jnp.sum(weighted, axis=0, keepdims=True)
                    ).astype(BF16)
                    made = dot_tn(keys, grad_scores)
                    parts.append(made[h * HEAD_DIM : (h + 1) * HEAD_DIM])
                    dk_acc[low:high, :] += dot_nn(grad_scores, picked)
                    dv_acc[low:high, :] += dot_nn(soft.astype(BF16), given)
                dqkv[0, pair, at, :] = (
                    jnp.concatenate(parts, axis=0).T * HEAD_DIM**-0.5
                ).astype(BF16)
            dqkv[1, pair] = dk_acc[...].astype(BF16)
            dqkv[2, pair] = dv_acc[...].astype(BF16)
            return carry

        lax.fori_loop(0, 2, back_pair, 0)
        if layer == 1:
            late_y.wait()
            wires.forget(late_y)
            act[1] = (
                middle[1] + grad[0].astype(F32) + part_in[0].astype(F32)
            ).astype(BF16)
            place(0, 1, act.at[1], act_out)
        down = sm[layer, 16:32, :].astype(BF16)
        if layer == 0:
            totals.finish()

        def block_grad(b, first):
            at = pl.ds(pl.multiple_of(b * block, block), block)
            parts = [
                jnp.concatenate([dqkv[k, 0, at, :], dqkv[k, 1, at, :]], axis=1) for k in range(3)
            ]
            low = factor * (
                dot_nt(parts[0], up_all[layer, 0]) + dot_nt(parts[2], up_all[layer, 1])
            )
            low_b = low.astype(BF16)
            term = dot_nn(low_b, down)
            for k in range(3):
                term = term + dot_nt(parts[k], wq_all[layer, k])
            kept = thin[layer, b]
            to_down = dot_tn(low_b, rows[layer, b])
            to_up = [factor * dot_tn(kept, parts[0]), factor * dot_tn(kept, parts[2])]
            if first:
                down_sums[...] = to_down
                up_sums[0], up_sums[1] = to_up
            else:
                down_sums[...] += to_down
                up_sums[0] += to_up[0]
                up_sums[1] += to_up[1]
            return term

        c_far = wires.copy(c_out.at[0], c_in.at[0], to_c)
        c_near = wires.copy(c_out.at[1], c_in.at[1], to_c)
        y_far = in_halves(lambda at: y_out.at[at], lambda at: y_in.at[at], to_y)
        c_out[0] = block_grad(far_twin, True).astype(BF16)
        c_far.start()
        term = block_grad(far, False)
        c_far.wait_recv()
        y_out[...] = (term + c_in[0].astype(F32)).astype(BF16)
        for copy in y_far:
            copy.start()
        c_out[1] = block_grad(twin, False).astype(BF16)
        c_near.start()
        term = block_grad(mine, False)
        total_out[layer, 0, 0:8] = down_sums[0:8]
        total_out[layer, 0, 8:16] = jnp.zeros((8, model), F32)
        low_rows = lax.broadcasted_iota(jnp.int32, (8, width), 0) < 4
        total_out[
            layer, 0, 8:16, pl.ds(pl.multiple_of(mine * width, width), width)
        ] = jnp.where(low_rows, up_sums[0, 0:8], up_sums[1, 0:8])
        totals = Totals(wires, layer, total_out, total_in, [to_c, to_x, to_y, *to_zs])
        c_near.wait_recv()
        term = term + c_in[1].astype(F32)
        source = xb if layer == 0 else act.at[0]
        unit, inverse = norm_stats(source[...].astype(F32))
        if layer == 0:
            totals.step()
            totals.step()
        if layer == 1:
            up_y = in_halves(lambda at: grad.at[1, at], lambda at: norm2.at[1, at], to_y)
        for h, at in enumerate(half_rows):
            y_far[h].wait_recv()
            grad_norm = term[at] + y_in[at].astype(F32)
            grad[layer, at] = (
                own_sum[at]
                + normalize_back(grad_norm, unit[at], inverse[at], sm[layer, 0:1, :])
            ).astype(BF16)
            if layer == 1:
                up_y[h].start()
            else:
                place(1, 0, grad.at[0], grad_out, at)
                if h == 0:
                    totals.step()
                    totals.step()
        for copy in (c_far, c_near, *y_far):
            copy.wait_send()
            wires.forget(copy)

    @pl.when(here)
    def _():
        x_copy.wait_send()
        cot_x.wait_send()


    totals.finish()
    sums_out[...] = jnp.where(c == 0, total_out[0, 0], total_out[1, 0])
    sent_wq()
    for copy in wires.sent:
        copy.wait_send()
    placed(0, act, act_out)
    placed(1, grad, grad_out)


def step_call(block, model, width, planes, operands):
    slots = 4 * block
    hops = 3 + (planes - 1).bit_length()
    in_vmem = pl.BlockSpec(memory_space=pltpu.VMEM)
    in_hbm = pl.BlockSpec(memory_space=pl.ANY)
    return pl.pallas_call(
        functools.partial(step_kernel, block, model, planes),
        out_shape=(
            jax.ShapeDtypeStruct((2, block, model), BF16),
            jax.ShapeDtypeStruct((2, block, model), BF16),
            jax.ShapeDtypeStruct((16, model), F32),
        ),
        in_specs=[in_hbm] * 2 + [in_vmem] * 6 + [in_hbm] * 4,
        out_specs=[in_vmem] * 3,
        scratch_shapes=[
            pltpu.VMEM((2, block, model), BF16),
            pltpu.VMEM((2, block, model), BF16),
            pltpu.VMEM((block, model), BF16),
            pltpu.VMEM((2, block, model), BF16),
            pltpu.VMEM((slots, 1), jnp.int32),
            pltpu.VMEM((1, slots), jnp.int32),
            pltpu.VMEM((2, 32, model), F32),
            pltpu.VMEM((2, 16, width), BF16),
            pltpu.VMEM((16, width), F32),
            pltpu.VMEM((2, 3, model, width), BF16),
            pltpu.VMEM((2, 2, 16, width), BF16),
            pltpu.VMEM((2, 4, width, model), BF16),
            pltpu.VMEM((2, 2, 2, model, model), BF16),
            pltpu.VMEM((2, 4, block, model), BF16),
            pltpu.VMEM((2, 4, block, 16), BF16),
            pltpu.VMEM((2, 3, 2, slots, 128), BF16),
            pltpu.VMEM((4, 2, block, 128), BF16),
            pltpu.VMEM((4, 2, block, 128), BF16),
            pltpu.VMEM((2, block, model), F32),
            pltpu.VMEM((2, block, model), BF16),
            pltpu.VMEM((2, 2, 2, block, model), BF16),
            pltpu.VMEM((block, model), BF16),
            pltpu.VMEM((2, block, model), BF16),
            pltpu.VMEM((block, model), F32),
            pltpu.VMEM((4, 2, block, 128), BF16),
            pltpu.VMEM((3, 2, slots, 128), BF16),
            pltpu.VMEM((slots, 128), F32),
            pltpu.VMEM((slots, 128), F32),
            pltpu.VMEM((2, block, model), BF16),
            pltpu.VMEM((2, block, model), BF16),
            pltpu.VMEM((block, model), BF16),
            pltpu.VMEM((block, model), BF16),
            pltpu.VMEM((16, model), F32),
            pltpu.VMEM((2, 16, width), F32),
            pltpu.VMEM((2, hops, 16, model), F32),
            pltpu.VMEM((2, hops, 16, model), F32),
            pltpu.SemaphoreType.DMA((WIRES,)),
            pltpu.SemaphoreType.DMA((WIRES,)),
            pltpu.SemaphoreType.DMA((3,)),
            pltpu.SemaphoreType.DMA((3,)),
            pltpu.SemaphoreType.DMA((4, 3)),
            pltpu.SemaphoreType.DMA((2, 2)),
            pltpu.SemaphoreType.DMA((2, 2, 3)),
            pltpu.SemaphoreType.DMA((3,)),
            pltpu.SemaphoreType.DMA((4,)),
            pltpu.SemaphoreType.DMA((4, 4)),
            pltpu.SemaphoreType.DMA((2, 2)),
            pltpu.SemaphoreType.DMA((2, 2)),
        ],
        compiler_params=pltpu.CompilerParams(
            collective_id=0, has_side_effects=True, vmem_limit_bytes=62 * 1024 * 1024
        ),
    )(*operands)


def fast_body(
    planes,
    inputs,
    segments,
    cotangent,
    gain_attn,
    joint_projection_weight,
    query_down_factor,
    query_up_factor,
    value_down_factor,
    value_up_factor,
    w_out,
    gain_mlp,
    w_fc,
    w_proj,
):
    block, _, model = inputs.shape
    width = joint_projection_weight.shape[3]
    rank = query_down_factor.shape[2]
    downs = jnp.concatenate([query_down_factor[0], value_down_factor[0]], axis=1)
    acts, grads, total = step_call(
        block,
        model,
        width,
        planes,
        (
            jnp.swapaxes(inputs, 0, 1),
            jnp.swapaxes(cotangent, 0, 1),
            segments,
            gain_attn,
            gain_mlp,
            downs.T,
            query_up_factor[0],
            value_up_factor[0],
            jnp.swapaxes(joint_projection_weight[0], 0, 1),
            w_out[0],
            w_fc[0],
            w_proj[0],
        ),
    )
    return (
        jnp.swapaxes(acts, 0, 1)[None],
        jnp.swapaxes(grads, 0, 1)[None],
        total[:rank].T[None],
        total[2 * rank : 3 * rank][None],
        total[rank : 2 * rank].T[None],
        total[3 * rank :][None],
    )


def fits_fast(mesh, shapes):
    planes = mesh.shape["dp"]
    slots, rows_all, model = shapes[0]
    return (
        mesh.shape["section"] == 2
        and mesh.shape["tensor"] == 4
        and planes > 1
        and planes & (planes - 1) == 0
        and rows_all == 2 * planes
        and slots == 1024
        and model == 1024
        and shapes[4][3] == 1024
        and shapes[5][2] == 4
        and shapes[11][2] == 4096
    )


def solution(mesh):
    placed = (
        P("tensor", "dp", None),
        P("dp", None),
        P("tensor", "dp", None),
        P("section", None),
        P("section", None, None, "tensor"),
        P("section", None, None),
        P("section", None, "tensor"),
        P("section", None, None),
        P("section", None, "tensor"),
        P("section", "tensor", None),
        P("section", None),
        P("section", None, "tensor"),
        P("section", "tensor", None),
    )

    def mapped(picked):
        return jax.shard_map(
            picked,
            mesh=mesh,
            in_specs=placed,
            out_specs=(
                P("section", "tensor", "dp", None),
                P("section", "tensor", "dp", None),
                P("section", None, None),
                P("section", None, None),
                P("section", None, None),
                P("section", None, None),
            ),
            check_vma=False,
        )

    def choose(*args):
        if fits_fast(mesh, [a.shape for a in args]):
            return mapped(functools.partial(fast_body, mesh.shape["dp"]))(*args)
        return mapped(body)(*args)

    return choose
```

```python
import functools

import jax
import jax.numpy as jnp
from jax import lax
from jax.experimental import pallas as pl
from jax.experimental.pallas import tpu as pltpu
from jax.sharding import PartitionSpec as P

HEAD_DIM = 64
MICRO = 2


EPSILON = 1e-05
PRECISE = lax.Precision.HIGHEST
MASKED = -1000000000.0
CUBIC_TERM = 0.044715
TANH_SCALE = 0.7978845608028654


def passed_along(block, axis, distance):
    devices = range(lax.axis_size(axis))
    route = [(i - distance, i) for i in devices if i - distance in devices]
    return lax.ppermute(block, axis, route)


def gelu_tanh(value):
    return 0.5 * value * (1.0 + jnp.tanh(TANH_SCALE * (value + CUBIC_TERM * value * value * value)))


def normalize(residual_stream, gain):
    middle = jnp.mean(residual_stream, axis=-1, keepdims=True)
    centred = residual_stream - middle
    inverse = lax.rsqrt(jnp.mean(centred * centred, axis=-1, keepdims=True) + EPSILON)
    unit_rows = centred * inverse
    return (unit_rows * gain, unit_rows, inverse)


def normalize_back(grad_norm, unit_rows, inverse, gain):
    scaled = grad_norm * gain
    return inverse * (
        scaled
        - jnp.mean(scaled, axis=-1, keepdims=True)
        - unit_rows * jnp.mean(scaled * unit_rows, axis=-1, keepdims=True)
    )


def block_mask(segment_row_span, first_row, block):
    length = segment_row_span.shape[1]
    segment_part = lax.dynamic_slice_in_dim(segment_row_span, first_row, block, 1)
    query_places = first_row + jnp.arange(block)
    key_places = jnp.arange(length)
    same_doc = segment_part[:, :, None] == segment_row_span[:, None, :]
    return same_doc & (key_places[None, None, :] <= query_places[None, :, None])


def projected_rows(row_portion, joint_projection_weight, adapter_pair):
    query_down_factor, query_up_factor, value_down_factor, value_up_factor = adapter_pair
    factor = 32.0 / query_down_factor.shape[-1]
    joined = jnp.einsum(
        "srd,dcf->srcf", row_portion, joint_projection_weight, preferred_element_type=jnp.float32
    )
    narrow_query_rows = jnp.einsum(
        "srd,dk->srk", row_portion, query_down_factor, preferred_element_type=jnp.float32
    )
    narrow_value_rows = jnp.einsum(
        "srd,dk->srk", row_portion, value_down_factor, preferred_element_type=jnp.float32
    )
    queries = joined[:, :, 0] + factor * jnp.einsum(
        "srk,kf->srf", narrow_query_rows, query_up_factor.astype(jnp.float32), precision=PRECISE
    )
    values_all = joined[:, :, 2] + factor * jnp.einsum(
        "srk,kf->srf", narrow_value_rows, value_up_factor.astype(jnp.float32), precision=PRECISE
    )
    stacked_weights = jnp.stack([queries, joined[:, :, 1], values_all], axis=2).astype(jnp.bfloat16)
    return (stacked_weights, narrow_query_rows, narrow_value_rows)


def attention_forward(queries, keys_all, values_all, segment_row_span):
    length, row_count, head_count, width = queries.shape
    block = min(512, length)
    factor = width ** (-0.5)

    def one_block(block_index):
        first_row = block_index * block
        query_part = lax.dynamic_slice_in_dim(queries, first_row, block, 0)
        scores = (
            jnp.einsum("qrhe,krhe->rhqk", query_part, keys_all, preferred_element_type=jnp.float32)
            * factor
        )
        allowed = block_mask(segment_row_span, first_row, block)
        scores = jnp.where(allowed[:, None], scores, MASKED)
        row_max = jnp.max(scores, axis=-1, keepdims=True)
        exponent = jnp.exp(scores - row_max)
        total = jnp.sum(exponent, axis=-1, keepdims=True)
        weights_soft = (exponent / total).astype(jnp.bfloat16)
        attended = jnp.einsum(
            "rhqk,krhe->qrhe", weights_soft, values_all, preferred_element_type=jnp.float32
        )
        return (attended, (row_max + jnp.log(total))[..., 0])

    attended, log_sums = lax.map(one_block, jnp.arange(length // block))
    attended = attended.reshape(length, row_count, head_count, width)
    log_sums = jnp.moveaxis(log_sums, 0, 2).reshape(row_count, head_count, length)
    return (attended, log_sums)


def attention_backward(queries, keys_all, values_all, segment_row_span, log_sums, grad_heads):
    length = queries.shape[0]
    block = min(512, length)
    factor = queries.shape[-1] ** (-0.5)

    def one_block(carry, block_index):
        grad_keys, grad_values = carry
        first_row = block_index * block
        query_part = lax.dynamic_slice_in_dim(queries, first_row, block, 0)
        grad_part = lax.dynamic_slice_in_dim(grad_heads, first_row, block, 0)
        sums_part = lax.dynamic_slice_in_dim(log_sums, first_row, block, 2)
        scores = (
            jnp.einsum("qrhe,krhe->rhqk", query_part, keys_all, preferred_element_type=jnp.float32)
            * factor
        )
        allowed = block_mask(segment_row_span, first_row, block)
        scores = jnp.where(allowed[:, None], scores, MASKED)
        weights_soft = jnp.exp(scores - sums_part[..., None])
        grad_soft = jnp.einsum(
            "qrhe,krhe->rhqk", grad_part, values_all, preferred_element_type=jnp.float32
        )
        grad_scores = weights_soft * (
            grad_soft - jnp.sum(weights_soft * grad_soft, axis=-1, keepdims=True)
        )
        grad_scores = grad_scores.astype(jnp.bfloat16)
        grad_query = (
            jnp.einsum("rhqk,krhe->qrhe", grad_scores, keys_all, preferred_element_type=jnp.float32)
            * factor
        )
        grad_keys = (
            grad_keys
            + jnp.einsum(
                "rhqk,qrhe->krhe", grad_scores, query_part, preferred_element_type=jnp.float32
            )
            * factor
        )
        grad_values = grad_values + jnp.einsum(
            "rhqk,qrhe->krhe",
            weights_soft.astype(jnp.bfloat16),
            grad_part,
            preferred_element_type=jnp.float32,
        )
        return ((grad_keys, grad_values), grad_query)

    start_state = (jnp.zeros(keys_all.shape, jnp.float32), jnp.zeros(values_all.shape, jnp.float32))
    (grad_keys, grad_values), grad_blocks = lax.scan(
        one_block, start_state, jnp.arange(length // block)
    )
    return (grad_blocks.reshape(queries.shape), grad_keys, grad_values)


def attend_all(stacked_weights, segment_row_span):
    length, row_count = (stacked_weights.shape[0], stacked_weights.shape[1])
    head_view = stacked_weights.reshape(length, row_count, 3, -1, HEAD_DIM)
    queries, keys_all, values_all = (head_view[:, :, 0], head_view[:, :, 1], head_view[:, :, 2])
    attended, log_sums = attention_forward(queries, keys_all, values_all, segment_row_span)
    return (
        attended.reshape(length, row_count, -1).astype(jnp.bfloat16),
        log_sums,
        (queries, keys_all, values_all),
    )


def attention_project(attended_b, w_out):
    return lax.psum_scatter(
        jnp.einsum("srf,fd->srd", attended_b, w_out, preferred_element_type=jnp.float32).astype(
            jnp.bfloat16
        ),
        "tensor",
        scatter_dimension=0,
        tiled=True,
    ).astype(jnp.float32)


def attention_grad_heads(grad_middle_b, w_out):
    grad_attended = jnp.einsum(
        "srd,fd->srf",
        lax.all_gather(grad_middle_b, "tensor", axis=0, tiled=True),
        w_out,
        preferred_element_type=jnp.float32,
    )
    return grad_attended.astype(jnp.bfloat16)


def mlp_pre(normed_b, w_fc):
    return jnp.einsum(
        "srd,df->srf",
        lax.all_gather(normed_b, "tensor", axis=0, tiled=True),
        w_fc,
        preferred_element_type=jnp.float32,
    )


def mlp_out(hidden_b, w_proj):
    return lax.psum_scatter(
        jnp.einsum("srf,fd->srd", hidden_b, w_proj, preferred_element_type=jnp.float32).astype(
            jnp.bfloat16
        ),
        "tensor",
        scatter_dimension=0,
        tiled=True,
    ).astype(jnp.float32)


def mlp_back(grad_mlp, pre_act, w_fc, w_proj):
    grad_hidden = jnp.einsum(
        "srd,fd->srf",
        lax.all_gather(grad_mlp, "tensor", axis=0, tiled=True),
        w_proj,
        preferred_element_type=jnp.float32,
    )
    activated, slope = jax.vjp(gelu_tanh, pre_act)
    grad_pre = slope(grad_hidden)[0].astype(jnp.bfloat16)
    return lax.psum_scatter(
        jnp.einsum("srf,df->srd", grad_pre, w_fc, preferred_element_type=jnp.float32).astype(
            jnp.bfloat16
        ),
        "tensor",
        scatter_dimension=0,
        tiled=True,
    ).astype(jnp.float32)


def forward_layer_step(layer_input_rows, segment_row_span, fixed_weights, adapter_pair):
    norm_rows = normalize(layer_input_rows, fixed_weights[0])[0].astype(jnp.bfloat16)
    stacked_weights = projected_rows(
        lax.all_gather(norm_rows, "tensor", axis=0, tiled=True), fixed_weights[1], adapter_pair
    )[0]
    attended_b = attend_all(stacked_weights, segment_row_span)[0]
    middle = layer_input_rows + attention_project(attended_b, fixed_weights[2])
    normed_mlp = normalize(middle, fixed_weights[3])[0].astype(jnp.bfloat16)
    pre_act = mlp_pre(normed_mlp, fixed_weights[4])
    hidden_b = gelu_tanh(pre_act).astype(jnp.bfloat16)
    return middle + mlp_out(hidden_b, fixed_weights[5])


def backward_layer_step(
    layer_input_rows, segment_row_span, upstream_gradient, fixed_weights, adapter_pair
):
    gain_a, joint_projection_weight, w_out, gain_m, w_fc, w_proj = fixed_weights
    query_down_factor, query_up_factor, value_down_factor, value_up_factor = adapter_pair
    factor = 32.0 / query_down_factor.shape[-1]
    norm_rows, unit_first, inverse_first = normalize(layer_input_rows, gain_a)
    collected_rows = lax.all_gather(norm_rows.astype(jnp.bfloat16), "tensor", axis=0, tiled=True)
    stacked_weights, narrow_query_rows, narrow_value_rows = projected_rows(
        collected_rows, joint_projection_weight, adapter_pair
    )
    length, row_count = (collected_rows.shape[0], collected_rows.shape[1])
    attended_b, log_sums, head_views = attend_all(stacked_weights, segment_row_span)
    queries, keys_all, values_all = head_views
    middle = layer_input_rows + attention_project(attended_b, w_out)
    normed_mlp, unit_second, inverse_second = normalize(middle, gain_m)
    pre_act = mlp_pre(normed_mlp.astype(jnp.bfloat16), w_fc)
    grad_norm_mlp = mlp_back(upstream_gradient.astype(jnp.bfloat16), pre_act, w_fc, w_proj)
    grad_middle = upstream_gradient + normalize_back(
        grad_norm_mlp, unit_second, inverse_second, gain_m
    )
    grad_attended = attention_grad_heads(grad_middle.astype(jnp.bfloat16), w_out)
    grad_heads = grad_attended.reshape(queries.shape)
    grad_queries, grad_keys, grad_values = attention_backward(
        queries, keys_all, values_all, segment_row_span, log_sums, grad_heads
    )
    grad_stack = (
        jnp.stack([grad_queries, grad_keys, grad_values], axis=2)
        .astype(jnp.bfloat16)
        .reshape(length, row_count, 3, -1)
    )
    grad_query_rows = grad_stack[:, :, 0]
    grad_value_rows = grad_stack[:, :, 2]
    thin_grad_query = factor * jnp.einsum(
        "srf,kf->srk", grad_query_rows, query_up_factor, preferred_element_type=jnp.float32
    )
    thin_grad_value = factor * jnp.einsum(
        "srf,kf->srk", grad_value_rows, value_up_factor, preferred_element_type=jnp.float32
    )
    grad_bq = factor * jnp.einsum(
        "srk,srf->kf", narrow_query_rows, grad_query_rows.astype(jnp.float32), precision=PRECISE
    )
    grad_bv = factor * jnp.einsum(
        "srk,srf->kf", narrow_value_rows, grad_value_rows.astype(jnp.float32), precision=PRECISE
    )
    gathered_wide = collected_rows.astype(jnp.float32)
    grad_aq = jnp.einsum("srd,srk->dk", gathered_wide, thin_grad_query, precision=PRECISE)
    grad_av = jnp.einsum("srd,srk->dk", gathered_wide, thin_grad_value, precision=PRECISE)
    a_query_wide = query_down_factor.astype(jnp.float32)
    a_value_wide = value_down_factor.astype(jnp.float32)
    term = jnp.einsum(
        "srcf,dcf->srd", grad_stack, joint_projection_weight, preferred_element_type=jnp.float32
    )
    term = term + jnp.einsum("srk,dk->srd", thin_grad_query, a_query_wide, precision=PRECISE)
    grad_norm_attn = lax.psum_scatter(
        (term + jnp.einsum("srk,dk->srd", thin_grad_value, a_value_wide, precision=PRECISE)).astype(
            jnp.bfloat16
        ),
        "tensor",
        scatter_dimension=0,
        tiled=True,
    ).astype(jnp.float32)
    layer_output_rows = grad_middle + normalize_back(
        grad_norm_attn, unit_first, inverse_first, gain_a
    )
    return (layer_output_rows, (grad_aq, grad_bq, grad_av, grad_bv))


def body(
    inputs,
    segments,
    cotangent,
    gain_attn,
    joint_projection_weight,
    query_down_factor,
    query_up_factor,
    value_down_factor,
    value_up_factor,
    w_out,
    gain_mlp,
    w_fc,
    w_proj,
):
    fixed_weights = (
        gain_attn[0],
        joint_projection_weight[0],
        w_out[0],
        gain_mlp[0],
        w_fc[0],
        w_proj[0],
    )
    adapter_pair = (
        query_down_factor[0],
        query_up_factor[0],
        value_down_factor[0],
        value_up_factor[0],
    )
    sections = lax.axis_size("section")
    section_index = lax.axis_index("section")
    is_first = section_index == 0
    is_last = section_index == sections - 1
    rows_mb = inputs.shape[1] // MICRO
    ticks = MICRO + sections - 1
    block_shape = (inputs.shape[0], rows_mb, inputs.shape[2])
    activations = jnp.zeros_like(inputs)
    kept_inputs = jnp.zeros((MICRO,) + block_shape, jnp.bfloat16)
    arriving = jnp.zeros(block_shape, jnp.bfloat16)
    for tick_index in range(ticks):
        own_index = min(tick_index, MICRO - 1)
        mb_slot = tick_index - section_index
        is_valid = (mb_slot >= 0) & (mb_slot < MICRO)
        mb_slot = jnp.clip(mb_slot, 0, MICRO - 1)
        fresh = lax.slice_in_dim(inputs, own_index * rows_mb, (own_index + 1) * rows_mb, axis=1)
        layer_input_rows = jnp.where(is_first, fresh, arriving)
        segment_row_span = lax.dynamic_slice_in_dim(segments, mb_slot * rows_mb, rows_mb, 0)
        layer_output_rows = forward_layer_step(
            layer_input_rows.astype(jnp.float32), segment_row_span, fixed_weights, adapter_pair
        ).astype(jnp.bfloat16)
        activations = jnp.where(
            is_valid,
            lax.dynamic_update_slice_in_dim(activations, layer_output_rows, mb_slot * rows_mb, 1),
            activations,
        )
        kept_inputs = jnp.where(
            is_valid, kept_inputs.at[mb_slot].set(layer_input_rows), kept_inputs
        )
        if tick_index < ticks - 1:
            arriving = passed_along(layer_output_rows, "section", 1)
    input_grads = jnp.zeros_like(inputs)
    gradient_totals = tuple(
        (jnp.zeros(factor_tensor.shape, jnp.float32) for factor_tensor in adapter_pair)
    )
    arriving = jnp.zeros(block_shape, jnp.bfloat16)
    for tick_index in range(ticks):
        own_index = min(tick_index, MICRO - 1)
        mb_slot = tick_index - (sections - 1 - section_index)
        is_valid = (mb_slot >= 0) & (mb_slot < MICRO)
        mb_slot = jnp.clip(mb_slot, 0, MICRO - 1)
        given = lax.slice_in_dim(cotangent, own_index * rows_mb, (own_index + 1) * rows_mb, axis=1)
        upstream_gradient = jnp.where(is_last, given, arriving).astype(jnp.float32)
        layer_input_rows = kept_inputs[mb_slot].astype(jnp.float32)
        segment_row_span = lax.dynamic_slice_in_dim(segments, mb_slot * rows_mb, rows_mb, 0)
        layer_output_rows, row_pieces = backward_layer_step(
            layer_input_rows, segment_row_span, upstream_gradient, fixed_weights, adapter_pair
        )
        leaving_b = layer_output_rows.astype(jnp.bfloat16)
        input_grads = jnp.where(
            is_valid,
            lax.dynamic_update_slice_in_dim(input_grads, leaving_b, mb_slot * rows_mb, 1),
            input_grads,
        )
        gradient_totals = tuple(
            (
                running + jnp.where(is_valid, piece_grad, 0.0)
                for running, piece_grad in zip(gradient_totals, row_pieces)
            )
        )
        if tick_index < ticks - 1:
            arriving = passed_along(leaving_b, "section", -1)
    adapter_rank = adapter_pair[1].shape[0]
    model_width = inputs.shape[2]
    column_total = adapter_pair[1].shape[1]
    offset = lax.axis_index("tensor") * column_total
    full_query = lax.dynamic_update_slice_in_dim(
        jnp.zeros((adapter_rank, model_width), jnp.float32), gradient_totals[1], offset, 1
    )
    full_value = lax.dynamic_update_slice_in_dim(
        jnp.zeros((adapter_rank, model_width), jnp.float32), gradient_totals[3], offset, 1
    )
    summed = lax.psum(
        (gradient_totals[0], full_query, gradient_totals[2], full_value), ("dp", "tensor")
    )
    return (
        activations[None],
        input_grads[None],
        summed[0][None],
        summed[1][None],
        summed[2][None],
        summed[3][None],
    )


REACH = 512
BF16 = jnp.bfloat16
F32 = jnp.float32
MESH = pl.DeviceIdType.MESH


def dot_nn(a, b):
    return lax.dot_general(a, b, (((1,), (0,)), ((), ())), preferred_element_type=F32)


def dot_nt(a, b):
    return lax.dot_general(a, b, (((1,), (1,)), ((), ())), preferred_element_type=F32)


def dot_tn(a, b):
    return lax.dot_general(a, b, (((0,), (0,)), ((), ())), preferred_element_type=F32)


def norm_stats(rows):
    middle = jnp.mean(rows, axis=-1, keepdims=True)
    centred = rows - middle
    inverse = lax.rsqrt(jnp.mean(centred * centred, axis=-1, keepdims=True) + EPSILON)
    return centred * inverse, inverse


def gelu_slope(pre):
    square = pre * pre
    bent = jnp.tanh(TANH_SCALE * (pre + CUBIC_TERM * square * pre))
    return 0.5 * (1.0 + bent) + (0.5 * TANH_SCALE) * pre * (1.0 - bent * bent) * (
        1.0 + (3.0 * CUBIC_TERM) * square
    )


def key_span(i, block):
    return max(0, i - REACH // block) * block, (i + 1) * block


def allowed_keys(i, block, seg_col_ref, seg_row_ref):
    low, high = key_span(i, block)
    seg_k = seg_col_ref[low:high, :]
    seg_q = seg_row_ref[:, i * block : (i + 1) * block]
    places_k = low + lax.broadcasted_iota(jnp.int32, (high - low, block), 0)
    places_q = i * block + lax.broadcasted_iota(jnp.int32, (high - low, block), 1)
    return (seg_q == seg_k) & (places_k <= places_q)


def head_lanes(rows, h):
    lane = lax.broadcasted_iota(jnp.int32, (rows, 128), 1)
    return (lane < HEAD_DIM) if h == 0 else (lane >= HEAD_DIM)


def both_halves(ref, *index):
    return jnp.concatenate([ref[(*index, 0)], ref[(*index, 1)]], axis=1)


class Wires:
    def __init__(self, send, recv):
        self.send, self.recv, self.count, self.sent = send, recv, 0, []

    def copy(self, source, target, where):
        k = self.count
        self.count += 1
        made = pltpu.make_async_remote_copy(
            src_ref=source,
            dst_ref=target,
            send_sem=self.send.at[k],
            recv_sem=self.recv.at[k],
            device_id=where,
            device_id_type=MESH,
        )
        self.sent.append(made)
        return made

    def forget(self, copy):
        self.sent = [one for one in self.sent if one is not copy]


class Totals:
    def __init__(self, wires, layer, out_ref, in_ref, hops):
        self.out_ref, self.in_ref, self.layer, self.at = out_ref, in_ref, layer, 0
        self.hops = [
            wires.copy(out_ref.at[layer, k], in_ref.at[layer, k], peer)
            for k, peer in enumerate(hops)
        ]
        self.wires = wires
        self.hops[0].start()

    def step(self):
        k, layer = self.at, self.layer
        self.hops[k].wait_recv()
        summed = self.out_ref[layer, k] + self.in_ref[layer, k]
        self.at = k + 1
        if self.at < len(self.hops):
            self.out_ref[layer, self.at] = summed
            self.hops[self.at].start()
        else:
            self.hops[0].wait_send()
            self.wires.forget(self.hops[0])
            self.out_ref[layer, 0] = summed

    def finish(self):
        while self.at < len(self.hops):
            self.step()


WIRES = 128


def step_kernel(
    block,
    model,
    planes,
    x_rows,
    cot_rows,
    seg_rows,
    gain_a,
    gain_m,
    downs_t,
    up_q,
    up_v,
    wq,
    wo,
    fc,
    proj,
    act_out,
    grad_out,
    sums_out,
    act,
    grad,
    xb,
    cb,
    seg_col,
    seg_row,
    sm,
    up,
    pad,
    wq_all,
    up_all,
    wo_all,
    ff,
    rows,
    thin,
    qkv,
    o_out,
    o_in,
    middle,
    norm2,
    pre,
    part_out,
    part_in,
    own_sum,
    do_in,
    dqkv,
    dk_acc,
    dv_acc,
    c_out,
    c_in,
    y_out,
    y_in,
    down_sums,
    up_sums,
    total_out,
    total_in,
    wire_send,
    wire_recv,
    row_send,
    row_recv,
    wq_send,
    wq_recv,
    wq_half,
    local_sem,
    o_send,
    o_recv,
    place_send,
    place_recv,
):
    c = lax.axis_index("section")
    z = lax.axis_index("dp")
    t = lax.axis_index("tensor")
    y, x = lax.div(t, 2), lax.rem(t, 2)
    over_x, over_y = 2 * y + (1 - x), 2 * (1 - y) + x
    mine, twin = 2 * y + c, 2 * y + (1 - c)
    far, far_twin = 2 * (1 - y) + c, 2 * (1 - y) + (1 - c)
    to_c, to_x, to_y = {"section": 1 - c}, {"tensor": over_x}, {"tensor": over_y}
    to_xc = {"section": 1 - c, "tensor": over_x}
    to_yc = {"section": 1 - c, "tensor": over_y}
    to_zs = []
    bit = 1
    while bit < planes:
        up_bit = lax.rem(lax.div(z, bit), 2)
        to_zs.append({"dp": z + bit - 2 * bit * up_bit})
        bit *= 2
    to_z = to_zs[0]
    odd = lax.rem(z, 2)
    here = c == x
    wires = Wires(wire_send, wire_recv)
    width = wq.shape[2]
    factor = 8.0

    barrier = pltpu.get_barrier_semaphore()
    peers = [to_c, to_x, to_y, to_xc, to_yc, *to_zs]
    for peer in peers:
        pl.semaphore_signal(barrier, inc=1, device_id=peer, device_id_type=MESH)
    pl.semaphore_wait(barrier, len(peers))

    def part(which, count):
        first = odd if which == 0 else 1 - odd
        return pl.ds(pl.multiple_of(first * (count // 2), count // 2), count // 2)

    def row_copy(source, target, k):
        return pltpu.make_async_remote_copy(
            src_ref=source,
            dst_ref=target,
            send_sem=row_send.at[k],
            recv_sem=row_recv.at[k],
            device_id=to_x,
            device_id_type=MESH,
        )

    x_copy = row_copy(x_rows.at[1 - x], xb, 0)
    cot_local = pltpu.make_async_copy(cot_rows.at[x], cb.at[0], row_recv.at[1])

    @pl.when(here)
    def _():
        x_copy.start()
        cot_local.start()
        pltpu.make_async_copy(x_rows.at[x], xb, row_recv.at[0]).start()

    pad[...] = jnp.zeros_like(pad)
    pad[0:4] = up_q[...].astype(F32)
    up[0] = pad[...].astype(BF16)
    pad[0:4] = jnp.zeros((4, width), F32)
    pad[4:8] = up_v[...].astype(F32)
    up[1] = pad[...].astype(BF16)

    def wq_twin():
        return [
            pltpu.make_async_remote_copy(
                src_ref=source,
                dst_ref=target.at[c],
                send_sem=wq_send.at[0, j],
                recv_sem=wq_recv.at[c, j],
                device_id=to_c,
                device_id_type=MESH,
            )
            for j, (source, target) in enumerate(((wq, wq_all), (up, up_all)))
        ]

    def wq_over_x():
        cut = part(0, model)
        where = {"section": x, "tensor": over_x}
        made = [
            pltpu.make_async_remote_copy(
                src_ref=wq.at[k, cut],
                dst_ref=wq_all.at[c, k, cut],
                send_sem=wq_send.at[1, k],
                recv_sem=wq_half.at[c, 0, k],
                device_id=where,
                device_id_type=MESH,
            )
            for k in range(3)
        ]
        made.append(
            pltpu.make_async_remote_copy(
                src_ref=up,
                dst_ref=up_all.at[c],
                send_sem=wq_send.at[0, 2],
                recv_sem=wq_recv.at[c, 1],
                device_id=where,
                device_id_type=MESH,
            )
        )
        return made

    def wq_over_z(layer):
        cut = part(0, model)
        return [
            pltpu.make_async_remote_copy(
                src_ref=wq_all.at[layer, k, cut],
                dst_ref=wq_all.at[layer, k, cut],
                send_sem=wq_send.at[2 + layer, k],
                recv_sem=wq_half.at[layer, 1, k],
                device_id=to_z,
                device_id_type=MESH,
            )
            for k in range(3)
        ]

    def wq_local(layer):
        return [
            pltpu.make_async_copy(source, target.at[layer], wq_recv.at[layer, j])
            for j, (source, target) in enumerate(((wq, wq_all), (up, up_all)))
        ]

    def send_wq_far(layer, pieces):
        @pl.when(c == layer)
        def _():
            copies = wq_over_x()
            for k in pieces:
                copies[k].start()

    def send_wq_near():
        @pl.when(here)
        def _():
            for copy in wq_local(c):
                copy.start()

        @pl.when(jnp.logical_not(here))
        def _():
            for copy in wq_twin():
                copy.start()

    def half_wait(layer, which, k):
        cut = part(which, model)
        pltpu.make_async_copy(
            wq.at[k, cut], wq_all.at[layer, k, cut], wq_half.at[layer, which, k]
        ).wait()

    def pass_wq(layer):
        @pl.when(jnp.logical_not(here))
        def _():
            for k, copy in enumerate(wq_over_z(layer)):
                half_wait(layer, 0, k)
                copy.start()

    def arrived_wq(layer):
        whole, small = wq_local(layer)
        small.wait()
        pl.when(here)(whole.wait)

        @pl.when(jnp.logical_not(here))
        def _():
            for k in range(3):
                half_wait(layer, 1, k)

    def sent_wq():
        for copy in wq_over_x():
            copy.wait_send()

        @pl.when(jnp.logical_not(here))
        def _():
            for copy in wq_twin():
                copy.wait_send()
            for layer in range(2):
                for copy in wq_over_z(layer):
                    copy.wait_send()

    send_wq_far(0, (3, 0, 1, 2))
    pl.when(c == 0)(send_wq_near)

    sm[c, 0:1] = gain_a[...]
    sm[c, 8:9] = gain_m[...]
    sm[c, 16:24] = downs_t[...].astype(F32)
    sm[c, 24:32] = jnp.zeros((8, model), F32)
    small_copy = wires.copy(sm.at[c], sm.at[c], to_c)
    small_copy.start()
    seg_row[...] = seg_rows[pl.ds(x, 1), :]
    same = lax.broadcasted_iota(jnp.int32, (128, 128), 0) == lax.broadcasted_iota(
        jnp.int32, (128, 128), 1
    )
    for k in range(4 * block // 128):
        lanes = slice(k * 128, (k + 1) * 128)
        seg_col[lanes, :] = jnp.sum(
            jnp.where(same, seg_row[:, lanes], 0), axis=1, keepdims=True
        )

    locals_ = [
        pltpu.make_async_copy(source, target, local_sem.at[k])
        for k, (source, target) in enumerate(
            ((fc, ff.at[c, 0, 0]), (proj, ff.at[c, 1, 0]), (wo, wo_all.at[c, t]))
        )
    ]
    piece = model // 4

    def ff_rows(p, which):
        first = odd if which == 0 else 1 - odd
        return pl.ds(pl.multiple_of(first * (model // 2) + (p % 2) * piece, piece), piece)

    def ff_same(p, which, where):
        at = ff.at[c, p // 2, 1, ff_rows(p, which)]
        return wires.copy(at, at, where)

    ff_twin = [wires.copy(one, ff.at[c, k, 0], to_c) for k, one in enumerate((fc, proj))]
    ff_x = [
        wires.copy(
            (fc, proj)[p // 2].at[ff_rows(p, 0)], ff.at[c, p // 2, 1, ff_rows(p, 0)], to_x
        )
        for p in range(4)
    ]
    ff_z = [ff_same(p, 0, to_z) for p in range(4)]
    ff_c = [[ff_same(p, which, to_c) for which in range(2)] for p in range(4)]

    def start_ff(layer):
        @pl.when(c == layer)
        def _():
            for copy in ff_x:
                copy.start()

    def pass_ff_x(layer, p):
        @pl.when(c == layer)
        def _():
            ff_x[p].wait_recv()
            ff_z[p].start()
            ff_c[p][0].start()

    def pass_ff_z(layer, p):
        @pl.when(c == layer)
        def _():
            ff_z[p].wait_recv()
            ff_c[p][1].start()

    def arrived_ff(layer):
        @pl.when(c != layer)
        def _():
            for pair in ff_c:
                for copy in pair:
                    copy.wait_recv()

    corner = 2 * (1 - y) + (1 - x)
    wo_cut = part(0, width)
    quart = width // 4
    wo_low = pl.ds(pl.multiple_of(odd * (width // 2), quart), quart)
    wo_high = pl.ds(pl.multiple_of(odd * (width // 2) + quart, quart), quart)

    def wo_same(q, cut, where):
        if cut is None:
            return wires.copy(wo_all.at[c, q], wo_all.at[c, q], where)
        return wires.copy(wo_all.at[c, q, cut], wo_all.at[c, q, cut], where)

    wo_twin = wires.copy(wo, wo_all.at[c, t], to_c)
    wo_x = wires.copy(wo.at[wo_cut], wo_all.at[c, t, wo_cut], to_x)
    wo_y = wires.copy(wo.at[wo_cut], wo_all.at[c, t, wo_cut], to_y)
    wo_dy = wo_same(over_x, wo_low, to_y)
    wo_dx = wo_same(over_y, wo_high, to_x)
    wo_z = [wo_same(q, wo_cut, to_z) for q in (over_x, over_y, corner)]
    wo_c = [wo_same(q, None, to_c) for q in (over_x, over_y, corner)]

    def start_wo_x(layer):
        pl.when(c == layer)(wo_x.start)

    def start_wo_y(layer):
        pl.when(c == layer)(wo_y.start)

    def pass_wo(layer, stage):
        @pl.when(c == layer)
        def _():
            if stage == 0:
                wo_x.wait_recv()
                wo_dy.start()
                wo_z[0].start()
                wo_y.wait_recv()
                wo_dx.start()
                wo_z[1].start()
            if stage == 1:
                wo_dy.wait_recv()
                wo_dx.wait_recv()
                wo_z[2].start()
            if stage == 2:
                for came, onward in zip(wo_z, wo_c):
                    came.wait_recv()
                    onward.start()

    def arrived_wo(layer):
        @pl.when(c == layer)
        def _():
            locals_[2].wait()

        @pl.when(c != layer)
        def _():
            wo_twin.wait_recv()
            for copy in wo_c:
                copy.wait_recv()

    for copy in locals_:
        copy.start()
    for copy in ff_twin + [wo_twin]:
        copy.start()
    start_wo_x(0)
    start_ff(0)

    def place_copy(kind, layer, source, target, at=slice(None)):
        return pltpu.make_async_remote_copy(
            src_ref=source.at[at],
            dst_ref=target.at[x, at],
            send_sem=place_send.at[kind, layer],
            recv_sem=place_recv.at[kind, x],
            device_id={"section": layer, "tensor": mine},
            device_id_type=MESH,
        )

    def place(kind, layer, source, target, at=slice(None)):
        stays = jnp.logical_and(here, c == layer)

        @pl.when(stays)
        def _():
            target[x, at] = source[at]

        @pl.when(jnp.logical_not(stays))
        def _():
            place_copy(kind, layer, source, target, at).start()

    def placed(kind, source, target):
        for layer in range(2):
            stays = jnp.logical_and(here, c == layer)

            @pl.when(jnp.logical_not(stays))
            def _():
                place_copy(kind, layer, source.at[layer], target).wait_send()

        for slot in range(2):
            came = jnp.logical_not(jnp.logical_and(here, x == slot))

            @pl.when(came)
            def _():
                pltpu.make_async_copy(
                    source.at[0], target.at[slot], place_recv.at[kind, slot]
                ).wait()

    def qkv_block(layer, b):
        normed = rows[layer, b]
        down = sm[layer, 16:32, :].astype(BF16)
        low = dot_nt(normed, down)
        low_b = low.astype(BF16)
        thin[layer, b] = low_b
        at = pl.ds(pl.multiple_of(b * block, block), block)
        for k in range(3):
            made = dot_nn(normed, wq_all[layer, k])
            if k == 0:
                made = made + factor * dot_nn(low_b, up_all[layer, 0])
            if k == 2:
                made = made + factor * dot_nn(low_b, up_all[layer, 1])
            made = made.astype(BF16)
            qkv[layer, k, 0, at, :] = made[:, :128]
            qkv[layer, k, 1, at, :] = made[:, 128:]

    def attend(layer, i):
        low, high = key_span(i, block)
        at = slice(i * block, (i + 1) * block)
        allowed = allowed_keys(i, block, seg_col, seg_row)

        def one_pair(pair, carry):
            queries = qkv[layer, 0, pair, at, :] * BF16(HEAD_DIM**-0.5)
            keys = qkv[layer, 1, pair, low:high, :]
            values = qkv[layer, 2, pair, low:high, :]
            parts = []
            for h in range(2):
                picked = jnp.where(head_lanes(block, h), queries, BF16(0))
                scores = jnp.where(allowed, dot_nt(keys, picked), MASKED)
                exponent = jnp.exp(scores - jnp.max(scores, axis=0, keepdims=True))
                total = jnp.sum(exponent, axis=0, keepdims=True)
                made = dot_tn(values, exponent.astype(BF16))
                parts.append(made[h * HEAD_DIM : (h + 1) * HEAD_DIM] / total)
            o_out[i, pair] = jnp.concatenate(parts, axis=0).T.astype(BF16)
            return carry

        lax.fori_loop(0, 2, one_pair, 0)

    def exchange_piece(i, target, phase):
        return pltpu.make_async_remote_copy(
            src_ref=o_out.at[i],
            dst_ref=target.at[mine],
            send_sem=o_send.at[i],
            recv_sem=o_recv.at[phase, mine],
            device_id={"section": i % 2, "tensor": 2 * (i // 2) + x},
            device_id_type=MESH,
        )

    def send_piece(i, target, phase):
        @pl.when(mine == i)
        def _():
            target[mine] = o_out[i]

        @pl.when(mine != i)
        def _():
            exchange_piece(i, target, phase).start()

    def wait_pieces(target, phase):
        for i in range(4):

            @pl.when(mine != i)
            def _():
                exchange_piece(i, target, phase).wait_send()
                pltpu.make_async_copy(o_out.at[i], target.at[i], o_recv.at[phase, i]).wait()

    def hidden_half(layer, who, source, q):
        total = None
        for cut in range(2):
            lanes = slice(cut * model // 2, (cut + 1) * model // 2)
            made = dot_nn(source, ff[layer, 0, q, :, lanes])
            pre[layer, who, q, :, lanes] = made.astype(BF16)
            term = dot_nn(gelu_tanh(made).astype(BF16), ff[layer, 1, q, lanes, :])
            total = term if total is None else total + term
        return total

    def hidden_back(layer, who, upstream, q):
        total = None
        for cut in range(2):
            lanes = slice(cut * model // 2, (cut + 1) * model // 2)
            grad_hidden = dot_nt(upstream, ff[layer, 1, q, lanes, :])
            slope = gelu_slope(pre[layer, who, q, :, lanes].astype(F32))
            term = dot_nt((grad_hidden * slope).astype(BF16), ff[layer, 0, q, :, lanes])
            total = term if total is None else total + term
        return total

    cuts = [
        (q, slice(cut * model // 2, (cut + 1) * model // 2)) for q in range(2) for cut in range(2)
    ]
    half_rows = [slice(h * block // 2, (h + 1) * block // 2) for h in range(2)]

    def in_halves(source, target, where):
        return [wires.copy(source(at), target(at), where) for at in half_rows]

    def give_rows(layer, h, source):
        at = half_rows[h]
        unit, _ = norm_stats(source[at, :].astype(F32))
        rows[layer, mine, at] = (unit * sm[layer, 0:1, :]).astype(BF16)
        row_y[layer][h].start()
        row_c[layer][h].start()

    row_y, row_c, row_yc = [], [], []
    for layer in range(2):
        for store, b, where in ((row_y, mine, to_y), (row_c, mine, to_c), (row_yc, far, to_c)):
            store.append(
                in_halves(
                    lambda at: rows.at[layer, b, at], lambda at: rows.at[layer, b, at], where
                )
            )

    pltpu.make_async_copy(x_rows.at[x], xb, row_recv.at[0]).wait()
    small_copy.wait_recv()
    cot_x = row_copy(cot_rows.at[1 - x], cb.at[0], 1)
    cot_y = wires.copy(cb.at[0], cb.at[1], to_y)

    for layer in range(2):
        source = xb if layer == 0 else act.at[0]
        if layer == 0:
            for h in range(2):
                give_rows(0, h, xb)
            pass_wq(0)
        else:
            pass_wo(1, 1)
            pass_ff_x(1, 2)
        arrived_wq(layer)
        qkv_block(layer, mine)
        if layer == 1:
            pass_ff_x(1, 3)
            pass_wo(1, 2)
            place(0, 0, act.at[0], act_out)
        for copy in row_c[layer]:
            copy.wait_recv()
        qkv_block(layer, twin)
        for copy, onward in zip(row_y[layer], row_yc[layer]):
            copy.wait_recv()
            onward.start()
        if layer == 0:
            start_wo_y(0)

            @pl.when(here)
            def _():
                cot_local.wait()
                cot_y.start()
        else:

            @pl.when(jnp.logical_not(here))
            def _():
                cot_local.wait()
                cot_y.start()
        qkv_block(layer, far)
        for copy in row_yc[layer]:
            copy.wait_recv()
        qkv_block(layer, far_twin)
        if layer == 0:
            pass_ff_x(0, 0)
        for i in range(4):
            attend(layer, i)
            send_piece(i, o_in, layer)
            if layer == 0 and i == 0:
                pass_wo(0, 0)
            if layer == 0 and i == 2:
                pass_wo(0, 1)
                pass_ff_x(0, 1)
            if layer == 0 and i == 3:
                pass_wo(0, 2)
            if layer == 1 and i >= 2:
                pass_ff_z(1, i - 2)
        arrived_wo(layer)
        wait_pieces(o_in, layer)
        if layer == 0:
            pass_ff_x(0, 2)
        else:
            pass_ff_z(1, 2)
        stream = source[...].astype(F32)
        for q in range(4):
            stream = stream + dot_nn(both_halves(o_in, q), wo_all[layer, q])
        middle[layer] = stream
        unit, _ = norm_stats(stream)
        norm2[0] = (unit * sm[layer, 8:9, :]).astype(BF16)
        norm_y = wires.copy(norm2.at[0], norm2.at[1], to_y)
        norm_y.start()
        if layer == 0:
            for copy in locals_[:2]:
                copy.wait()
            for copy in ff_twin:
                copy.wait_recv()
            pass_ff_z(0, 0)
            pass_ff_x(0, 3)
            pl.when(c == 1)(send_wq_near)
            send_wq_far(1, (3, 0, 1, 2))
            start_wo_x(1)
            start_wo_y(1)
            start_ff(1)
            pass_ff_z(0, 1)
        else:
            pass_ff_z(1, 3)
        own_sum[...] = hidden_half(layer, 0, norm2[0], 0)
        if layer == 0:
            pass_ff_z(0, 2)
            pass_ff_z(0, 3)
        arrived_ff(layer)
        own_sum[...] += hidden_half(layer, 0, norm2[0], 1)
        if layer == 1:
            grad[0] = own_sum[...].astype(BF16)
            own_sum[...] = hidden_back(1, 0, cb[0], 0) + hidden_back(1, 0, cb[0], 1)
            cot_y.wait_recv()
            for q in range(2):
                c_out[q] = dot_nt(cb[1], ff[1, 1, q]).astype(BF16)
        norm_y.wait_recv()
        if layer == 0:
            away = hidden_half(0, 1, norm2[1], 0) + hidden_half(0, 1, norm2[1], 1)
        else:
            away = None
            for q, lanes in cuts:
                made = dot_nn(norm2[1], ff[1, 0, q, :, lanes])
                pre[1, 1, q, :, lanes] = made.astype(BF16)
                grad_pre = (c_out[q, :, lanes].astype(F32) * gelu_slope(made)).astype(BF16)
                term = dot_nt(grad_pre, ff[1, 0, q, :, lanes])
                away = term if away is None else away + term
        part_out[...] = away.astype(BF16)
        part_y = in_halves(
            lambda at: part_out.at[at], lambda at: part_in.at[layer, at], to_y
        )
        for copy in part_y:
            copy.start()
        if layer == 1:
            late = None
            for q, lanes in cuts:
                hidden = gelu_tanh(pre[1, 1, q, :, lanes].astype(F32)).astype(BF16)
                term = dot_nn(hidden, ff[1, 1, q, lanes, :])
                late = term if late is None else late + term
            y_out[...] = late.astype(BF16)
        if layer == 0:
            stream = middle[layer] + own_sum[...]
            pass_wq(1)
            pass_wo(1, 0)
            pass_ff_x(1, 0)
            pass_ff_x(1, 1)

            pl.when(here)(cot_x.start)
            for h, at in enumerate(half_rows):
                part_y[h].wait()
                wires.forget(part_y[h])
                act[0, at] = (stream[at] + part_in[0, at].astype(F32)).astype(BF16)
                give_rows(1, h, act.at[0])
            norm_y.wait_send()
            wires.forget(norm_y)

    for layer in (1, 0):
        upstream = cb[0] if layer == 1 else grad[1]
        if layer == 0:
            own_sum[...] = hidden_back(layer, 0, upstream, 0) + hidden_back(layer, 0, upstream, 1)
            for copy in up_y:
                copy.wait_recv()
            totals.step()
            away = hidden_back(layer, 1, norm2[1], 0) + hidden_back(layer, 1, norm2[1], 1)
            part_out[...] = away.astype(BF16)
            part_y = in_halves(
                lambda at: part_out.at[at], lambda at: part_in.at[1, at], to_y
            )
            for copy in part_y:
                copy.start()
        unit, inverse = norm_stats(middle[layer])
        for copy in part_y:
            copy.wait()
            wires.forget(copy)
        if layer == 0:
            totals.step()
        grad_norm = own_sum[...] + part_in[1].astype(F32)
        grad_middle = upstream.astype(F32) + normalize_back(
            grad_norm, unit, inverse, sm[layer, 8:9, :]
        )
        own_sum[...] = grad_middle
        grad_b = grad_middle.astype(BF16)
        for q in range(4):
            made = dot_nt(grad_b, wo_all[layer, q]).astype(BF16)
            o_out[q, 0] = made[:, :128]
            o_out[q, 1] = made[:, 128:]
            send_piece(q, do_in, 2 + layer)
        if layer == 0:
            place(1, 1, grad.at[1], grad_out)
        else:
            late_y = wires.copy(y_out, part_in.at[0], to_y)
            late_y.start()
        wait_pieces(do_in, 2 + layer)
        if layer == 0:
            totals.step()

        def back_pair(pair, carry):
            dk_acc[...] = jnp.zeros_like(dk_acc)
            dv_acc[...] = jnp.zeros_like(dv_acc)
            for i in range(4):
                low, high = key_span(i, block)
                at = slice(i * block, (i + 1) * block)
                allowed = allowed_keys(i, block, seg_col, seg_row)
                queries = qkv[layer, 0, pair, at, :] * BF16(HEAD_DIM**-0.5)
                keys = qkv[layer, 1, pair, low:high, :]
                values = qkv[layer, 2, pair, low:high, :]
                grads = do_in[i, pair]
                parts = []
                for h in range(2):
                    lanes = head_lanes(block, h)
                    picked = jnp.where(lanes, queries, BF16(0))
                    given = jnp.where(lanes, grads, BF16(0))
                    scores = jnp.where(allowed, dot_nt(keys, picked), MASKED)
                    exponent = jnp.exp(scores - jnp.max(scores, axis=0, keepdims=True))
                    soft = exponent * (1.0 / jnp.sum(exponent, axis=0, keepdims=True))
                    weighted = soft * dot_nt(values, given)
                    grad_scores = (
                        weighted - soft * jnp.sum(weighted, axis=0, keepdims=True)
                    ).astype(BF16)
                    made = dot_tn(keys, grad_scores)
                    parts.append(made[h * HEAD_DIM : (h + 1) * HEAD_DIM])
                    dk_acc[low:high, :] += dot_nn(grad_scores, picked)
                    dv_acc[low:high, :] += dot_nn(soft.astype(BF16), given)
                dqkv[0, pair, at, :] = (
                    jnp.concatenate(parts, axis=0).T * HEAD_DIM**-0.5
                ).astype(BF16)
            dqkv[1, pair] = dk_acc[...].astype(BF16)
            dqkv[2, pair] = dv_acc[...].astype(BF16)
            return carry

        lax.fori_loop(0, 2, back_pair, 0)
        if layer == 1:
            late_y.wait()
            wires.forget(late_y)
            act[1] = (
                middle[1] + grad[0].astype(F32) + part_in[0].astype(F32)
            ).astype(BF16)
            place(0, 1, act.at[1], act_out)
        down = sm[layer, 16:32, :].astype(BF16)
        if layer == 0:
            totals.finish()

        def block_grad(b, first):
            at = pl.ds(pl.multiple_of(b * block, block), block)
            parts = [
                jnp.concatenate([dqkv[k, 0, at, :], dqkv[k, 1, at, :]], axis=1) for k in range(3)
            ]
            low = factor * (
                dot_nt(parts[0], up_all[layer, 0]) + dot_nt(parts[2], up_all[layer, 1])
            )
            low_b = low.astype(BF16)
            term = dot_nn(low_b, down)
            for k in range(3):
                term = term + dot_nt(parts[k], wq_all[layer, k])
            kept = thin[layer, b]
            to_down = dot_tn(low_b, rows[layer, b])
            to_up = [factor * dot_tn(kept, parts[0]), factor * dot_tn(kept, parts[2])]
            if first:
                down_sums[...] = to_down
                up_sums[0], up_sums[1] = to_up
            else:
                down_sums[...] += to_down
                up_sums[0] += to_up[0]
                up_sums[1] += to_up[1]
            return term

        c_far = wires.copy(c_out.at[0], c_in.at[0], to_c)
        c_near = wires.copy(c_out.at[1], c_in.at[1], to_c)
        y_far = in_halves(lambda at: y_out.at[at], lambda at: y_in.at[at], to_y)
        c_out[0] = block_grad(far_twin, True).astype(BF16)
        c_far.start()
        term = block_grad(far, False)
        c_far.wait_recv()
        y_out[...] = (term + c_in[0].astype(F32)).astype(BF16)
        for copy in y_far:
            copy.start()
        c_out[1] = block_grad(twin, False).astype(BF16)
        c_near.start()
        term = block_grad(mine, False)
        total_out[layer, 0, 0:8] = down_sums[0:8]
        total_out[layer, 0, 8:16] = jnp.zeros((8, model), F32)
        low_rows = lax.broadcasted_iota(jnp.int32, (8, width), 0) < 4
        total_out[
            layer, 0, 8:16, pl.ds(pl.multiple_of(mine * width, width), width)
        ] = jnp.where(low_rows, up_sums[0, 0:8], up_sums[1, 0:8])
        totals = Totals(wires, layer, total_out, total_in, [to_c, to_x, to_y, *to_zs])
        c_near.wait_recv()
        term = term + c_in[1].astype(F32)
        source = xb if layer == 0 else act.at[0]
        unit, inverse = norm_stats(source[...].astype(F32))
        if layer == 0:
            totals.step()
            totals.step()
        if layer == 1:
            up_y = in_halves(lambda at: grad.at[1, at], lambda at: norm2.at[1, at], to_y)
        for h, at in enumerate(half_rows):
            y_far[h].wait_recv()
            grad_norm = term[at] + y_in[at].astype(F32)
            grad[layer, at] = (
                own_sum[at]
                + normalize_back(grad_norm, unit[at], inverse[at], sm[layer, 0:1, :])
            ).astype(BF16)
            if layer == 1:
                up_y[h].start()
            else:
                place(1, 0, grad.at[0], grad_out, at)
                if h == 0:
                    totals.step()
                    totals.step()
        for copy in (c_far, c_near, *y_far):
            copy.wait_send()
            wires.forget(copy)

    @pl.when(here)
    def _():
        x_copy.wait_send()
        cot_x.wait_send()


    totals.finish()
    sums_out[...] = jnp.where(c == 0, total_out[0, 0], total_out[1, 0])
    sent_wq()
    for copy in wires.sent:
        copy.wait_send()
    placed(0, act, act_out)
    placed(1, grad, grad_out)


def step_call(block, model, width, planes, operands):
    slots = 4 * block
    hops = 3 + (planes - 1).bit_length()
    in_vmem = pl.BlockSpec(memory_space=pltpu.VMEM)
    in_hbm = pl.BlockSpec(memory_space=pl.ANY)
    return pl.pallas_call(
        functools.partial(step_kernel, block, model, planes),
        out_shape=(
            jax.ShapeDtypeStruct((2, block, model), BF16),
            jax.ShapeDtypeStruct((2, block, model), BF16),
            jax.ShapeDtypeStruct((16, model), F32),
        ),
        in_specs=[in_hbm] * 2 + [in_vmem] * 6 + [in_hbm] * 4,
        out_specs=[in_vmem] * 3,
        scratch_shapes=[
            pltpu.VMEM((2, block, model), BF16),
            pltpu.VMEM((2, block, model), BF16),
            pltpu.VMEM((block, model), BF16),
            pltpu.VMEM((2, block, model), BF16),
            pltpu.VMEM((slots, 1), jnp.int32),
            pltpu.VMEM((1, slots), jnp.int32),
            pltpu.VMEM((2, 32, model), F32),
            pltpu.VMEM((2, 16, width), BF16),
            pltpu.VMEM((16, width), F32),
            pltpu.VMEM((2, 3, model, width), BF16),
            pltpu.VMEM((2, 2, 16, width), BF16),
            pltpu.VMEM((2, 4, width, model), BF16),
            pltpu.VMEM((2, 2, 2, model, model), BF16),
            pltpu.VMEM((2, 4, block, model), BF16),
            pltpu.VMEM((2, 4, block, 16), BF16),
            pltpu.VMEM((2, 3, 2, slots, 128), BF16),
            pltpu.VMEM((4, 2, block, 128), BF16),
            pltpu.VMEM((4, 2, block, 128), BF16),
            pltpu.VMEM((2, block, model), F32),
            pltpu.VMEM((2, block, model), BF16),
            pltpu.VMEM((2, 2, 2, block, model), BF16),
            pltpu.VMEM((block, model), BF16),
            pltpu.VMEM((2, block, model), BF16),
            pltpu.VMEM((block, model), F32),
            pltpu.VMEM((4, 2, block, 128), BF16),
            pltpu.VMEM((3, 2, slots, 128), BF16),
            pltpu.VMEM((slots, 128), F32),
            pltpu.VMEM((slots, 128), F32),
            pltpu.VMEM((2, block, model), BF16),
            pltpu.VMEM((2, block, model), BF16),
            pltpu.VMEM((block, model), BF16),
            pltpu.VMEM((block, model), BF16),
            pltpu.VMEM((16, model), F32),
            pltpu.VMEM((2, 16, width), F32),
            pltpu.VMEM((2, hops, 16, model), F32),
            pltpu.VMEM((2, hops, 16, model), F32),
            pltpu.SemaphoreType.DMA((WIRES,)),
            pltpu.SemaphoreType.DMA((WIRES,)),
            pltpu.SemaphoreType.DMA((3,)),
            pltpu.SemaphoreType.DMA((3,)),
            pltpu.SemaphoreType.DMA((4, 3)),
            pltpu.SemaphoreType.DMA((2, 2)),
            pltpu.SemaphoreType.DMA((2, 2, 3)),
            pltpu.SemaphoreType.DMA((3,)),
            pltpu.SemaphoreType.DMA((4,)),
            pltpu.SemaphoreType.DMA((4, 4)),
            pltpu.SemaphoreType.DMA((2, 2)),
            pltpu.SemaphoreType.DMA((2, 2)),
        ],
        compiler_params=pltpu.CompilerParams(
            collective_id=0, has_side_effects=True, vmem_limit_bytes=62 * 1024 * 1024
        ),
    )(*operands)


def fast_body(
    planes,
    inputs,
    segments,
    cotangent,
    gain_attn,
    joint_projection_weight,
    query_down_factor,
    query_up_factor,
    value_down_factor,
    value_up_factor,
    w_out,
    gain_mlp,
    w_fc,
    w_proj,
):
    block, _, model = inputs.shape
    width = joint_projection_weight.shape[3]
    rank = query_down_factor.shape[2]
    downs = jnp.concatenate([query_down_factor[0], value_down_factor[0]], axis=1)
    acts, grads, total = step_call(
        block,
        model,
        width,
        planes,
        (
            jnp.swapaxes(inputs, 0, 1),
            jnp.swapaxes(cotangent, 0, 1),
            segments,
            gain_attn,
            gain_mlp,
            downs.T,
            query_up_factor[0],
            value_up_factor[0],
            jnp.swapaxes(joint_projection_weight[0], 0, 1),
            w_out[0],
            w_fc[0],
            w_proj[0],
        ),
    )
    return (
        jnp.swapaxes(acts, 0, 1)[None],
        jnp.swapaxes(grads, 0, 1)[None],
        total[:rank].T[None],
        total[2 * rank : 3 * rank][None],
        total[rank : 2 * rank].T[None],
        total[3 * rank :][None],
    )


def fits_fast(mesh, shapes):
    planes = mesh.shape["dp"]
    slots, rows_all, model = shapes[0]
    return (
        mesh.shape["section"] == 2
        and mesh.shape["tensor"] == 4
        and planes > 1
        and planes & (planes - 1) == 0
        and rows_all == 2 * planes
        and slots == 1024
        and model == 1024
        and shapes[4][3] == 1024
        and shapes[5][2] == 4
        and shapes[11][2] == 4096
    )


def solution(mesh):
    placed = (
        P("tensor", "dp", None),
        P("dp", None),
        P("tensor", "dp", None),
        P("section", None),
        P("section", None, None, "tensor"),
        P("section", None, None),
        P("section", None, "tensor"),
        P("section", None, None),
        P("section", None, "tensor"),
        P("section", "tensor", None),
        P("section", None),
        P("section", None, "tensor"),
        P("section", "tensor", None),
    )

    def mapped(picked):
        return jax.shard_map(
            picked,
            mesh=mesh,
            in_specs=placed,
            out_specs=(
                P("section", "tensor", "dp", None),
                P("section", "tensor", "dp", None),
                P("section", None, None),
                P("section", None, None),
                P("section", None, None),
                P("section", None, None),
            ),
            check_vma=False,
        )

    def choose(*args):
        if fits_fast(mesh, [a.shape for a in args]):
            return mapped(functools.partial(fast_body, mesh.shape["dp"]))(*args)
        return mapped(body)(*args)

    return choose
```
